32 devices in a mesh: dp: 8 (over z, x), tensor: 4 (over y, core).
Axes of the slice: x: 2, y: 2, z: 4, core: 2. Of those that a mesh axis runs over, the one named last changes fastest.
Arguments:
- hidden_in: bfloat16 [1024, 32, 768], P('tensor', 'dp'), may hold values from -6 to 6
- cotangent: bfloat16 [1024, 32, 768], P('tensor', 'dp'), may hold values from -6 to 6
- prefix: int32 [32], P('dp'), may hold values from 102 to 512, as said below
- w_qkv: bfloat16 [768, 3, 768], P('dp', None, 'tensor'), may hold values from -0.21875 to 0.21875
- w_out: bfloat16 [768, 768], P('tensor', 'dp'), may hold values from -3 to 3
- w_in: bfloat16 [768, 3072], P('dp', 'tensor'), may hold values from -0.21875 to 0.21875
- w_down: bfloat16 [3072, 768], P('tensor', 'dp'), may hold values from -0.109375 to 0.109375
- biases: float32 [10, 768], P(None, ('dp', 'tensor')), may hold values from -1 to 1
- gains: float32 [2, 768], P(None, ('dp', 'tensor')), may hold values from 0.25 to 1.75
Outputs:
- output: bfloat16 [1024, 32, 768], P('tensor', 'dp')
- grad_input: bfloat16 [1024, 32, 768], P('tensor', 'dp')
- grad_qkv: float32 [768, 3, 768], P('dp', None, 'tensor')
- grad_out: float32 [768, 768], P('tensor', 'dp')
- grad_in: float32 [768, 3072], P('dp', 'tensor')
- grad_down: float32 [3072, 768], P('tensor', 'dp')
- grad_biases: float32 [10, 768], P(None, ('dp', 'tensor'))
- grad_gains: float32 [2, 768], P(None, ('dp', 'tensor'))
The draws below stay inside these ranges and needn't reach their ends.
Inputs may be any that keep to these rules, and one draw needn't show every extreme that they name: Every draw has a sequence whose prefix is 512.
All inputs are finite; a program needn't handle non-finite values.
Results may differ from the reference program's by a relative error of at most 0.018.
Values may be sent and summed in bfloat16 or wider, within the bound.
A program may use at most 192 MiB of HBM per device.

```python
import math
import jax
import jax.numpy as jnp
from jax import lax

D = 768
HEADS = 12
HEAD = 64
FF = 3072
L = 1024
SEQS = 32


def draw_prefix(key, part):
    base_draw = jax.random.randint(key, (SEQS,), L // 10, L // 2 + 1)
    chosen = jax.random.randint(jax.random.fold_in(key, 7), (), 0, SEQS)
    return jnp.where(jnp.arange(SEQS) == chosen, L // 2, base_draw).astype(jnp.int32)


def with_spikes(entries, key, source, target, blocks, factor):
    def block_of(dim):
        return (jnp.arange(entries.shape[dim]) // (entries.shape[dim] // blocks)).reshape((-1,) + (1,) * (entries.ndim - 1 - dim))

    one_side = jax.random.permutation(key, blocks)[block_of(target)]
    far = (block_of(target) + blocks // 2) % blocks
    return jnp.where((block_of(source) == one_side) | (block_of(source) == far), factor * entries, entries)


def shard_levels(key, dims, pieces, smallest, high):
    loudness = 1.0
    for axis_at, blocks in pieces:
        heights = jax.random.uniform(jax.random.fold_in(jax.random.fold_in(key, 6), axis_at), (blocks,), jnp.float32, smallest / len(pieces), high / len(pieces))
        loudness = loudness * jnp.repeat(jnp.exp(heights), dims[axis_at] // blocks).reshape((-1,) + (1,) * (len(dims) - 1 - axis_at))
    return loudness


def scatter_about(key, shape, width, limit, shards=(), kind=jnp.bfloat16):
    drawn = jax.random.normal(key, shape, jnp.float32) * width
    if len(shards) > 0:
        drawn = shard_levels(key, shape, shards, -0.22, 0.18) * drawn
    return jnp.clip(drawn, min=-limit, max=limit).astype(kind)


def bell_draw_with(own_key, dims, scale, bound, shards, heavy, held_as=jnp.bfloat16):
    result = scale * jax.random.normal(own_key, dims, jnp.float32)
    if shards:
        result = result * shard_levels(own_key, dims, shards, -0.22, 0.18)
    return jnp.clip(with_spikes(result, jax.random.fold_in(own_key, 3), *heavy), -bound, bound).astype(held_as)


def setup_inputs(seed: int = 0) -> dict:
    keys = jax.random.split(jax.random.key(seed), 10)
    hidden_in = scatter_about(keys[0], (L, SEQS, D), 1.0, 6.0, ((0, 4), (1, 8)))
    cotangent = bell_draw_with(keys[1], (L, SEQS, D), 1.0, 6.0, ((0, 4), (1, 8)), (1, 2, 8, 2.0))
    prefix = draw_prefix(jax.random.fold_in(keys[9], 71), 0)
    w_qkv = scatter_about(keys[3], (D, 3, D), D ** -0.5, 0.21875, ((0, 8), (2, 4)))
    w_out = scatter_about(keys[4], (D, D), (max(D // 192, 1)) ** -0.5, 3.0, ((0, 4), (1, 8)))
    w_in = scatter_about(keys[5], (D, FF), D ** -0.5, 0.21875, ((0, 8), (1, 4)))
    w_down = scatter_about(keys[6], (FF, D), FF ** -0.5, 0.109375, ((0, 4), (1, 8)))
    biases = scatter_about(keys[7], (10, D), 0.2, 1.0, ((1, 32),), jnp.float32)
    gains = jnp.clip(1.0 + 0.15 * jax.random.normal(keys[8], (2, D), jnp.float32), 0.25, 1.75)
    return {"hidden_in": hidden_in, "cotangent": cotangent, "prefix": prefix, "w_qkv": w_qkv, "w_out": w_out, "w_in": w_in, "w_down": w_down, "biases": biases, "gains": gains}


@jax.custom_vjp
def low(v):
    return lax.optimization_barrier(v.astype(jnp.bfloat16)).astype(jnp.float32)

@jax.custom_vjp
def low_back(v):
    return v

def low_keep(v):
    return (low(v), None)

def low_pass(kept, grad):
    return (grad,)

def back_keep(v):
    return (v, None)

def back_low(kept, grad):
    return (low(grad),)
low.defvjp(low_keep, low_pass)
low_back.defvjp(back_keep, back_low)
EPSILON = 1e-12
MASKED = -1e+30
HIGHEST = lax.Precision.HIGHEST

def layer_norm(inputs, gain_vec, offset):
    center = inputs - lax.optimization_barrier(jnp.mean(inputs, axis=-1, keepdims=True))
    spread = lax.optimization_barrier(jnp.mean(center * center, axis=-1, keepdims=True))
    return center * lax.rsqrt(spread + EPSILON) * gain_vec + offset

def attend_one(operands):
    queries, keys_all, values_all, prefix_one = operands
    length = queries.shape[0]
    raw_scores = jnp.einsum('qhd,khd->hqk', queries, keys_all, precision=HIGHEST)
    scores = low_back(raw_scores) * HEAD ** (-0.5)
    positions = jnp.arange(length, dtype=jnp.int32)
    allowed = jnp.logical_or(positions[None, :] <= positions[:, None], positions[None, :] < prefix_one)
    scores = jnp.where(allowed[None], scores, MASKED)
    probs = low(jax.nn.softmax(scores, axis=-1))
    mixed = jnp.einsum('hqk,khd->qhd', probs, values_all, precision=HIGHEST)
    return low(low_back(mixed))

def forward(hidden, w_qkv, w_out, w_in, w_down, biases, gains, prefix_group):
    length, seq_count, model_width = hidden.shape
    rows_hidden = FF // model_width
    bias_three = jnp.stack([biases[0], jnp.zeros_like(biases[0]), biases[1]])
    raw_qkv = jnp.einsum('psd,dch->psch', hidden, w_qkv, precision=HIGHEST) + bias_three
    proj_qkv = low(low_back(raw_qkv)).reshape(length, seq_count, 3, HEADS, HEAD)
    per_seq = jnp.transpose(proj_qkv, (1, 2, 0, 3, 4))
    mixed = lax.map(jax.checkpoint(attend_one), (per_seq[:, 0], per_seq[:, 1], per_seq[:, 2], prefix_group))
    heads_flat = jnp.transpose(mixed, (1, 0, 2, 3)).reshape(length, seq_count, model_width)
    attn_branch = low_back(jnp.einsum('psh,hd->psd', heads_flat, w_out, precision=HIGHEST))
    resid_one = hidden + attn_branch + biases[2]
    normed = layer_norm(resid_one, gains[0], biases[4 + rows_hidden])
    bias_hidden = biases[3:3 + rows_hidden].reshape(FF)
    pre_act = low_back(jnp.einsum('psd,df->psf', low(normed), w_in, precision=HIGHEST) + bias_hidden)
    activated = low(jax.nn.gelu(pre_act, approximate=False))
    ffn_branch = low_back(jnp.einsum('psf,fd->psd', activated, w_down, precision=HIGHEST))
    resid_two = normed + ffn_branch + biases[3 + rows_hidden]
    return layer_norm(resid_two, gains[1], biases[5 + rows_hidden])

def reference(hidden_in, cotangent, prefix, w_qkv, w_out, w_in, w_down, biases, gains):
    group_size = math.gcd(SEQS, 4)
    n_groups = SEQS // group_size
    mat_qkv = w_qkv.astype(jnp.float32)
    mat_out = w_out.astype(jnp.float32)
    mat_in = w_in.astype(jnp.float32)
    mat_down = w_down.astype(jnp.float32)
    hidden_groups = jnp.transpose(hidden_in.reshape(L, n_groups, group_size, D), (1, 0, 2, 3))
    cot_groups = jnp.transpose(cotangent.reshape(L, n_groups, group_size, D), (1, 0, 2, 3))
    prefix_groups = prefix.reshape(n_groups, group_size)

    def one_group(totals, operands):
        hidden_one, cot_one, prefix_one = operands

        def apply_layer(hidden_val, qkv_val, out_val, in_val, down_val, bias_val, gain_val):
            return forward(hidden_val, qkv_val, out_val, in_val, down_val, bias_val, gain_val, prefix_one)
        out_value, pullback = jax.vjp(apply_layer, hidden_one.astype(jnp.float32), mat_qkv, mat_out, mat_in, mat_down, biases, gains)
        grad_terms = pullback(cot_one.astype(jnp.float32))
        new_totals = tuple((acc + term for acc, term in zip(totals, grad_terms[1:])))
        return (new_totals, (out_value.astype(jnp.bfloat16), grad_terms[0].astype(jnp.bfloat16)))
    start_totals = (jnp.zeros(mat_qkv.shape, jnp.float32), jnp.zeros(mat_out.shape, jnp.float32), jnp.zeros(mat_in.shape, jnp.float32), jnp.zeros(mat_down.shape, jnp.float32), jnp.zeros(biases.shape, jnp.float32), jnp.zeros(gains.shape, jnp.float32))
    totals, (outputs, grad_hidden) = lax.scan(one_group, start_totals, (hidden_groups, cot_groups, prefix_groups))
    output = jnp.transpose(outputs, (1, 0, 2, 3)).reshape(L, SEQS, D)
    grad_input = jnp.transpose(grad_hidden, (1, 0, 2, 3)).reshape(L, SEQS, D)
    return (output, grad_input, totals[0], totals[1], totals[2], totals[3], totals[4], totals[5])
```

```python
import functools
import math

import jax
import jax.numpy as jnp
from jax import lax
from jax.experimental import pallas as pl
from jax.experimental.pallas import tpu as pltpu
from jax.sharding import PartitionSpec as P

f32=jnp.float32; bf16=jnp.bfloat16
L=1024; QB=256; NK=(512,512,768,1024)
C2=0.125*math.log2(math.e)
NEG=-1e30
def dotf(a,b): return jnp.dot(a,b,preferred_element_type=f32)
def dot_nt(a,b): return lax.dot_general(a,b,(((1,),(1,)),((),())),preferred_element_type=f32)
def masks(mask_ref, prefix):
    k=lax.broadcasted_iota(jnp.int32,(256,256),0); q=lax.broadcasted_iota(jnp.int32,(256,256),1)
    diag=k<=q
    mask_ref[0]=jnp.where(diag|(k<prefix),0.0,NEG)
    mask_ref[1]=jnp.where(k+256<prefix,0.0,NEG)+jnp.zeros((256,256),f32)
    mask_ref[2]=jnp.where(diag|(k+256<prefix),0.0,NEG)
    mask_ref[3]=jnp.where(diag,0.0,NEG)
MASKMAP={0:{0:0,1:1},1:{1:2},2:{2:3},3:{3:3}}
def masked(st,qb,mask_ref):
    parts=[]
    for kb in range(NK[qb]//256):
        p=st[kb*256:(kb+1)*256]
        mi=MASKMAP[qb].get(kb)
        parts.append(p if mi is None else p+mask_ref[mi])
    return jnp.concatenate(parts,0)
def fwd_kernel(prefix_ref,x_ref,w_ref,b_ref,proj_ref,projT_ref,heads_ref,ot_ref,lse_ref,zq_ref,mask_ref):
    masks(mask_ref,prefix_ref[0])
    proj=(dotf(x_ref[...],w_ref[:,:640])+b_ref[...]).astype(bf16)
    proj_ref[...]=proj
    projT_ref[...]=proj.T
    zq_ref[...]=jnp.zeros_like(zq_ref)
    for h in range(3):
        zq_ref[h,64+64*h:128+64*h,:]=projT_ref[64*h:64*h+64,:]
    ot_ref[...]=jnp.zeros_like(ot_ref)
    for h in range(3):
        for qb in range(4):
            nk=NK[qb]; qs=slice(qb*QB,qb*QB+QB)
            st=dotf(proj_ref[:nk,128:384],zq_ref[h,:,qs])
            st=masked(st,qb,mask_ref)
            m=jnp.max(st,axis=0,keepdims=True)
            p=jnp.exp2((st-m)*C2)
            l=jnp.sum(p,axis=0,keepdims=True)
            ot=dotf(projT_ref[384+64*h:448+64*h,:nk],p.astype(bf16))
            ot_ref[64+64*h:128+64*h,qs]=(ot/l).astype(bf16)
            lse_ref[h:h+1,qs]=m*C2+jnp.log2(l)
    heads_ref[...]=ot_ref[...].T
def attn_fwd(prefix,x,w1,bqkv):
    sq=pl.squeezed
    return pl.pallas_call(fwd_kernel,grid_spec=pltpu.PrefetchScalarGridSpec(num_scalar_prefetch=1,grid=(4,),
      in_specs=[pl.BlockSpec((L,768),lambda t,p:(0,0)),pl.BlockSpec((sq,768,768),lambda t,p:(t,0,0)),pl.BlockSpec((sq,1,640),lambda t,p:(t,0,0))],
      out_specs=[pl.BlockSpec((sq,L,640),lambda t,p:(t,0,0)),pl.BlockSpec((sq,640,L),lambda t,p:(t,0,0)),pl.BlockSpec((sq,L,256),lambda t,p:(t,0,0)),pl.BlockSpec((sq,256,L),lambda t,p:(t,0,0)),pl.BlockSpec((sq,8,L),lambda t,p:(t,0,0))],
      scratch_shapes=[pltpu.VMEM((3,256,L),bf16),pltpu.VMEM((4,256,256),f32)]),
      out_shape=[jax.ShapeDtypeStruct((4,L,640),bf16),jax.ShapeDtypeStruct((4,640,L),bf16),jax.ShapeDtypeStruct((4,L,256),bf16),jax.ShapeDtypeStruct((4,256,L),bf16),jax.ShapeDtypeStruct((4,8,L),f32)],
      compiler_params=pltpu.CompilerParams(vmem_limit_bytes=62<<20))(prefix,x,w1,bqkv)
def bwd_kernel(prefix_ref,g_ref,w_ref,proj_ref,projT_ref,ot_ref,lse_ref,gproj_ref,
               zq_ref,zdo_ref,qm_ref,dom_ref,pt_ref,ds_ref,mask_ref,gt_ref,dqt_ref):
    masks(mask_ref,prefix_ref[0])
    gh=dotf(g_ref[...],w_ref[:,512:768]).astype(bf16)
    gt_ref[...]=gh.T
    zq_ref[...]=jnp.zeros_like(zq_ref); zdo_ref[...]=jnp.zeros_like(zdo_ref)
    lane=lax.broadcasted_iota(jnp.int32,(1,256),1)
    for h in range(3):
        zq_ref[h,64+64*h:128+64*h,:]=projT_ref[64*h:64*h+64,:]
        zdo_ref[h,64*h:64*h+64,:]=gt_ref[64+64*h:128+64*h,:]*0.125
        sel=(lane>=64*h)&(lane<64*h+64)
        qm_ref[h]=jnp.where(sel,proj_ref[:,0:256],0)
        sel2=(lane>=64*h+64)&(lane<64*h+128)
        dom_ref[h]=jnp.where(sel2,gh,0)
    for h in range(3):
        d=jnp.sum(gt_ref[64+64*h:128+64*h,:].astype(f32)*ot_ref[64+64*h:128+64*h,:].astype(f32),axis=0,keepdims=True)*0.125
        for qb in range(4):
            nk=NK[qb]; qs=slice(qb*QB,qb*QB+QB)
            st=dotf(proj_ref[:nk,128:384],zq_ref[h,:,qs])
            st=masked(st,qb,mask_ref)
            p=jnp.exp2(st*C2-lse_ref[h:h+1,qs])
            dp=dotf(proj_ref[:nk,384:640],zdo_ref[h,:,qs])
            ds=(p*(dp-d[:,qs])).astype(bf16)
            pt_ref[h,:nk,qs]=p.astype(bf16)
            ds_ref[h,:nk,qs]=ds
            dqt_ref[64*h:64*h+64,qs]=dotf(projT_ref[192+64*h:256+64*h,:nk],ds).astype(bf16)
    gproj_ref[:,0:192]=dqt_ref[...].T
    for (k0,k1,q0) in ((0,512,0),(512,768,512),(768,1024,768)):
        dk=jnp.zeros((k1-k0,256),f32); dv=jnp.zeros((k1-k0,256),f32)
        for h in range(3):
            dk=dk+dotf(ds_ref[h,k0:k1,q0:],qm_ref[h,q0:,:])
            dv=dv+dotf(pt_ref[h,k0:k1,q0:],dom_ref[h,q0:,:])
        gproj_ref[k0:k1,192:384]=dk[:,0:192].astype(bf16)
        gproj_ref[k0:k1,384:576]=dv[:,64:256].astype(bf16)
    gproj_ref[:,576:640]=jnp.zeros((L,64),bf16)
def attn_bwd(prefix,g,w1,proj,projT,ot,lse):
    sq=pl.squeezed
    sp=lambda *s: pl.BlockSpec((sq,)+s,lambda t,p:(t,0,0))
    return pl.pallas_call(functools.partial(bwd_kernel),grid_spec=pltpu.PrefetchScalarGridSpec(num_scalar_prefetch=1,grid=(4,),
      in_specs=[pl.BlockSpec((L,768),lambda t,p:(0,0)),sp(768,768),sp(L,640),sp(640,L),sp(256,L),sp(8,L)],
      out_specs=sp(L,640),
      scratch_shapes=[pltpu.VMEM((3,256,L),bf16),pltpu.VMEM((3,256,L),bf16),pltpu.VMEM((3,L,256),bf16),pltpu.VMEM((3,L,256),bf16),pltpu.VMEM((3,L,L),bf16),pltpu.VMEM((3,L,L),bf16),pltpu.VMEM((4,256,256),f32),pltpu.VMEM((256,L),bf16),pltpu.VMEM((192,L),bf16)]),
      out_shape=jax.ShapeDtypeStruct((4,L,640),bf16),
      compiler_params=pltpu.CompilerParams(vmem_limit_bytes=62<<20))(prefix,g,w1,proj,projT,ot,lse)
MESH=pl.DeviceIdType.MESH
class Place:
    def __init__(self):
        dp=lax.axis_index("dp"); t=lax.axis_index("tensor")
        self.dp,self.t=dp,t
        self.z,self.x,self.y,self.c=dp//2,dp%2,t//2,t%2
    def peer(self,dim,j=1):
        return {'x':lambda:(self.dp^1,self.t),'z':lambda:(self.dp^(2*j),self.t),'y':lambda:(self.dp,self.t^2),'c':lambda:(self.dp,self.t^1)}[dim]()
    def peers_all(self):
        return [self.peer('x'),self.peer('y'),self.peer('c'),self.peer('z',1),self.peer('z',2),self.peer('z',3),(self.dp,self.t^3)]
def barrier(peers):
    b=pltpu.get_barrier_semaphore()
    for p in peers: pl.semaphore_signal(b,inc=1,device_id=p,device_id_type=MESH)
    pl.semaphore_wait(b,len(peers))
class Sems:
    def __init__(self,send,recv): self.s,self.r,self.n=send,recv,0
    def take(self):
        i=self.n; self.n+=1
        return self.s.at[i],self.r.at[i]
def rcopy(src,dst,sems,dev):
    a,b=sems.take()
    return pltpu.make_async_remote_copy(src_ref=src,dst_ref=dst,send_sem=a,recv_sem=b,device_id=dev,device_id_type=MESH)
class Gather:
    def __init__(self,pc,src,dst,rows,order,sems):
        self.pc,self.src,self.dst,self.rows,self.order,self.sems=pc,src,dst,rows,order,sems
        self.full=set(); self.pend=[]; self.core=[]
    def at(self,ref,over,full):
        pc=self.pc; ix={}
        for d in 'yzx':
            if d in over: ix[d]=over[d]
            elif d in full: ix[d]=slice(None)
            else: ix[d]=pl.ds(getattr(pc,d),1)
        i=(ix['y'],pl.ds(pc.c,1),ix['z'],ix['x'])
        if self.rows is not None: i=i+(pl.ds(*self.rows),)
        return ref.at[i]
    def to_core(self,over,full):
        sl=self.at(self.dst,over,full)
        k=rcopy(sl,sl,self.sems,self.pc.peer('c')); k.start(); self.core.append(k)
    def phase(self,p):
        if p>0: self.finish()
        if p==0: self.to_core({},self.full)
        d=self.order[p];
        for j in ((1,2,3) if d=='z' else (1,)):
            sl=self.at(self.dst,{},self.full)
            k=rcopy(sl,sl,self.sems,self.pc.peer(d,j)); k.start()
            self.pend.append((k,{d:pl.ds(getattr(self.pc,d)^j,1)},set(self.full)))
        self.full.add(d)
    def finish(self):
        for k,over,full in self.pend:
            k.wait_recv(); self.to_core(over,full)
        self.done=getattr(self,'done',[])+[k for k,_,_ in self.pend]
        self.pend=[]
    def drain(self):
        for k in self.core: k.wait_recv()
        for k in self.core+self.done: k.wait_send()
def local(src,dst,sem):
    k=pltpu.make_async_copy(src,dst,sem); k.start(); return k
def exchange(pc,src,dst,sems):
    out=[]
    for j in (2,3,1):
        p=(pc.dp,pc.t^j)
        k=rcopy(src.at[pc.t^j],dst.at[pc.t],sems,p); k.start(); out.append(k)
    return out
N_AG=6*11+11+6
ORD=(('z','y','x'),('z','x','y'))
def ag_kernel(s_ref,h_ref,c_ref,b_ref,g_ref,xo_ref,co_ref,bo_ref,ss,rs,ls):
    pc=Place(); sems=Sems(ss,rs)
    own=(pc.y,pc.c,pc.z,pc.x)
    loc=[local(s_ref.at[g],g_ref.at[g].at[own],ls.at[g]) for g in range(3)]
    loc+=[local(b_ref,bo_ref.at[own],ls.at[3]),local(h_ref.at[pc.t],xo_ref.at[pc.t],ls.at[4]),local(c_ref.at[pc.t],co_ref.at[pc.t],ls.at[5])]
    barrier(pc.peers_all())
    hx=exchange(pc,h_ref,xo_ref,sems)
    for k in loc: k.wait()
    gs=[Gather(pc,None,bo_ref,None,ORD[0],sems)]
    gs+=[Gather(pc,None,g_ref.at[g],(48*i,48),ORD[i],sems) for g in range(3) for i in range(2)]
    for p in range(3):
        for k in gs: k.phase(p)
    cx=exchange(pc,c_ref,co_ref,sems)
    for k in gs: k.finish()
    for k in gs: k.drain()
    for k in hx+cx: k.wait()
HBM=pl.BlockSpec(memory_space=pltpu.HBM); VM=pl.BlockSpec(memory_space=pltpu.VMEM)
def gather_all(s,h,c,b):
    return pl.pallas_call(ag_kernel,out_shape=[jax.ShapeDtypeStruct((3,2,2,4,2)+s.shape[1:],bf16),jax.ShapeDtypeStruct(h.shape,bf16),jax.ShapeDtypeStruct(c.shape,bf16),jax.ShapeDtypeStruct((2,2,4,2)+b.shape,f32)],
      in_specs=[HBM]*4,out_specs=[HBM]*4,scratch_shapes=[pltpu.SemaphoreType.DMA((N_AG,)),pltpu.SemaphoreType.DMA((N_AG,)),pltpu.SemaphoreType.DMA((6,))],
      compiler_params=pltpu.CompilerParams(collective_id=0,has_side_effects=True))(s,h,c,b)
N_RS=36+6+6
def rs_kernel(d_ref,v_ref,o_ref,x_ref,gs_ref,vs_ref,oo_ref,xo_ref,lc,rc,r1a,r1b,r2,r3,vb,vr,ss,rs,ls):
    pc=Place(); sems=Sems(ss,rs)
    loc=[local(o_ref.at[pc.t],oo_ref.at[pc.t],ls.at[0]),local(x_ref.at[pc.t],xo_ref.at[pc.t],ls.at[1])]
    lk=[]
    for k in range(6):
        g,i=divmod(k,2)
        lk.append(local(d_ref.at[g,:,pc.c,:,:,pl.ds(48*i,48)],lc.at[k],ls.at[2+k]))
    barrier(pc.peers_all())
    tail=[]
    cur=[]
    for k in range(6):
        g,i=divmod(k,2)
        q=rcopy(d_ref.at[g,:,1-pc.c,:,:,pl.ds(48*i,48)],rc.at[k],sems,pc.peer('c')); q.start(); cur.append(q)
    vb[0]=v_ref[...]
    vq=rcopy(vb.at[0],vr.at[0],sems,pc.peer('c')); vq.start()
    ox=exchange(pc,o_ref,oo_ref,sems)
    n1=[]
    for k in range(6):
        i=k%2
        lk[k].wait(); cur[k].wait_recv()
        def add(j,_):
            y,z,x=j//8,(j//2)%4,j%2
            lc[k,y,z,x]=(lc[k,y,z,x].astype(f32)+rc[k,y,z,x].astype(f32)).astype(bf16)
            return 0
        lax.fori_loop(0,16,add,0)
        if i==0:
            q=rcopy(lc.at[k,:,:,1-pc.x],r1a.at[k//2],sems,pc.peer('x'))
        else:
            q=rcopy(lc.at[k,1-pc.y],r1b.at[k//2],sems,pc.peer('y'))
        q.start(); n1.append(q)
    xx=exchange(pc,x_ref,xo_ref,sems)
    vq.wait_recv(); tail.append(vq)
    vb[1]=vb[0]+vr[0]
    vq=rcopy(vb.at[1],vr.at[1],sems,pc.peer('x')); vq.start()
    n2=[]
    for k in range(6):
        i=k%2
        n1[k].wait_recv()
        def add(j,_):
            if i==0:
                a,z=j//4,j%4
                lc[k,a,z,pc.x]=(lc[k,a,z,pc.x].astype(f32)+r1a[k//2,a,z].astype(f32)).astype(bf16)
            else:
                z,x=j//2,j%2
                lc[k,pc.y,z,x]=(lc[k,pc.y,z,x].astype(f32)+r1b[k//2,z,x].astype(f32)).astype(bf16)
            return 0
        lax.fori_loop(0,8,add,0)
        if i==0: q=rcopy(lc.at[k,1-pc.y,:,pc.x],r2.at[k],sems,pc.peer('y'))
        else: q=rcopy(lc.at[k,pc.y,:,1-pc.x],r2.at[k],sems,pc.peer('x'))
        q.start(); n2.append(q)
    vq.wait_recv(); tail.append(vq)
    vb[2]=vb[1]+vr[1]
    vq=rcopy(vb.at[2],vr.at[2],sems,pc.peer('y')); vq.start()
    n3=[]
    for k in range(6):
        n2[k].wait_recv()
        def add(z,_):
            lc[k,pc.y,z,pc.x]=(lc[k,pc.y,z,pc.x].astype(f32)+r2[k,z].astype(f32)).astype(bf16)
            return 0
        lax.fori_loop(0,4,add,0)
        qs=[]
        for j in (3,2,1):
            q=rcopy(lc.at[k,pc.y,pc.z^j,pc.x],r3.at[k,j-1],sems,pc.peer('z',j)); q.start(); qs.append(q)
        n3.append(qs)
    vq.wait_recv(); tail.append(vq)
    vb[3]=vb[2]+vr[2]
    vqs=[]
    for j in (3,2,1):
        q=rcopy(vb.at[3],vr.at[2+j],sems,pc.peer('z',j)); q.start(); vqs.append(q)
    for k in range(6):
        g,i=divmod(k,2)
        for q in n3[k]: q.wait_recv()
        gs_ref[g,48*i:48*i+48]=(lc[k,pc.y,pc.z,pc.x].astype(f32)+r3[k,0].astype(f32))+(r3[k,1].astype(f32)+r3[k,2].astype(f32))
    for q in vqs: q.wait_recv()
    vs_ref[...]=(vb[3]+vr[3])+(vr[4]+vr[5])
    for q in loc: q.wait()
    for q in ox+xx: q.wait()
    for q in cur+n1+n2+sum(n3,[])+vqs+tail: q.wait_send()
def reduce_all(d,v,o,x):
    r=d.shape[5]
    return pl.pallas_call(rs_kernel,out_shape=[jax.ShapeDtypeStruct((3,r,768),f32),jax.ShapeDtypeStruct(v.shape,f32),jax.ShapeDtypeStruct(o.shape,bf16),jax.ShapeDtypeStruct(x.shape,bf16)],
      in_specs=[HBM,VM,HBM,HBM],out_specs=[VM,VM,HBM,HBM],
      scratch_shapes=[pltpu.VMEM((6,2,4,2,48,768),bf16),pltpu.VMEM((6,2,4,2,48,768),bf16),pltpu.VMEM((3,2,4,48,768),bf16),pltpu.VMEM((3,4,2,48,768),bf16),pltpu.VMEM((6,4,48,768),bf16),pltpu.VMEM((6,3,48,768),bf16),pltpu.VMEM((4,16,768),f32),pltpu.VMEM((6,16,768),f32),
        pltpu.SemaphoreType.DMA((N_RS,)),pltpu.SemaphoreType.DMA((N_RS,)),pltpu.SemaphoreType.DMA((8,))],
      compiler_params=pltpu.CompilerParams(collective_id=1,has_side_effects=True,vmem_limit_bytes=62<<20))(d,v,o,x)


EPSILON = 1e-12


def norm_stats(r):
    center = r - jnp.mean(r, axis=-1, keepdims=True)
    inv = lax.rsqrt(jnp.mean(center * center, axis=-1, keepdims=True) + EPSILON)
    return center * inv, inv


def norm_back(cot, gain, xhat, inv):
    e = cot * gain
    grad = (e - jnp.mean(e, -1, keepdims=True) - xhat * jnp.mean(e * xhat, -1, keepdims=True)) * inv
    return grad, jnp.sum(cot * xhat, 0), jnp.sum(cot, 0)


def middle(x, cot, heads, w1, w2, w3, bias_o, bias_h, bias_d, shift1, shift2, gain1, gain2):
    ein = functools.partial(jnp.einsum, preferred_element_type=f32)
    hid = x.astype(f32)
    resid1 = hid + ein("tpw,tdw->pd", heads, w1[:, :, 512:]) + bias_o
    xhat1, inv1 = norm_stats(resid1)
    normed = xhat1 * gain1 + shift1
    low = normed.astype(bf16)
    pre = ein("pd,tdf->tpf", low, w2) + bias_h[:, None, :]
    act, gelu_back = jax.vjp(lambda v: jax.nn.gelu(v, approximate=False), pre)
    act = act.astype(bf16)
    resid2 = normed + ein("tpf,tdf->pd", act, w3) + bias_d
    xhat2, inv2 = norm_stats(resid2)
    out = (xhat2 * gain2 + shift2).astype(bf16)
    g2, dgain2, dshift2 = norm_back(cot.astype(f32), gain2, xhat2, inv2)
    g2low = g2.astype(bf16)
    d3 = ein("pd,tpf->tdf", g2low, act).astype(bf16)
    gpre = gelu_back(ein("pd,tdf->tpf", g2low, w3))[0].astype(bf16)
    d2 = ein("pd,tpf->tdf", low, gpre).astype(bf16)
    gn = g2 + ein("tpf,tdf->pd", gpre, w2)
    g1, dgain1, dshift1 = norm_back(gn, gain1, xhat1, inv1)
    g1low = g1.astype(bf16)
    dout = ein("pd,tpw->tdw", g1low, heads[:, :, 64:]).astype(bf16)
    dbh = jnp.sum(gpre, 1, dtype=f32)
    return out, g1, g1low, dout, d2, d3, (dgain1, dgain2, dshift1, dshift2, jnp.sum(g1, 0), dbh, jnp.sum(g2, 0))


def on_device(hidden_in, cotangent, prefix, w_qkv, w_out, w_in, w_down, biases, gains):
    rows = w_qkv.shape[0]
    n_t = lax.axis_size("tensor")
    t_me, d_me = lax.axis_index("tensor"), lax.axis_index("dp")
    n_dev = n_t * lax.axis_size("dp")
    s = jnp.stack([jnp.concatenate([w_qkv.reshape(rows, -1), w_out.T], axis=1), w_in, w_down.T])
    vecs = jnp.concatenate([biases, gains], 0)
    width = vecs.shape[1]
    vecs = jnp.pad(vecs, ((0, 4), (0, 128 - width)))
    seqs = lambda a: jnp.transpose(a, (1, 0, 2))
    h, c = seqs(hidden_in), seqs(cotangent)
    if lax.axis_size("dp") == 8:
        g, xs, cs, b = gather_all(s, h, c, vecs)
        b = b.transpose(2, 3, 0, 1, 4, 5)
    else:
        g = lax.all_gather(lax.all_gather(s, "dp", axis=1, tiled=True), "tensor", axis=1)
        xs = lax.all_to_all(h, "tensor", 0, 0, tiled=True)
        cs = lax.all_to_all(c, "tensor", 0, 0, tiled=True)
        b = lax.all_gather(vecs, ("dp", "tensor"), axis=0)
    w1, w2, w3 = [a.reshape(n_t, 768, 768) for a in g]
    vec = b.reshape(n_dev, 16, 128)[:, :12, :width].transpose(1, 0, 2).reshape(12, 768)
    x = xs.reshape(1024, 768)
    bqkv = jnp.pad(jnp.stack([vec[0].reshape(4, 192), jnp.zeros((4, 192), f32), vec[1].reshape(4, 192)], 1).reshape(4, 1, 576), ((0, 0), (0, 0), (0, 64)))
    my_prefix = lax.dynamic_slice_in_dim(prefix, t_me, 1, 0)
    proj, projT, heads, ot, lse = attn_fwd(my_prefix, x, w1, bqkv)
    out, g1, g1low, dout, d2, d3, small = middle(
        x, cs.reshape(1024, 768), heads, w1, w2, w3, vec[2], vec[3:7].reshape(4, 768), vec[7], vec[8], vec[9], vec[10], vec[11]
    )
    gproj = attn_bwd(my_prefix, g1low, w1, proj, projT, ot, lse)
    ein = functools.partial(jnp.einsum, preferred_element_type=f32)
    gp = gproj[:, :, :576]
    dqkv = ein("pd,tpc->tdc", x, gp).astype(bf16)
    dx = (g1 + ein("tpc,tdc->pd", gp, w1[:, :, :576])).astype(bf16)
    dgain1, dgain2, dshift1, dshift2, dbo, dbh, dbd = small
    dbq = jnp.sum(gp[:, :, :192], 1, dtype=f32).reshape(768)
    dbv = jnp.sum(gp[:, :, 384:], 1, dtype=f32).reshape(768)
    v = jnp.concatenate([jnp.stack([dbq, dbv, dbo]), dbh, jnp.stack([dbd, dshift1, dshift2, dgain1, dgain2]), jnp.zeros((4, 768), f32)])
    d = jnp.stack([jnp.concatenate([dqkv, dout], 2), d2, d3])
    o4, x4 = out.reshape(4, 256, 768), dx.reshape(4, 256, 768)
    if lax.axis_size("dp") == 8:
        gs, vs, oo, xx = reduce_all(d.reshape(3, 2, 2, 4, 2, rows, 768), v, o4, x4)
    else:
        part = lax.all_to_all(d, "tensor", 1, 1, tiled=True).astype(f32).sum(1)
        part = part.astype(bf16).reshape(3, -1, rows, 768)
        gs = lax.all_to_all(part, "dp", 1, 1, tiled=True).astype(f32).sum(1)
        vs = lax.psum(v, ("dp", "tensor"))
        oo = lax.all_to_all(o4, "tensor", 0, 0, tiled=True)
        xx = lax.all_to_all(x4, "tensor", 0, 0, tiled=True)
    mine = lax.dynamic_slice_in_dim(vs, (d_me * n_t + t_me) * width, width, 1)
    return (
        seqs(oo),
        seqs(xx),
        gs[0, :, :576].reshape(rows, 3, 192),
        gs[0, :, 576:].T,
        gs[1],
        gs[2].T,
        mine[:10],
        mine[10:12],
    )


def solution(mesh):
    placed = (
        P("tensor", "dp", None),
        P("tensor", "dp", None),
        P("dp"),
        P("dp", None, "tensor"),
        P("tensor", "dp"),
        P("dp", "tensor"),
        P("tensor", "dp"),
        P(None, ("dp", "tensor")),
        P(None, ("dp", "tensor")),
    )
    return jax.shard_map(on_device, mesh=mesh, in_specs=placed, out_specs=placed[:2] + placed[3:], check_vma=False)
```

```python
import functools
import math

import jax
import jax.numpy as jnp
from jax import lax
from jax.experimental import pallas as pl
from jax.experimental.pallas import tpu as pltpu
from jax.sharding import PartitionSpec as P

f32=jnp.float32; bf16=jnp.bfloat16
L=1024; QB=256; NK=(512,512,768,1024)
C2=0.125*math.log2(math.e)
NEG=-1e30
def dotf(a,b): return jnp.dot(a,b,preferred_element_type=f32)
def dot_nt(a,b): return lax.dot_general(a,b,(((1,),(1,)),((),())),preferred_element_type=f32)
def masks(mask_ref, prefix):
    k=lax.broadcasted_iota(jnp.int32,(256,256),0); q=lax.broadcasted_iota(jnp.int32,(256,256),1)
    diag=k<=q
    mask_ref[0]=jnp.where(diag|(k<prefix),0.0,NEG)
    mask_ref[1]=jnp.where(k+256<prefix,0.0,NEG)+jnp.zeros((256,256),f32)
    mask_ref[2]=jnp.where(diag|(k+256<prefix),0.0,NEG)
    mask_ref[3]=jnp.where(diag,0.0,NEG)
MASKMAP={0:{0:0,1:1},1:{1:2},2:{2:3},3:{3:3}}
def masked(st,qb,mask_ref):
    parts=[]
    for kb in range(NK[qb]//256):
        p=st[kb*256:(kb+1)*256]
        mi=MASKMAP[qb].get(kb)
        parts.append(p if mi is None else p+mask_ref[mi])
    return jnp.concatenate(parts,0)
def fwd_kernel(prefix_ref,x_ref,w_ref,b_ref,proj_ref,projT_ref,heads_ref,ot_ref,lse_ref,zq_ref,mask_ref):
    masks(mask_ref,prefix_ref[0])
    proj=(dotf(x_ref[...],w_ref[:,:640])+b_ref[...]).astype(bf16)
    proj_ref[...]=proj
    projT_ref[...]=proj.T
    zq_ref[...]=jnp.zeros_like(zq_ref)
    for h in range(3):
        zq_ref[h,64+64*h:128+64*h,:]=projT_ref[64*h:64*h+64,:]
    ot_ref[...]=jnp.zeros_like(ot_ref)
    for h in range(3):
        for qb in range(4):
            nk=NK[qb]; qs=slice(qb*QB,qb*QB+QB)
            st=dotf(proj_ref[:nk,128:384],zq_ref[h,:,qs])
            st=masked(st,qb,mask_ref)
            m=jnp.max(st,axis=0,keepdims=True)
            p=jnp.exp2((st-m)*C2)
            l=jnp.sum(p,axis=0,keepdims=True)
            ot=dotf(projT_ref[384+64*h:448+64*h,:nk],p.astype(bf16))
            ot_ref[64+64*h:128+64*h,qs]=(ot/l).astype(bf16)
            lse_ref[h:h+1,qs]=m*C2+jnp.log2(l)
    heads_ref[...]=ot_ref[...].T
def attn_fwd(prefix,x,w1,bqkv):
    sq=pl.squeezed
    return pl.pallas_call(fwd_kernel,grid_spec=pltpu.PrefetchScalarGridSpec(num_scalar_prefetch=1,grid=(4,),
      in_specs=[pl.BlockSpec((L,768),lambda t,p:(0,0)),pl.BlockSpec((sq,768,768),lambda t,p:(t,0,0)),pl.BlockSpec((sq,1,640),lambda t,p:(t,0,0))],
      out_specs=[pl.BlockSpec((sq,L,640),lambda t,p:(t,0,0)),pl.BlockSpec((sq,640,L),lambda t,p:(t,0,0)),pl.BlockSpec((sq,L,256),lambda t,p:(t,0,0)),pl.BlockSpec((sq,256,L),lambda t,p:(t,0,0)),pl.BlockSpec((sq,8,L),lambda t,p:(t,0,0))],
      scratch_shapes=[pltpu.VMEM((3,256,L),bf16),pltpu.VMEM((4,256,256),f32)]),
      out_shape=[jax.ShapeDtypeStruct((4,L,640),bf16),jax.ShapeDtypeStruct((4,640,L),bf16),jax.ShapeDtypeStruct((4,L,256),bf16),jax.ShapeDtypeStruct((4,256,L),bf16),jax.ShapeDtypeStruct((4,8,L),f32)],
      compiler_params=pltpu.CompilerParams(vmem_limit_bytes=62<<20))(prefix,x,w1,bqkv)
def bwd_kernel(prefix_ref,g_ref,w_ref,proj_ref,projT_ref,ot_ref,lse_ref,gproj_ref,
               zq_ref,zdo_ref,qm_ref,dom_ref,pt_ref,ds_ref,mask_ref,gt_ref,dqt_ref):
    masks(mask_ref,prefix_ref[0])
    gh=dotf(g_ref[...],w_ref[:,512:768]).astype(bf16)
    gt_ref[...]=gh.T
    zq_ref[...]=jnp.zeros_like(zq_ref); zdo_ref[...]=jnp.zeros_like(zdo_ref)
    lane=lax.broadcasted_iota(jnp.int32,(1,256),1)
    for h in range(3):
        zq_ref[h,64+64*h:128+64*h,:]=projT_ref[64*h:64*h+64,:]
        zdo_ref[h,64*h:64*h+64,:]=gt_ref[64+64*h:128+64*h,:]*0.125
        sel=(lane>=64*h)&(lane<64*h+64)
        qm_ref[h]=jnp.where(sel,proj_ref[:,0:256],0)
        sel2=(lane>=64*h+64)&(lane<64*h+128)
        dom_ref[h]=jnp.where(sel2,gh,0)
    for h in range(3):
        d=jnp.sum(gt_ref[64+64*h:128+64*h,:].astype(f32)*ot_ref[64+64*h:128+64*h,:].astype(f32),axis=0,keepdims=True)*0.125
        for qb in range(4):
            nk=NK[qb]; qs=slice(qb*QB,qb*QB+QB)
            st=dotf(proj_ref[:nk,128:384],zq_ref[h,:,qs])
            st=masked(st,qb,mask_ref)
            p=jnp.exp2(st*C2-lse_ref[h:h+1,qs])
            dp=dotf(proj_ref[:nk,384:640],zdo_ref[h,:,qs])
            ds=(p*(dp-d[:,qs])).astype(bf16)
            pt_ref[h,:nk,qs]=p.astype(bf16)
            ds_ref[h,:nk,qs]=ds
            dqt_ref[64*h:64*h+64,qs]=dotf(projT_ref[192+64*h:256+64*h,:nk],ds).astype(bf16)
    gproj_ref[:,0:192]=dqt_ref[...].T
    for (k0,k1,q0) in ((0,512,0),(512,768,512),(768,1024,768)):
        dk=jnp.zeros((k1-k0,256),f32); dv=jnp.zeros((k1-k0,256),f32)
        for h in range(3):
            dk=dk+dotf(ds_ref[h,k0:k1,q0:],qm_ref[h,q0:,:])
            dv=dv+dotf(pt_ref[h,k0:k1,q0:],dom_ref[h,q0:,:])
        gproj_ref[k0:k1,192:384]=dk[:,0:192].astype(bf16)
        gproj_ref[k0:k1,384:576]=dv[:,64:256].astype(bf16)
    gproj_ref[:,576:640]=jnp.zeros((L,64),bf16)
def attn_bwd(prefix,g,w1,proj,projT,ot,lse):
    sq=pl.squeezed
    sp=lambda *s: pl.BlockSpec((sq,)+s,lambda t,p:(t,0,0))
    return pl.pallas_call(functools.partial(bwd_kernel),grid_spec=pltpu.PrefetchScalarGridSpec(num_scalar_prefetch=1,grid=(4,),
      in_specs=[pl.BlockSpec((L,768),lambda t,p:(0,0)),sp(768,768),sp(L,640),sp(640,L),sp(256,L),sp(8,L)],
      out_specs=sp(L,640),
      scratch_shapes=[pltpu.VMEM((3,256,L),bf16),pltpu.VMEM((3,256,L),bf16),pltpu.VMEM((3,L,256),bf16),pltpu.VMEM((3,L,256),bf16),pltpu.VMEM((3,L,L),bf16),pltpu.VMEM((3,L,L),bf16),pltpu.VMEM((4,256,256),f32),pltpu.VMEM((256,L),bf16),pltpu.VMEM((192,L),bf16)]),
      out_shape=jax.ShapeDtypeStruct((4,L,640),bf16),
      compiler_params=pltpu.CompilerParams(vmem_limit_bytes=62<<20))(prefix,g,w1,proj,projT,ot,lse)
MESH=pl.DeviceIdType.MESH
class Place:
    def __init__(self):
        dp=lax.axis_index("dp"); t=lax.axis_index("tensor")
        self.dp,self.t=dp,t
        self.z,self.x,self.y,self.c=dp//2,dp%2,t//2,t%2
    def peer(self,dim,j=1):
        return {'x':lambda:(self.dp^1,self.t),'z':lambda:(self.dp^(2*j),self.t),'y':lambda:(self.dp,self.t^2),'c':lambda:(self.dp,self.t^1)}[dim]()
    def peers_all(self):
        return [self.peer('x'),self.peer('y'),self.peer('c'),self.peer('z',1),self.peer('z',2),self.peer('z',3),(self.dp,self.t^3)]
def barrier(peers):
    b=pltpu.get_barrier_semaphore()
    for p in peers: pl.semaphore_signal(b,inc=1,device_id=p,device_id_type=MESH)
    pl.semaphore_wait(b,len(peers))
class Sems:
    def __init__(self,send,recv): self.s,self.r,self.n=send,recv,0
    def take(self):
        i=self.n; self.n+=1
        return self.s.at[i],self.r.at[i]
def rcopy(src,dst,sems,dev):
    a,b=sems.take()
    return pltpu.make_async_remote_copy(src_ref=src,dst_ref=dst,send_sem=a,recv_sem=b,device_id=dev,device_id_type=MESH)
class Gather:
    def __init__(self,pc,src,dst,rows,order,sems):
        self.pc,self.src,self.dst,self.rows,self.order,self.sems=pc,src,dst,rows,order,sems
        self.full=set(); self.pend=[]; self.core=[]
    def at(self,ref,over,full):
        pc=self.pc; ix={}
        for d in 'yzx':
            if d in over: ix[d]=over[d]
            elif d in full: ix[d]=slice(None)
            else: ix[d]=pl.ds(getattr(pc,d),1)
        i=(ix['y'],pl.ds(pc.c,1),ix['z'],ix['x'])
        if self.rows is not None: i=i+(pl.ds(*self.rows),)
        return ref.at[i]
    def to_core(self,over,full):
        sl=self.at(self.dst,over,full)
        k=rcopy(sl,sl,self.sems,self.pc.peer('c')); k.start(); self.core.append(k)
    def phase(self,p):
        if p>0: self.finish()
        if p==0: self.to_core({},self.full)
        d=self.order[p];
        for j in ((1,2,3) if d=='z' else (1,)):
            sl=self.at(self.dst,{},self.full)
            k=rcopy(sl,sl,self.sems,self.pc.peer(d,j)); k.start()
            self.pend.append((k,{d:pl.ds(getattr(self.pc,d)^j,1)},set(self.full)))
        self.full.add(d)
    def finish(self):
        for k,over,full in self.pend:
            k.wait_recv(); self.to_core(over,full)
        self.done=getattr(self,'done',[])+[k for k,_,_ in self.pend]
        self.pend=[]
    def drain(self):
        for k in self.core: k.wait_recv()
        for k in self.core+self.done: k.wait_send()
def local(src,dst,sem):
    k=pltpu.make_async_copy(src,dst,sem); k.start(); return k
def exchange(pc,src,dst,sems):
    out=[]
    for j in (2,3,1):
        p=(pc.dp,pc.t^j)
        k=rcopy(src.at[pc.t^j],dst.at[pc.t],sems,p); k.start(); out.append(k)
    return out
N_AG=6*11+11+6
ORD=(('z','y','x'),('z','x','y'))
def ag_kernel(s_ref,h_ref,c_ref,b_ref,g_ref,xo_ref,co_ref,bo_ref,ss,rs,ls):
    pc=Place(); sems=Sems(ss,rs)
    own=(pc.y,pc.c,pc.z,pc.x)
    loc=[local(s_ref.at[g],g_ref.at[g].at[own],ls.at[g]) for g in range(3)]
    loc+=[local(b_ref,bo_ref.at[own],ls.at[3]),local(h_ref.at[pc.t],xo_ref.at[pc.t],ls.at[4]),local(c_ref.at[pc.t],co_ref.at[pc.t],ls.at[5])]
    barrier(pc.peers_all())
    hx=exchange(pc,h_ref,xo_ref,sems)
    for k in loc: k.wait()
    gs=[Gather(pc,None,bo_ref,None,ORD[0],sems)]
    gs+=[Gather(pc,None,g_ref.at[g],(48*i,48),ORD[i],sems) for g in range(3) for i in range(2)]
    for p in range(3):
        for k in gs: k.phase(p)
    cx=exchange(pc,c_ref,co_ref,sems)
    for k in gs: k.finish()
    for k in gs: k.drain()
    for k in hx+cx: k.wait()
HBM=pl.BlockSpec(memory_space=pltpu.HBM); VM=pl.BlockSpec(memory_space=pltpu.VMEM)
def gather_all(s,h,c,b):
    return pl.pallas_call(ag_kernel,out_shape=[jax.ShapeDtypeStruct((3,2,2,4,2)+s.shape[1:],bf16),jax.ShapeDtypeStruct(h.shape,bf16),jax.ShapeDtypeStruct(c.shape,bf16),jax.ShapeDtypeStruct((2,2,4,2)+b.shape,f32)],
      in_specs=[HBM]*4,out_specs=[HBM]*4,scratch_shapes=[pltpu.SemaphoreType.DMA((N_AG,)),pltpu.SemaphoreType.DMA((N_AG,)),pltpu.SemaphoreType.DMA((6,))],
      compiler_params=pltpu.CompilerParams(collective_id=0,has_side_effects=True))(s,h,c,b)
def point(steps, k, h):
    for kk in range(4):
        todo = steps.get((kk, h))
        if todo:
            @pl.when(k == kk)
            def _(todo=todo):
                for step in todo:
                    step()


def add_into(dst, src, n, pick_dst, pick_src):
    def body(j, _):
        a, b = pick_dst(j), pick_src(j)
        dst[a] = (dst[a].astype(f32) + src[b].astype(f32)).astype(bf16)
        return 0
    lax.fori_loop(0, n, body, 0)


class Reduce:
    def __init__(self, pc, d_ref, half, lc, rc, r1, r2, r3, sems, lsem):
        self.pc, self.lc, self.rc, self.r1, self.r2, self.r3 = pc, lc, rc, r1, r2, r3
        rows = pl.ds(48 * half, 48)
        self.own = pltpu.make_async_copy(d_ref.at[:, pc.c, :, :, rows], lc, lsem)
        self.q0 = rcopy(d_ref.at[:, 1 - pc.c, :, :, rows], rc, sems, pc.peer("c"))
        self.q1 = rcopy(lc.at[:, :, 1 - pc.x], r1, sems, pc.peer("x"))
        self.q2 = [rcopy(lc.at[:, pc.z ^ j, pc.x], r2.at[j - 1], sems, pc.peer("z", j)) for j in (3, 2, 1)]
        self.q3 = rcopy(lc.at[1 - pc.y, pc.z, pc.x], r3, sems, pc.peer("y"))

    def s0(self):
        self.own.start()
        self.q0.start()

    def s1(self):
        self.own.wait()
        self.q0.wait_recv()
        at = lambda j: (j // 8, (j // 2) % 4, j % 2)
        add_into(self.lc, self.rc, 16, at, at)
        self.q1.start()

    def s2(self):
        self.q1.wait_recv()
        add_into(self.lc, self.r1, 8, lambda j: (j // 4, j % 4, self.pc.x), lambda j: (j // 4, j % 4))
        for q in self.q2:
            q.start()

    def s3(self):
        pc = self.pc
        for q in self.q2:
            q.wait_recv()
        for y in range(2):
            at = (y, pc.z, pc.x)
            total = (self.lc[at].astype(f32) + self.r2[0, y].astype(f32)) + (self.r2[1, y].astype(f32) + self.r2[2, y].astype(f32))
            self.lc[at] = total.astype(bf16)
        self.q3.start()

    def s4(self, out_ref, rows):
        pc = self.pc
        self.q3.wait_recv()
        out_ref[rows] = self.lc[pc.y, pc.z, pc.x].astype(f32) + self.r3[...].astype(f32)

    def end(self):
        for q in [self.q0, self.q1, self.q3] + self.q2:
            q.wait_send()


N_C = 4 * 6 + 1 + 1 + 1 + 2 + 6 + 6 + 6


def back_kernel(
    prefix_ref, x_ref, g_ref, gf_ref, w_ref, proj_ref, projT_ref, ot_ref, lse_ref, dout_ref, d_ref, v_ref, out_ref,
    gs_ref, vs_ref, oo_ref, xo_ref,
    xT, gl, dxa, w_b, proj_b, projT_b, ot_b, lse_b, dout_b,
    zq, zdo, qm, dom, pt, ds, mask_ref, gt, dqt, dkb, dvb, gproj,
    lc, rc, r1, r2, r3, dwb, cr, yr, xr, zr, vb, vr, xst, ss, rs, ls, ins,
):
    pc = Place()
    sems = Sems(ss, rs)
    w1 = w_ref.at[0]
    lane = lax.broadcasted_iota(jnp.int32, (1, 256), 1)

    def loads(k, slot):
        t = pc.t ^ (3 - k)
        pairs = [
            (w1.at[t // 2, t % 2], w_b), (proj_ref.at[t], proj_b), (projT_ref.at[t], projT_b),
            (ot_ref.at[t], ot_b), (lse_ref.at[t], lse_b), (dout_ref.at[t], dout_b),
        ]
        return [pltpu.make_async_copy(a, b.at[slot], ins.at[slot, n]) for n, (a, b) in enumerate(pairs)]

    first = loads(0, 0)
    for q in first:
        q.start()
    l_x = local(x_ref, xst, ls.at[4])
    l_g = local(g_ref, gl, ls.at[5])
    l_f = local(gf_ref, dxa, ls.at[6])
    barrier(pc.peers_all())
    red = {}
    for n, (g, i) in enumerate(((1, 0), (1, 1), (0, 0), (0, 1))):
        red[n] = Reduce(pc, d_ref.at[g], i, lc.at[n], rc.at[n], r1.at[n], r2.at[n], r3.at[n], sems, ls.at[n])
        red[n].s0()
    ox = exchange(pc, out_ref, oo_ref, sems)
    l_o = [local(out_ref.at[pc.t], oo_ref.at[pc.t], ls.at[7])]
    q_c0 = rcopy(dwb.at[0], cr.at[0], sems, pc.peer("c"))
    q_y = rcopy(dwb.at[1], yr, sems, pc.peer("y"))
    q_c1 = rcopy(dwb.at[2], cr.at[1], sems, pc.peer("c"))
    half = [pl.ds(48 * i, 48) for i in range(2)]
    q_x = [rcopy(dwb.at[3, :, 1 - pc.x, half[i]], xr.at[i], sems, pc.peer("x")) for i in range(2)]
    q_z = [[rcopy(dwb.at[3, pc.z ^ j, pc.x, half[i]], zr.at[i, j - 1], sems, pc.peer("z", j)) for j in (3, 2, 1)] for i in range(2)]
    steps = {
        (0, 1): [red[0].s1], (0, 2): [red[1].s1], (0, 3): [red[2].s1], (1, 1): [red[3].s1],
        (1, 3): [red[0].s2], (2, 3): [red[1].s2], (3, 0): [red[0].s3], (3, 3): [red[2].s2],
    }
    masks(mask_ref, prefix_ref[0])
    zq[...] = jnp.zeros_like(zq)
    zdo[...] = jnp.zeros_like(zdo)
    gproj[:, 576:640] = jnp.zeros((L, 64), bf16)
    vb[0] = v_ref[...]
    l_x.wait()
    xT[...] = xst[...].reshape(L, 768).T
    l_g.wait()
    l_f.wait()

    def group(k, _):
        slot = k % 2
        for q in loads(k, slot):
            q.wait()

        @pl.when(k < 3)
        def _():
            for q in loads(k + 1, 1 - slot):
                q.start()

        t = pc.t ^ (3 - k)
        w, pj, pjT, o_t, lse = w_b.at[slot], proj_b.at[slot], projT_b.at[slot], ot_b.at[slot], lse_b.at[slot]
        gh = dotf(gl[...], w[...].reshape(768, 768)[:, 512:768]).astype(bf16)
        gt[...] = gh.T
        for h in range(3):
            point(steps, k, h)
            own = slice(64 + 64 * h, 128 + 64 * h)
            zq[h, own, :] = pjT[64 * h : 64 * h + 64, :]
            zdo[h, 64 * h : 64 * h + 64, :] = gt[own, :] * 0.125
            qm[...] = jnp.where((lane >= 64 * h) & (lane < 64 * h + 64), pj[:, 0:256], 0)
            dom[...] = jnp.where((lane >= 64 * h + 64) & (lane < 64 * h + 128), gh, 0)
            d = jnp.sum(gt[own, :].astype(f32) * o_t[own, :].astype(f32), axis=0, keepdims=True) * 0.125
            for qb in range(4):
                nk = NK[qb]
                qs = slice(qb * QB, qb * QB + QB)
                st = masked(dotf(pj[:nk, 128:384], zq[h, :, qs]), qb, mask_ref)
                p = jnp.exp2(st * C2 - lse[h : h + 1, qs])
                dp = dotf(pj[:nk, 384:640], zdo[h, :, qs])
                dsv = (p * (dp - d[:, qs])).astype(bf16)
                pt[:nk, qs] = p.astype(bf16)
                ds[:nk, qs] = dsv
                dqt[64 * h : 64 * h + 64, qs] = dotf(pjT[192 + 64 * h : 256 + 64 * h, :nk], dsv).astype(bf16)
            for k0, k1, q0 in ((0, 512, 0), (512, 768, 512), (768, 1024, 768)):
                dk = dotf(ds[k0:k1, q0:], qm[q0:, :]).astype(bf16)
                dv = dotf(pt[k0:k1, q0:], dom[q0:, :]).astype(bf16)
                dkb[k0:k1] = dk if h == 0 else dkb[k0:k1] + dk
                dvb[k0:k1] = dv if h == 0 else dvb[k0:k1] + dv
        point(steps, k, 3)
        gproj[:, 0:192] = dqt[...].T
        gproj[:, 192:384] = dkb[:, 0:192]
        gproj[:, 384:576] = dvb[:, 64:256]
        vb[0, pl.ds(16 + 2 * t, 1), 0:256] = jnp.sum(gproj[:, 0:256].astype(f32), axis=0, keepdims=True)
        vb[0, pl.ds(17 + 2 * t, 1), 0:256] = jnp.sum(gproj[:, 384:640].astype(f32), axis=0, keepdims=True)
        dw = dotf(xT[...], gproj[...])
        do = dout_b[slot].astype(f32)
        shape = lambda a: a.astype(bf16).reshape(4, 2, 96, a.shape[1])
        dwb[k, :, :, :, 0:512] = shape(dw[:, 0:512])
        dwb[k, :, :, :, 512:640] = shape(dw[:, 512:640] + do[:, 0:128])
        dwb[k, :, :, :, 640:768] = shape(do[:, 128:256])

        @pl.when(k == 0)
        def _():
            q_c0.start()

        @pl.when(k == 1)
        def _():
            q_c0.wait_recv()
            add_into(dwb.at[1], cr.at[0], 8, lambda j: (j // 2, j % 2), lambda j: (j // 2, j % 2))
            q_y.start()

        @pl.when(k == 2)
        def _():
            q_c1.start()

        @pl.when(k == 3)
        def _():
            q_c1.wait_recv()
            add_into(dwb.at[3], cr.at[1], 8, lambda j: (j // 2, j % 2), lambda j: (j // 2, j % 2))
            q_y.wait_recv()
            add_into(dwb.at[3], yr, 8, lambda j: (j // 2, j % 2), lambda j: (j // 2, j % 2))
            for q in q_x:
                q.start()

        dxa[...] += dot_nt(gproj[...], w[...].reshape(768, 768)[:, 0:640])
        return 0

    lax.fori_loop(0, 4, group, 0)
    xst[...] = dxa[...].astype(bf16).reshape(4, 256, 768)
    v_q = [rcopy(vb.at[0], vr.at[0], sems, pc.peer("c"))]
    v_q[0].start()
    xx = exchange(pc, xst, xo_ref, sems)
    l_o.append(local(xst.at[pc.t], xo_ref.at[pc.t], ls.at[8]))

    def vstep(n, dim):
        v_q[n].wait_recv()
        vb[n + 1] = vb[n] + vr[n]
        v_q.append(rcopy(vb.at[n + 1], vr.at[n + 1], sems, pc.peer(dim)))
        v_q[n + 1].start()

    vstep(0, "x")
    red[1].s3()
    for i in range(2):
        q_x[i].wait_recv()
        for z in range(4):
            dwb[3, z, pc.x, half[i]] = (dwb[3, z, pc.x, half[i]].astype(f32) + xr[i, z].astype(f32)).astype(bf16)
        for q in q_z[i]:
            q.start()
    vstep(1, "y")
    red[3].s2()
    red[2].s3()
    v_q[2].wait_recv()
    vb[3] = vb[2] + vr[2]
    v_z = [rcopy(vb.at[3], vr.at[2 + j], sems, pc.peer("z", j)) for j in (3, 2, 1)]
    for q in v_z:
        q.start()
    red[0].s4(gs_ref.at[2], slice(0, 48))
    red[1].s4(gs_ref.at[2], slice(48, 96))
    red[3].s3()
    for i in range(2):
        for q in q_z[i]:
            q.wait_recv()
        gs_ref[0, 48 * i : 48 * i + 48] = (dwb[3, pc.z, pc.x, half[i]].astype(f32) + zr[i, 0].astype(f32)) + (zr[i, 1].astype(f32) + zr[i, 2].astype(f32))
    red[2].s4(gs_ref.at[1], slice(0, 48))
    for q in v_z:
        q.wait_recv()
    vs_ref[...] = (vb[3] + vr[3]) + (vr[4] + vr[5])
    red[3].s4(gs_ref.at[1], slice(48, 96))
    for q in l_o:
        q.wait()
    for q in ox + xx:
        q.wait()
    for n in range(4):
        red[n].end()
    for q in [q_c0, q_y, q_c1] + q_x + q_z[0] + q_z[1] + v_q + v_z:
        q.wait_send()


def back(prefix, x, g1low, g1, g, proj, projT, ot, lse, doutw, d, v, out4):
    v_ = pltpu.VMEM
    dma = pltpu.SemaphoreType.DMA
    sd = jax.ShapeDtypeStruct
    return pl.pallas_call(
        back_kernel,
        out_shape=[sd((3, 96, 768), f32), sd((24, 768), f32), sd((4, 256, 768), bf16), sd((4, 256, 768), bf16)],
        in_specs=[pl.BlockSpec(memory_space=pltpu.SMEM)] + [HBM] * 10 + [VM, HBM],
        out_specs=[VM, VM, HBM, HBM],
        scratch_shapes=[
            v_((768, L), bf16), v_((L, 768), bf16), v_((L, 768), f32),
            v_((2, 4, 2, 96, 768), bf16), v_((2, L, 640), bf16), v_((2, 640, L), bf16), v_((2, 256, L), bf16), v_((2, 8, L), f32), v_((2, 768, 256), bf16),
            v_((3, 256, L), bf16), v_((3, 256, L), bf16), v_((L, 256), bf16), v_((L, 256), bf16), v_((L, L), bf16), v_((L, L), bf16),
            v_((4, 256, 256), f32), v_((256, L), bf16), v_((192, L), bf16), v_((L, 256), bf16), v_((L, 256), bf16), v_((L, 640), bf16),
            v_((4, 2, 4, 2, 48, 768), bf16), v_((4, 2, 4, 2, 48, 768), bf16), v_((4, 2, 4, 48, 768), bf16), v_((4, 3, 2, 48, 768), bf16), v_((4, 48, 768), bf16),
            v_((4, 4, 2, 96, 768), bf16), v_((2, 4, 2, 96, 768), bf16), v_((4, 2, 96, 768), bf16), v_((2, 4, 48, 768), bf16), v_((2, 3, 48, 768), bf16),
            v_((4, 24, 768), f32), v_((6, 24, 768), f32), v_((4, 256, 768), bf16),
            dma((N_C,)), dma((N_C,)), dma((9,)), dma((2, 6)),
        ],
        compiler_params=pltpu.CompilerParams(collective_id=1, has_side_effects=True, vmem_limit_bytes=67043328),
    )(prefix, x, g1low, g1, g, proj, projT, ot, lse, doutw, d, v, out4)


EPSILON = 1e-12


def norm_stats(r):
    center = r - jnp.mean(r, axis=-1, keepdims=True)
    inv = lax.rsqrt(jnp.mean(center * center, axis=-1, keepdims=True) + EPSILON)
    return center * inv, inv


def norm_back(cot, gain, xhat, inv):
    e = cot * gain
    grad = (e - jnp.mean(e, -1, keepdims=True) - xhat * jnp.mean(e * xhat, -1, keepdims=True)) * inv
    return grad, jnp.sum(cot * xhat, 0), jnp.sum(cot, 0)


def middle(x, cot, heads, w1, w2, w3, bias_o, bias_h, bias_d, shift1, shift2, gain1, gain2):
    ein = functools.partial(jnp.einsum, preferred_element_type=f32)
    hid = x.astype(f32)
    resid1 = hid + ein("tpw,tdw->pd", heads, w1[:, :, 512:]) + bias_o
    xhat1, inv1 = norm_stats(resid1)
    normed = xhat1 * gain1 + shift1
    low = normed.astype(bf16)
    pre = ein("pd,tdf->tpf", low, w2) + bias_h[:, None, :]
    act, gelu_back = jax.vjp(lambda v: jax.nn.gelu(v, approximate=False), pre)
    act = act.astype(bf16)
    resid2 = normed + ein("tpf,tdf->pd", act, w3) + bias_d
    xhat2, inv2 = norm_stats(resid2)
    out = (xhat2 * gain2 + shift2).astype(bf16)
    g2, dgain2, dshift2 = norm_back(cot.astype(f32), gain2, xhat2, inv2)
    g2low = g2.astype(bf16)
    d3 = ein("pd,tpf->tdf", g2low, act).astype(bf16)
    gpre = gelu_back(ein("pd,tdf->tpf", g2low, w3))[0].astype(bf16)
    d2 = ein("pd,tpf->tdf", low, gpre).astype(bf16)
    gn = g2 + ein("tpf,tdf->pd", gpre, w2)
    g1, dgain1, dshift1 = norm_back(gn, gain1, xhat1, inv1)
    g1low = g1.astype(bf16)
    dout = ein("pd,tpw->tdw", g1low, heads).astype(bf16)
    dbh = jnp.sum(gpre, 1, dtype=f32)
    return out, g1, g1low, dout, d2, d3, (dgain1, dgain2, dshift1, dshift2, jnp.sum(g1, 0), dbh, jnp.sum(g2, 0))


def on_device(hidden_in, cotangent, prefix, w_qkv, w_out, w_in, w_down, biases, gains):
    rows = w_qkv.shape[0]
    n_t = lax.axis_size("tensor")
    t_me, d_me = lax.axis_index("tensor"), lax.axis_index("dp")
    n_dev = n_t * lax.axis_size("dp")
    s = jnp.stack([jnp.concatenate([w_qkv.reshape(rows, -1), w_out.T], axis=1), w_in, w_down.T])
    vecs = jnp.concatenate([biases, gains], 0)
    width = vecs.shape[1]
    vecs = jnp.pad(vecs, ((0, 4), (0, 128 - width)))
    seqs = lambda a: jnp.transpose(a, (1, 0, 2))
    h, c = seqs(hidden_in), seqs(cotangent)
    if lax.axis_size("dp") == 8:
        g, xs, cs, b = gather_all(s, h, c, vecs)
        b = b.transpose(2, 3, 0, 1, 4, 5)
    else:
        g = lax.all_gather(lax.all_gather(s, "dp", axis=1, tiled=True), "tensor", axis=1)
        xs = lax.all_to_all(h, "tensor", 0, 0, tiled=True)
        cs = lax.all_to_all(c, "tensor", 0, 0, tiled=True)
        b = lax.all_gather(vecs, ("dp", "tensor"), axis=0)
    w1, w2, w3 = [a.reshape(n_t, 768, 768) for a in g]
    vec = b.reshape(n_dev, 16, 128)[:, :12, :width].transpose(1, 0, 2).reshape(12, 768)
    x = xs.reshape(1024, 768)
    bqkv = jnp.pad(jnp.stack([vec[0].reshape(4, 192), jnp.zeros((4, 192), f32), vec[1].reshape(4, 192)], 1).reshape(4, 1, 576), ((0, 0), (0, 0), (0, 64)))
    my_prefix = lax.dynamic_slice_in_dim(prefix, t_me, 1, 0)
    proj, projT, heads, ot, lse = attn_fwd(my_prefix, x, w1, bqkv)
    out, g1, g1low, doutw, d2, d3, small = middle(
        x, cs.reshape(1024, 768), heads, w1, w2, w3, vec[2], vec[3:7].reshape(4, 768), vec[7], vec[8], vec[9], vec[10], vec[11]
    )
    ein = functools.partial(jnp.einsum, preferred_element_type=f32)
    dgain1, dgain2, dshift1, dshift2, dbo, dbh, dbd = small
    o4 = out.reshape(4, 256, 768)
    none = jnp.zeros((1, 768), f32)
    v = [none, none, dbo[None], dbh, jnp.stack([dbd, dshift1, dshift2, dgain1, dgain2]), jnp.zeros((4, 768), f32)]
    if lax.axis_size("dp") == 8:
        gs, vs, oo, xx = back(
            my_prefix, xs, g1low, g1, g, proj, projT, ot, lse, doutw, jnp.stack([d2, d3]).reshape(2, 2, 2, 4, 2, rows, 768),
            jnp.concatenate(v + [jnp.zeros((8, 768), f32)]), o4,
        )
        qv = vs[16:24, :256].reshape(4, 2, 256)
        vs = jnp.concatenate([qv[:, 0, :192].reshape(1, 768), qv[:, 1, :192].reshape(1, 768), vs[2:16]])
    else:
        gproj = attn_bwd(my_prefix, g1low, w1, proj, projT, ot, lse)
        gp = gproj[:, :, :576]
        dqkv = ein("pd,tpc->tdc", x, gp).astype(bf16)
        x4 = (g1 + ein("tpc,tdc->pd", gp, w1[:, :, :576])).astype(bf16).reshape(4, 256, 768)
        v[0] = jnp.sum(gp[:, :, :192], 1, dtype=f32).reshape(1, 768)
        v[1] = jnp.sum(gp[:, :, 384:], 1, dtype=f32).reshape(1, 768)
        d = jnp.stack([jnp.concatenate([dqkv, doutw[:, :, 64:]], 2), d2, d3])
        part = lax.all_to_all(d, "tensor", 1, 1, tiled=True).astype(f32).sum(1)
        part = part.astype(bf16).reshape(3, -1, rows, 768)
        gs = lax.all_to_all(part, "dp", 1, 1, tiled=True).astype(f32).sum(1)
        vs = lax.psum(jnp.concatenate(v), ("dp", "tensor"))
        oo = lax.all_to_all(o4, "tensor", 0, 0, tiled=True)
        xx = lax.all_to_all(x4, "tensor", 0, 0, tiled=True)
    mine = lax.dynamic_slice_in_dim(vs, (d_me * n_t + t_me) * width, width, 1)
    return (
        seqs(oo),
        seqs(xx),
        gs[0, :, :576].reshape(rows, 3, 192),
        gs[0, :, 576:].T,
        gs[1],
        gs[2].T,
        mine[:10],
        mine[10:12],
    )


def solution(mesh):
    placed = (
        P("tensor", "dp", None),
        P("tensor", "dp", None),
        P("dp"),
        P("dp", None, "tensor"),
        P("tensor", "dp"),
        P("dp", "tensor"),
        P("tensor", "dp"),
        P(None, ("dp", "tensor")),
        P(None, ("dp", "tensor")),
    )
    return jax.shard_map(on_device, mesh=mesh, in_specs=placed, out_specs=placed[:2] + placed[3:], check_vma=False)
```

```python
import functools
import math

import jax
import jax.numpy as jnp
from jax import lax
from jax.experimental import pallas as pl
from jax.experimental.pallas import tpu as pltpu
from jax.sharding import PartitionSpec as P

f32=jnp.float32; bf16=jnp.bfloat16
L=1024; QB=256; NK=(512,512,768,1024)
C2=0.125*math.log2(math.e)
NEG=-1e30
def dotf(a,b): return jnp.dot(a,b,preferred_element_type=f32)
def dot_nt(a,b): return lax.dot_general(a,b,(((1,),(1,)),((),())),preferred_element_type=f32)
def masks(mask_ref, prefix):
    k=lax.broadcasted_iota(jnp.int32,(256,256),0); q=lax.broadcasted_iota(jnp.int32,(256,256),1)
    diag=k<=q
    mask_ref[0]=jnp.where(diag|(k<prefix),0.0,NEG)
    mask_ref[1]=jnp.where(k+256<prefix,0.0,NEG)+jnp.zeros((256,256),f32)
    mask_ref[2]=jnp.where(diag|(k+256<prefix),0.0,NEG)
    mask_ref[3]=jnp.where(diag,0.0,NEG)
MASKMAP={0:{0:0,1:1},1:{1:2},2:{2:3},3:{3:3}}
def masked(st,qb,mask_ref):
    parts=[]
    for kb in range(NK[qb]//256):
        p=st[kb*256:(kb+1)*256]
        mi=MASKMAP[qb].get(kb)
        parts.append(p if mi is None else p+mask_ref[mi])
    return jnp.concatenate(parts,0)
def fwd_kernel(prefix_ref,x_ref,w_ref,b_ref,proj_ref,projT_ref,heads_ref,ot_ref,lse_ref,zq_ref,mask_ref):
    masks(mask_ref,prefix_ref[0])
    proj=(dotf(x_ref[...],w_ref[:,:640])+b_ref[...]).astype(bf16)
    proj_ref[...]=proj
    projT_ref[...]=proj.T
    zq_ref[...]=jnp.zeros_like(zq_ref)
    for h in range(3):
        zq_ref[h,64+64*h:128+64*h,:]=projT_ref[64*h:64*h+64,:]
    ot_ref[...]=jnp.zeros_like(ot_ref)
    for h in range(3):
        for qb in range(4):
            nk=NK[qb]; qs=slice(qb*QB,qb*QB+QB)
            st=dotf(proj_ref[:nk,128:384],zq_ref[h,:,qs])
            st=masked(st,qb,mask_ref)
            m=jnp.max(st,axis=0,keepdims=True)
            p=jnp.exp2((st-m)*C2)
            l=jnp.sum(p,axis=0,keepdims=True)
            ot=dotf(projT_ref[384+64*h:448+64*h,:nk],p.astype(bf16))
            ot_ref[64+64*h:128+64*h,qs]=(ot/l).astype(bf16)
            lse_ref[h:h+1,qs]=m*C2+jnp.log2(l)
    heads_ref[...]=ot_ref[...].T
def attn_fwd(prefix,x,w1,bqkv):
    sq=pl.squeezed
    return pl.pallas_call(fwd_kernel,grid_spec=pltpu.PrefetchScalarGridSpec(num_scalar_prefetch=1,grid=(4,),
      in_specs=[pl.BlockSpec((L,768),lambda t,p:(0,0)),pl.BlockSpec((sq,768,768),lambda t,p:(t,0,0)),pl.BlockSpec((sq,1,640),lambda t,p:(t,0,0))],
      out_specs=[pl.BlockSpec((sq,L,640),lambda t,p:(t,0,0)),pl.BlockSpec((sq,640,L),lambda t,p:(t,0,0)),pl.BlockSpec((sq,L,256),lambda t,p:(t,0,0)),pl.BlockSpec((sq,256,L),lambda t,p:(t,0,0)),pl.BlockSpec((sq,8,L),lambda t,p:(t,0,0))],
      scratch_shapes=[pltpu.VMEM((3,256,L),bf16),pltpu.VMEM((4,256,256),f32)]),
      out_shape=[jax.ShapeDtypeStruct((4,L,640),bf16),jax.ShapeDtypeStruct((4,640,L),bf16),jax.ShapeDtypeStruct((4,L,256),bf16),jax.ShapeDtypeStruct((4,256,L),bf16),jax.ShapeDtypeStruct((4,8,L),f32)],
      compiler_params=pltpu.CompilerParams(vmem_limit_bytes=62<<20))(prefix,x,w1,bqkv)
def bwd_kernel(prefix_ref,g_ref,w_ref,proj_ref,projT_ref,ot_ref,lse_ref,gproj_ref,
               zq_ref,zdo_ref,qm_ref,dom_ref,pt_ref,ds_ref,mask_ref,gt_ref,dqt_ref):
    masks(mask_ref,prefix_ref[0])
    gh=dotf(g_ref[...],w_ref[:,512:768]).astype(bf16)
    gt_ref[...]=gh.T
    zq_ref[...]=jnp.zeros_like(zq_ref); zdo_ref[...]=jnp.zeros_like(zdo_ref)
    lane=lax.broadcasted_iota(jnp.int32,(1,256),1)
    for h in range(3):
        zq_ref[h,64+64*h:128+64*h,:]=projT_ref[64*h:64*h+64,:]
        zdo_ref[h,64*h:64*h+64,:]=gt_ref[64+64*h:128+64*h,:]*0.125
        sel=(lane>=64*h)&(lane<64*h+64)
        qm_ref[h]=jnp.where(sel,proj_ref[:,0:256],0)
        sel2=(lane>=64*h+64)&(lane<64*h+128)
        dom_ref[h]=jnp.where(sel2,gh,0)
    for h in range(3):
        d=jnp.sum(gt_ref[64+64*h:128+64*h,:].astype(f32)*ot_ref[64+64*h:128+64*h,:].astype(f32),axis=0,keepdims=True)*0.125
        for qb in range(4):
            nk=NK[qb]; qs=slice(qb*QB,qb*QB+QB)
            st=dotf(proj_ref[:nk,128:384],zq_ref[h,:,qs])
            st=masked(st,qb,mask_ref)
            p=jnp.exp2(st*C2-lse_ref[h:h+1,qs])
            dp=dotf(proj_ref[:nk,384:640],zdo_ref[h,:,qs])
            ds=(p*(dp-d[:,qs])).astype(bf16)
            pt_ref[h,:nk,qs]=p.astype(bf16)
            ds_ref[h,:nk,qs]=ds
            dqt_ref[64*h:64*h+64,qs]=dotf(projT_ref[192+64*h:256+64*h,:nk],ds).astype(bf16)
    gproj_ref[:,0:192]=dqt_ref[...].T
    for (k0,k1,q0) in ((0,512,0),(512,768,512),(768,1024,768)):
        dk=jnp.zeros((k1-k0,256),f32); dv=jnp.zeros((k1-k0,256),f32)
        for h in range(3):
            dk=dk+dotf(ds_ref[h,k0:k1,q0:],qm_ref[h,q0:,:])
            dv=dv+dotf(pt_ref[h,k0:k1,q0:],dom_ref[h,q0:,:])
        gproj_ref[k0:k1,192:384]=dk[:,0:192].astype(bf16)
        gproj_ref[k0:k1,384:576]=dv[:,64:256].astype(bf16)
    gproj_ref[:,576:640]=jnp.zeros((L,64),bf16)
def attn_bwd(prefix,g,w1,proj,projT,ot,lse):
    sq=pl.squeezed
    sp=lambda *s: pl.BlockSpec((sq,)+s,lambda t,p:(t,0,0))
    return pl.pallas_call(functools.partial(bwd_kernel),grid_spec=pltpu.PrefetchScalarGridSpec(num_scalar_prefetch=1,grid=(4,),
      in_specs=[pl.BlockSpec((L,768),lambda t,p:(0,0)),sp(768,768),sp(L,640),sp(640,L),sp(256,L),sp(8,L)],
      out_specs=sp(L,640),
      scratch_shapes=[pltpu.VMEM((3,256,L),bf16),pltpu.VMEM((3,256,L),bf16),pltpu.VMEM((3,L,256),bf16),pltpu.VMEM((3,L,256),bf16),pltpu.VMEM((3,L,L),bf16),pltpu.VMEM((3,L,L),bf16),pltpu.VMEM((4,256,256),f32),pltpu.VMEM((256,L),bf16),pltpu.VMEM((192,L),bf16)]),
      out_shape=jax.ShapeDtypeStruct((4,L,640),bf16),
      compiler_params=pltpu.CompilerParams(vmem_limit_bytes=62<<20))(prefix,g,w1,proj,projT,ot,lse)
MESH=pl.DeviceIdType.MESH
class Place:
    def __init__(self):
        dp=lax.axis_index("dp"); t=lax.axis_index("tensor")
        self.dp,self.t=dp,t
        self.z,self.x,self.y,self.c=dp//2,dp%2,t//2,t%2
    def peer(self,dim,j=1):
        return {'x':lambda:(self.dp^1,self.t),'z':lambda:(self.dp^(2*j),self.t),'y':lambda:(self.dp,self.t^2),'c':lambda:(self.dp,self.t^1)}[dim]()
    def peers_all(self):
        return [self.peer('x'),self.peer('y'),self.peer('c'),self.peer('z',1),self.peer('z',2),self.peer('z',3),(self.dp,self.t^3)]
def barrier(peers):
    b=pltpu.get_barrier_semaphore()
    for p in peers: pl.semaphore_signal(b,inc=1,device_id=p,device_id_type=MESH)
    pl.semaphore_wait(b,len(peers))
class Sems:
    def __init__(self,send,recv): self.s,self.r,self.n=send,recv,0
    def take(self):
        i=self.n; self.n+=1
        return self.s.at[i],self.r.at[i]
def rcopy(src,dst,sems,dev):
    a,b=sems.take()
    return pltpu.make_async_remote_copy(src_ref=src,dst_ref=dst,send_sem=a,recv_sem=b,device_id=dev,device_id_type=MESH)
def local(src,dst,sem):
    k=pltpu.make_async_copy(src,dst,sem); k.start(); return k
def exchange(pc,src,dst,sems):
    out=[]
    for j in (2,3,1):
        p=(pc.dp,pc.t^j)
        k=rcopy(src.at[pc.t^j],dst.at[pc.t],sems,p); k.start(); out.append(k)
    return out
HBM=pl.BlockSpec(memory_space=pltpu.HBM); VM=pl.BlockSpec(memory_space=pltpu.VMEM)
def point(steps, k, h):
    for kk in range(4):
        todo = steps.get((kk, h))
        if todo:
            @pl.when(k == kk)
            def _(todo=todo):
                for step in todo:
                    step()


def add_into(dst, src, n, pick_dst, pick_src):
    def body(j, _):
        a, b = pick_dst(j), pick_src(j)
        dst[a] = (dst[a].astype(f32) + src[b].astype(f32)).astype(bf16)
        return 0
    lax.fori_loop(0, n, body, 0)


class Reduce:
    def __init__(self, pc, d_ref, half, lc, rc, r1, r2, r3, sems, lsem):
        self.pc, self.lc, self.rc, self.r1, self.r2, self.r3 = pc, lc, rc, r1, r2, r3
        rows = pl.ds(48 * half, 48)
        self.own = pltpu.make_async_copy(d_ref.at[:, pc.c, :, :, rows], lc, lsem)
        self.q0 = rcopy(d_ref.at[:, 1 - pc.c, :, :, rows], rc, sems, pc.peer("c"))
        self.q1 = rcopy(lc.at[:, :, 1 - pc.x], r1, sems, pc.peer("x"))
        self.q2 = [rcopy(lc.at[:, pc.z ^ j, pc.x], r2.at[j - 1], sems, pc.peer("z", j)) for j in (3, 2, 1)]
        self.q3 = rcopy(lc.at[1 - pc.y, pc.z, pc.x], r3, sems, pc.peer("y"))

    def s0(self):
        self.own.start()
        self.q0.start()

    def s1(self):
        self.own.wait()
        self.q0.wait_recv()
        at = lambda j: (j // 8, (j // 2) % 4, j % 2)
        add_into(self.lc, self.rc, 16, at, at)
        self.q1.start()

    def s2(self):
        self.q1.wait_recv()
        add_into(self.lc, self.r1, 8, lambda j: (j // 4, j % 4, self.pc.x), lambda j: (j // 4, j % 4))
        for q in self.q2:
            q.start()

    def s3(self):
        pc = self.pc
        for q in self.q2:
            q.wait_recv()
        for y in range(2):
            at = (y, pc.z, pc.x)
            total = (self.lc[at].astype(f32) + self.r2[0, y].astype(f32)) + (self.r2[1, y].astype(f32) + self.r2[2, y].astype(f32))
            self.lc[at] = total.astype(bf16)
        self.q3.start()

    def s4(self, out_ref, rows):
        pc = self.pc
        self.q3.wait_recv()
        out_ref[rows] = self.lc[pc.y, pc.z, pc.x].astype(f32) + self.r3[...].astype(f32)

    def end(self):
        for q in [self.q0, self.q1, self.q3] + self.q2:
            q.wait_send()


N_C = 4 * 6 + 1 + 1 + 1 + 2 + 6 + 6 + 6


def back_kernel(
    prefix_ref, x_ref, g_ref, gf_ref, w_ref, proj_ref, projT_ref, ot_ref, lse_ref, dout_ref, d_ref, v_ref, out_ref,
    gs_ref, vs_ref, oo_ref, xo_ref,
    xT, gl, dxa, w_b, proj_b, projT_b, ot_b, lse_b, dout_b,
    zq, zdo, qm, dom, pt, ds, mask_ref, gt, dqt, dkb, dvb, gproj,
    lc, rc, r1, r2, r3, dwb, cr, yr, xr, zr, vb, vr, xst, ss, rs, ls, ins,
):
    pc = Place()
    sems = Sems(ss, rs)
    w1 = w_ref.at[0]
    lane = lax.broadcasted_iota(jnp.int32, (1, 256), 1)

    def loads(k, slot):
        t = pc.t ^ (3 - k)
        pairs = [
            (w1.at[t // 2, t % 2], w_b), (proj_ref.at[t], proj_b), (projT_ref.at[t], projT_b),
            (ot_ref.at[t], ot_b), (lse_ref.at[t], lse_b), (dout_ref.at[t], dout_b),
        ]
        return [pltpu.make_async_copy(a, b.at[slot], ins.at[slot, n]) for n, (a, b) in enumerate(pairs)]

    first = loads(0, 0)
    for q in first:
        q.start()
    l_x = local(x_ref, xst, ls.at[4])
    l_g = local(g_ref, gl, ls.at[5])
    l_f = local(gf_ref, dxa, ls.at[6])
    barrier(pc.peers_all())
    red = {}
    for n, (g, i) in enumerate(((1, 0), (1, 1), (0, 0), (0, 1))):
        red[n] = Reduce(pc, d_ref.at[g], i, lc.at[n], rc.at[n], r1.at[n], r2.at[n], r3.at[n], sems, ls.at[n])
        red[n].s0()
    ox = exchange(pc, out_ref, oo_ref, sems)
    l_o = [local(out_ref.at[pc.t], oo_ref.at[pc.t], ls.at[7])]
    q_c0 = rcopy(dwb.at[0], cr.at[0], sems, pc.peer("c"))
    q_y = rcopy(dwb.at[1], yr, sems, pc.peer("y"))
    q_c1 = rcopy(dwb.at[2], cr.at[1], sems, pc.peer("c"))
    half = [pl.ds(48 * i, 48) for i in range(2)]
    q_x = [rcopy(dwb.at[3, :, 1 - pc.x, half[i]], xr.at[i], sems, pc.peer("x")) for i in range(2)]
    q_z = [[rcopy(dwb.at[3, pc.z ^ j, pc.x, half[i]], zr.at[i, j - 1], sems, pc.peer("z", j)) for j in (3, 2, 1)] for i in range(2)]
    steps = {
        (0, 1): [red[0].s1], (0, 2): [red[1].s1], (0, 3): [red[2].s1], (1, 1): [red[3].s1],
        (1, 3): [red[0].s2], (2, 3): [red[1].s2], (3, 0): [red[0].s3], (3, 3): [red[2].s2],
    }
    masks(mask_ref, prefix_ref[0])
    zq[...] = jnp.zeros_like(zq)
    zdo[...] = jnp.zeros_like(zdo)
    gproj[:, 576:640] = jnp.zeros((L, 64), bf16)
    vb[0] = v_ref[...]
    l_x.wait()
    xT[...] = xst[...].reshape(L, 768).T
    l_g.wait()
    l_f.wait()

    def group(k, _):
        slot = k % 2
        for q in loads(k, slot):
            q.wait()

        @pl.when(k < 3)
        def _():
            for q in loads(k + 1, 1 - slot):
                q.start()

        t = pc.t ^ (3 - k)
        w, pj, pjT, o_t, lse = w_b.at[slot], proj_b.at[slot], projT_b.at[slot], ot_b.at[slot], lse_b.at[slot]
        gh = dotf(gl[...], w[...].reshape(768, 768)[:, 512:768]).astype(bf16)
        gt[...] = gh.T
        for h in range(3):
            point(steps, k, h)
            own = slice(64 + 64 * h, 128 + 64 * h)
            zq[h, own, :] = pjT[64 * h : 64 * h + 64, :]
            zdo[h, 64 * h : 64 * h + 64, :] = gt[own, :] * 0.125
            qm[...] = jnp.where((lane >= 64 * h) & (lane < 64 * h + 64), pj[:, 0:256], 0)
            dom[...] = jnp.where((lane >= 64 * h + 64) & (lane < 64 * h + 128), gh, 0)
            d = jnp.sum(gt[own, :].astype(f32) * o_t[own, :].astype(f32), axis=0, keepdims=True) * 0.125
            for qb in range(4):
                nk = NK[qb]
                qs = slice(qb * QB, qb * QB + QB)
                st = masked(dotf(pj[:nk, 128:384], zq[h, :, qs]), qb, mask_ref)
                p = jnp.exp2(st * C2 - lse[h : h + 1, qs])
                dp = dotf(pj[:nk, 384:640], zdo[h, :, qs])
                dsv = (p * (dp - d[:, qs])).astype(bf16)
                pt[:nk, qs] = p.astype(bf16)
                ds[:nk, qs] = dsv
                dqt[64 * h : 64 * h + 64, qs] = dotf(pjT[192 + 64 * h : 256 + 64 * h, :nk], dsv).astype(bf16)
            for k0, k1, q0 in ((0, 512, 0), (512, 768, 512), (768, 1024, 768)):
                dk = dotf(ds[k0:k1, q0:], qm[q0:, :]).astype(bf16)
                dv = dotf(pt[k0:k1, q0:], dom[q0:, :]).astype(bf16)
                dkb[k0:k1] = dk if h == 0 else dkb[k0:k1] + dk
                dvb[k0:k1] = dv if h == 0 else dvb[k0:k1] + dv
        point(steps, k, 3)
        gproj[:, 0:192] = dqt[...].T
        gproj[:, 192:384] = dkb[:, 0:192]
        gproj[:, 384:576] = dvb[:, 64:256]
        vb[0, pl.ds(16 + 2 * t, 1), 0:256] = jnp.sum(gproj[:, 0:256].astype(f32), axis=0, keepdims=True)
        vb[0, pl.ds(17 + 2 * t, 1), 0:256] = jnp.sum(gproj[:, 384:640].astype(f32), axis=0, keepdims=True)
        dw = dotf(xT[...], gproj[...])
        do = dout_b[slot].astype(f32)
        shape = lambda a: a.astype(bf16).reshape(4, 2, 96, a.shape[1])
        dwb[k, :, :, :, 0:512] = shape(dw[:, 0:512])
        dwb[k, :, :, :, 512:640] = shape(dw[:, 512:640] + do[:, 0:128])
        dwb[k, :, :, :, 640:768] = shape(do[:, 128:256])

        @pl.when(k == 0)
        def _():
            q_c0.start()

        @pl.when(k == 1)
        def _():
            q_c0.wait_recv()
            add_into(dwb.at[1], cr.at[0], 8, lambda j: (j // 2, j % 2), lambda j: (j // 2, j % 2))
            q_y.start()

        @pl.when(k == 2)
        def _():
            q_c1.start()

        @pl.when(k == 3)
        def _():
            q_c1.wait_recv()
            add_into(dwb.at[3], cr.at[1], 8, lambda j: (j // 2, j % 2), lambda j: (j // 2, j % 2))
            q_y.wait_recv()
            add_into(dwb.at[3], yr, 8, lambda j: (j // 2, j % 2), lambda j: (j // 2, j % 2))
            for q in q_x:
                q.start()

        dxa[...] += dot_nt(gproj[...], w[...].reshape(768, 768)[:, 0:640])
        return 0

    lax.fori_loop(0, 4, group, 0)
    xst[...] = dxa[...].astype(bf16).reshape(4, 256, 768)
    v_q = [rcopy(vb.at[0], vr.at[0], sems, pc.peer("c"))]
    v_q[0].start()
    xx = exchange(pc, xst, xo_ref, sems)
    l_o.append(local(xst.at[pc.t], xo_ref.at[pc.t], ls.at[8]))

    def vstep(n, dim):
        v_q[n].wait_recv()
        vb[n + 1] = vb[n] + vr[n]
        v_q.append(rcopy(vb.at[n + 1], vr.at[n + 1], sems, pc.peer(dim)))
        v_q[n + 1].start()

    vstep(0, "x")
    red[1].s3()
    for i in range(2):
        q_x[i].wait_recv()
        for z in range(4):
            dwb[3, z, pc.x, half[i]] = (dwb[3, z, pc.x, half[i]].astype(f32) + xr[i, z].astype(f32)).astype(bf16)
        for q in q_z[i]:
            q.start()
    vstep(1, "y")
    red[3].s2()
    red[2].s3()
    v_q[2].wait_recv()
    vb[3] = vb[2] + vr[2]
    v_z = [rcopy(vb.at[3], vr.at[2 + j], sems, pc.peer("z", j)) for j in (3, 2, 1)]
    for q in v_z:
        q.start()
    red[0].s4(gs_ref.at[2], slice(0, 48))
    red[1].s4(gs_ref.at[2], slice(48, 96))
    red[3].s3()
    for i in range(2):
        for q in q_z[i]:
            q.wait_recv()
        gs_ref[0, 48 * i : 48 * i + 48] = (dwb[3, pc.z, pc.x, half[i]].astype(f32) + zr[i, 0].astype(f32)) + (zr[i, 1].astype(f32) + zr[i, 2].astype(f32))
    red[2].s4(gs_ref.at[1], slice(0, 48))
    for q in v_z:
        q.wait_recv()
    vs_ref[...] = (vb[3] + vr[3]) + (vr[4] + vr[5])
    red[3].s4(gs_ref.at[1], slice(48, 96))
    for q in l_o:
        q.wait()
    for q in ox + xx:
        q.wait()
    for n in range(4):
        red[n].end()
    for q in [q_c0, q_y, q_c1] + q_x + q_z[0] + q_z[1] + v_q + v_z:
        q.wait_send()


def back(prefix, x, g1low, g1, g, proj, projT, ot, lse, doutw, d, v, out4):
    v_ = pltpu.VMEM
    dma = pltpu.SemaphoreType.DMA
    sd = jax.ShapeDtypeStruct
    return pl.pallas_call(
        back_kernel,
        out_shape=[sd((3, 96, 768), f32), sd((24, 768), f32), sd((4, 256, 768), bf16), sd((4, 256, 768), bf16)],
        in_specs=[pl.BlockSpec(memory_space=pltpu.SMEM)] + [HBM] * 10 + [VM, HBM],
        out_specs=[VM, VM, HBM, HBM],
        scratch_shapes=[
            v_((768, L), bf16), v_((L, 768), bf16), v_((L, 768), f32),
            v_((2, 4, 2, 96, 768), bf16), v_((2, L, 640), bf16), v_((2, 640, L), bf16), v_((2, 256, L), bf16), v_((2, 8, L), f32), v_((2, 768, 256), bf16),
            v_((3, 256, L), bf16), v_((3, 256, L), bf16), v_((L, 256), bf16), v_((L, 256), bf16), v_((L, L), bf16), v_((L, L), bf16),
            v_((4, 256, 256), f32), v_((256, L), bf16), v_((192, L), bf16), v_((L, 256), bf16), v_((L, 256), bf16), v_((L, 640), bf16),
            v_((4, 2, 4, 2, 48, 768), bf16), v_((4, 2, 4, 2, 48, 768), bf16), v_((4, 2, 4, 48, 768), bf16), v_((4, 3, 2, 48, 768), bf16), v_((4, 48, 768), bf16),
            v_((4, 4, 2, 96, 768), bf16), v_((2, 4, 2, 96, 768), bf16), v_((4, 2, 96, 768), bf16), v_((2, 4, 48, 768), bf16), v_((2, 3, 48, 768), bf16),
            v_((4, 24, 768), f32), v_((6, 24, 768), f32), v_((4, 256, 768), bf16),
            dma((N_C,)), dma((N_C,)), dma((9,)), dma((2, 6)),
        ],
        compiler_params=pltpu.CompilerParams(collective_id=1, has_side_effects=True, vmem_limit_bytes=67043328),
    )(prefix, x, g1low, g1, g, proj, projT, ot, lse, doutw, d, v, out4)


class Gather:
    def __init__(self, pc, src, dst, rows, order, sems):
        self.pc, self.src, self.dst, self.rows, self.order, self.sems = pc, src, dst, rows, order, sems
        self.full, self.sent, self.core = set(), [], []
        self.plan()

    def at(self, over, full):
        pc = self.pc
        ix = {d: over.get(d, slice(None) if d in full else getattr(pc, d)) for d in "yzx"}
        return self.dst.at[(ix["y"], pc.c, ix["z"], ix["x"]) + ((pl.ds(*self.rows),) if self.rows else ())]

    def plan(self):
        pc = self.pc
        src = self.src.at[pl.ds(*self.rows)] if self.rows else self.src
        mine = self.at({}, set())
        self.core.append(rcopy(src, mine, self.sems, pc.peer("c")))
        self.phases = []
        full = set()
        for d in self.order:
            ks = []
            for j in (1, 2, 3) if d == "z" else (1,):
                here = self.at({}, full)
                ks.append(rcopy(here if full else src, here, self.sems, pc.peer(d, j)))
                there = self.at({d: getattr(pc, d) ^ j}, full)
                self.core.append(rcopy(there, there, self.sems, pc.peer("c")))
            self.phases.append(ks)
            full = full | {d}
        self.first = [1]
        for ks in self.phases:
            self.first.append(self.first[-1] + len(ks))

    def start(self):
        self.core[0].start()
        for k in self.phases[0]:
            k.start()

    def arrive(self, p):
        for n, k in enumerate(self.phases[p]):
            k.wait_recv()
            self.core[self.first[p] + n].start()

    def next(self, p):
        self.arrive(p - 1)
        for k in self.phases[p]:
            k.start()

    def from_core(self, a, b):
        for k in self.core[a:b]:
            k.wait_recv()

    def end(self):
        for k in self.core + sum(self.phases, []):
            k.wait_send()


N_A = 6 * 11 + 6


def front_kernel(
    prefix_ref, s_ref, h_ref, c_ref, b_ref,
    g_ref, x_ref, co_ref, bv, proj_ref, projT_ref, heads_ref, ot_ref, lse_ref,
    sv, xv, cst, wv, proj_b, projT_b, heads_b, ot_b, lse_b, zq, mask_ref, ss, rs, ls, os_,
):
    pc = Place()
    sems = Sems(ss, rs)
    own = (pc.y, pc.c, pc.z, pc.x)
    l_s = local(s_ref, sv, ls.at[0])
    l_h = local(h_ref.at[pc.t], xv.at[pc.t], ls.at[1])
    l_c = local(c_ref.at[pc.t], cst, ls.at[2])
    l_b = local(b_ref, bv.at[own], ls.at[9])
    barrier(pc.peers_all())
    bias = Gather(pc, b_ref, bv, None, "zxy", sems)
    w1 = Gather(pc, s_ref.at[0], g_ref.at[0], None, "zxy", sems)
    w2 = [Gather(pc, s_ref.at[1], g_ref.at[1], (48 * i, 48), "yzx", sems) for i in range(2)]
    w3 = [Gather(pc, s_ref.at[2], g_ref.at[2], (48 * i, 48), "yzx", sems) for i in range(2)]
    bias.start()
    w1.start()
    w2[0].start()
    w2[1].start()
    hx = exchange(pc, h_ref, xv, sems)
    w3[0].start()
    w3[1].start()
    l_s.wait()
    l_g = [local(sv.at[g], g_ref.at[g].at[own], ls.at[3 + g]) for g in range(3)]
    l_c.wait()
    l_c2 = local(cst, co_ref.at[pc.t], ls.at[6])
    masks(mask_ref, prefix_ref[0])
    zq[...] = jnp.zeros_like(zq)
    ot_b[...] = jnp.zeros_like(ot_b)
    for q in l_g:
        q.wait()
    l_b.wait()
    w1.next(1)
    bias.next(1)
    w2[0].next(1)
    w1.next(2)
    bias.next(2)
    w2[1].next(1)
    bias.arrive(2)
    bias.from_core(0, len(bias.core))
    l_h.wait()
    for q in hx:
        q.wait_recv()
    l_x = local(xv, x_ref, ls.at[7])
    c_plan = [rcopy(c_ref.at[pc.t ^ j], co_ref.at[pc.t], sems, (pc.dp, pc.t ^ j)) for j in (2, 3, 1)]

    def load(k, slot):
        t = pc.t ^ k
        return pltpu.make_async_copy(g_ref.at[0, t // 2, t % 2], wv.at[slot], ls.at[8])

    def start_cot():
        for q in c_plan:
            q.start()

    steps = {
        (0, 1): [lambda: w3[0].next(1), lambda: w3[1].next(1)],
        (0, 2): [lambda: w1.from_core(0, 5), lambda: load(1, 1).start()],
        (1, 0): [lambda: w2[0].next(2)],
        (1, 1): [start_cot],
        (1, 3): [lambda: w1.arrive(2), lambda: load(2, 0).start()],
        (2, 0): [lambda: w2[1].next(2)],
        (2, 2): [lambda: w1.from_core(5, 6), lambda: load(3, 1).start()],
        (3, 2): [lambda: w3[0].next(2)],
    }
    load(0, 0).start()

    def outs(k, slot):
        t = pc.t ^ k
        pairs = [(proj_b, proj_ref), (projT_b, projT_ref), (heads_b, heads_ref), (ot_b, ot_ref), (lse_b, lse_ref)]
        return [pltpu.make_async_copy(a.at[slot], b.at[t], os_.at[slot, n]) for n, (a, b) in enumerate(pairs)]

    def group(k, _):
        slot = k % 2
        t = pc.t ^ k
        load(k, slot).wait()

        @pl.when(k >= 2)
        def _():
            for q in outs(k - 2, slot):
                q.wait()

        row = jnp.zeros((8, 256), f32)
        for i in range(8):
            piece = bv[(i // 2) % 2, i % 2, t, i // 4, 0:8, :]
            row = row + pltpu.roll(jnp.concatenate([piece, jnp.zeros((8, 128), f32)], 1), 24 * i, 1)
        brow = jnp.concatenate([row[0:1], jnp.zeros((1, 128), f32), row[1:2]], 1)
        pj, pjT, ot, lse = proj_b.at[slot], projT_b.at[slot], ot_b.at[slot], lse_b.at[slot]
        proj = (dotf(xv[...].reshape(L, 768), wv[slot].reshape(768, 768)[:, :640]) + brow).astype(bf16)
        pj[...] = proj
        pjT[...] = proj.T
        for h in range(3):
            point(steps, k, h)
            zq[h, 64 + 64 * h : 128 + 64 * h, :] = pjT[64 * h : 64 * h + 64, :]
            for qb in range(4):
                nk = NK[qb]
                qs = slice(qb * QB, qb * QB + QB)
                st = masked(dotf(pj[:nk, 128:384], zq[h, :, qs]), qb, mask_ref)
                m = jnp.max(st, axis=0, keepdims=True)
                p = jnp.exp2((st - m) * C2)
                l = jnp.sum(p, axis=0, keepdims=True)
                o = dotf(pjT[384 + 64 * h : 448 + 64 * h, :nk], p.astype(bf16))
                ot[64 + 64 * h : 128 + 64 * h, qs] = (o / l).astype(bf16)
                lse[h : h + 1, qs] = m * C2 + jnp.log2(l)
        point(steps, k, 3)
        heads_b[slot] = ot[...].T
        for q in outs(k, slot):
            q.start()
        return 0

    lax.fori_loop(0, 4, group, 0)
    w3[1].next(2)
    for g in w2 + w3:
        g.arrive(2)
    for g in w2 + w3:
        g.from_core(0, 6)
    for q in hx:
        q.wait_send()
    for q in c_plan:
        q.wait()
    l_x.wait()
    l_c2.wait()
    for k in (2, 3):
        for q in outs(k, k % 2):
            q.wait()
    for g in [bias, w1] + w2 + w3:
        g.end()


def front(prefix, s, h, c, b):
    v_ = pltpu.VMEM
    dma = pltpu.SemaphoreType.DMA
    sd = jax.ShapeDtypeStruct
    return pl.pallas_call(
        front_kernel,
        out_shape=[
            sd((3, 2, 2, 4, 2, 96, 768), bf16), sd((4, 256, 768), bf16), sd((4, 256, 768), bf16), sd((2, 2, 4, 2, 16, 128), f32),
            sd((4, L, 640), bf16), sd((4, 640, L), bf16), sd((4, L, 256), bf16), sd((4, 256, L), bf16), sd((4, 8, L), f32),
        ],
        in_specs=[pl.BlockSpec(memory_space=pltpu.SMEM)] + [HBM] * 3 + [VM],
        out_specs=[HBM] * 3 + [VM] + [HBM] * 5,
        scratch_shapes=[
            v_((3, 96, 768), bf16), v_((4, 256, 768), bf16), v_((256, 768), bf16), v_((2, 4, 2, 96, 768), bf16),
            v_((2, L, 640), bf16), v_((2, 640, L), bf16), v_((2, L, 256), bf16), v_((2, 256, L), bf16), v_((2, 8, L), f32),
            v_((3, 256, L), bf16), v_((4, 256, 256), f32),
            dma((N_A,)), dma((N_A,)), dma((10,)), dma((2, 5)),
        ],
        compiler_params=pltpu.CompilerParams(collective_id=0, has_side_effects=True, vmem_limit_bytes=67043328),
    )(prefix, s, h, c, b)


EPSILON = 1e-12


def norm_stats(r):
    center = r - jnp.mean(r, axis=-1, keepdims=True)
    inv = lax.rsqrt(jnp.mean(center * center, axis=-1, keepdims=True) + EPSILON)
    return center * inv, inv


def norm_back(cot, gain, xhat, inv):
    e = cot * gain
    grad = (e - jnp.mean(e, -1, keepdims=True) - xhat * jnp.mean(e * xhat, -1, keepdims=True)) * inv
    return grad, jnp.sum(cot * xhat, 0), jnp.sum(cot, 0)


def middle(x, cot, heads, w1, w2, w3, bias_o, bias_h, bias_d, shift1, shift2, gain1, gain2):
    ein = functools.partial(jnp.einsum, preferred_element_type=f32)
    hid = x.astype(f32)
    resid1 = hid + ein("tpw,tdw->pd", heads, w1[:, :, 512:]) + bias_o
    xhat1, inv1 = norm_stats(resid1)
    normed = xhat1 * gain1 + shift1
    low = normed.astype(bf16)
    pre = ein("pd,tdf->tpf", low, w2) + bias_h[:, None, :]
    act, gelu_back = jax.vjp(lambda v: jax.nn.gelu(v, approximate=False), pre)
    act = act.astype(bf16)
    resid2 = normed + ein("tpf,tdf->pd", act, w3) + bias_d
    xhat2, inv2 = norm_stats(resid2)
    out = (xhat2 * gain2 + shift2).astype(bf16)
    g2, dgain2, dshift2 = norm_back(cot.astype(f32), gain2, xhat2, inv2)
    g2low = g2.astype(bf16)
    d3 = ein("pd,tpf->tdf", g2low, act).astype(bf16)
    gpre = gelu_back(ein("pd,tdf->tpf", g2low, w3))[0].astype(bf16)
    d2 = ein("pd,tpf->tdf", low, gpre).astype(bf16)
    gn = g2 + ein("tpf,tdf->pd", gpre, w2)
    g1, dgain1, dshift1 = norm_back(gn, gain1, xhat1, inv1)
    g1low = g1.astype(bf16)
    dout = ein("pd,tpw->tdw", g1low, heads).astype(bf16)
    dbh = jnp.sum(gpre, 1, dtype=f32)
    return out, g1, g1low, dout, d2, d3, (dgain1, dgain2, dshift1, dshift2, jnp.sum(g1, 0), dbh, jnp.sum(g2, 0))


def on_device(hidden_in, cotangent, prefix, w_qkv, w_out, w_in, w_down, biases, gains):
    rows = w_qkv.shape[0]
    n_t = lax.axis_size("tensor")
    t_me, d_me = lax.axis_index("tensor"), lax.axis_index("dp")
    n_dev = n_t * lax.axis_size("dp")
    s = jnp.stack([jnp.concatenate([w_qkv.reshape(rows, -1), w_out.T], axis=1), w_in, w_down.T])
    vecs = jnp.concatenate([biases, gains], 0)
    width = vecs.shape[1]
    vecs = jnp.pad(vecs, ((0, 4), (0, 128 - width)))
    seqs = lambda a: jnp.transpose(a, (1, 0, 2))
    h, c = seqs(hidden_in), seqs(cotangent)
    my_prefix = lax.dynamic_slice_in_dim(prefix, t_me, 1, 0)
    if lax.axis_size("dp") == 8:
        g, xs, cs, b, proj, projT, heads, ot, lse = front(my_prefix, s, h, c, vecs)
        b = b.transpose(2, 3, 0, 1, 4, 5)
    else:
        g = lax.all_gather(lax.all_gather(s, "dp", axis=1, tiled=True), "tensor", axis=1)
        xs = lax.all_to_all(h, "tensor", 0, 0, tiled=True)
        cs = lax.all_to_all(c, "tensor", 0, 0, tiled=True)
        b = lax.all_gather(vecs, ("dp", "tensor"), axis=0)
    w1, w2, w3 = [a.reshape(n_t, 768, 768) for a in g]
    vec = b.reshape(n_dev, 16, 128)[:, :12, :width].transpose(1, 0, 2).reshape(12, 768)
    x = xs.reshape(1024, 768)
    if lax.axis_size("dp") != 8:
        bqkv = jnp.pad(jnp.stack([vec[0].reshape(4, 192), jnp.zeros((4, 192), f32), vec[1].reshape(4, 192)], 1).reshape(4, 1, 576), ((0, 0), (0, 0), (0, 64)))
        proj, projT, heads, ot, lse = attn_fwd(my_prefix, x, w1, bqkv)
    out, g1, g1low, doutw, d2, d3, small = middle(
        x, cs.reshape(1024, 768), heads, w1, w2, w3, vec[2], vec[3:7].reshape(4, 768), vec[7], vec[8], vec[9], vec[10], vec[11]
    )
    ein = functools.partial(jnp.einsum, preferred_element_type=f32)
    dgain1, dgain2, dshift1, dshift2, dbo, dbh, dbd = small
    o4 = out.reshape(4, 256, 768)
    none = jnp.zeros((1, 768), f32)
    v = [none, none, dbo[None], dbh, jnp.stack([dbd, dshift1, dshift2, dgain1, dgain2]), jnp.zeros((4, 768), f32)]
    if lax.axis_size("dp") == 8:
        gs, vs, oo, xx = back(
            my_prefix, xs, g1low, g1, g, proj, projT, ot, lse, doutw, jnp.stack([d2, d3]).reshape(2, 2, 2, 4, 2, rows, 768),
            jnp.concatenate(v + [jnp.zeros((8, 768), f32)]), o4,
        )
        qv = vs[16:24, :256].reshape(4, 2, 256)
        vs = jnp.concatenate([qv[:, 0, :192].reshape(1, 768), qv[:, 1, :192].reshape(1, 768), vs[2:16]])
    else:
        gproj = attn_bwd(my_prefix, g1low, w1, proj, projT, ot, lse)
        gp = gproj[:, :, :576]
        dqkv = ein("pd,tpc->tdc", x, gp).astype(bf16)
        x4 = (g1 + ein("tpc,tdc->pd", gp, w1[:, :, :576])).astype(bf16).reshape(4, 256, 768)
        v[0] = jnp.sum(gp[:, :, :192], 1, dtype=f32).reshape(1, 768)
        v[1] = jnp.sum(gp[:, :, 384:], 1, dtype=f32).reshape(1, 768)
        d = jnp.stack([jnp.concatenate([dqkv, doutw[:, :, 64:]], 2), d2, d3])
        part = lax.all_to_all(d, "tensor", 1, 1, tiled=True).astype(f32).sum(1)
        part = part.astype(bf16).reshape(3, -1, rows, 768)
        gs = lax.all_to_all(part, "dp", 1, 1, tiled=True).astype(f32).sum(1)
        vs = lax.psum(jnp.concatenate(v), ("dp", "tensor"))
        oo = lax.all_to_all(o4, "tensor", 0, 0, tiled=True)
        xx = lax.all_to_all(x4, "tensor", 0, 0, tiled=True)
    mine = lax.dynamic_slice_in_dim(vs, (d_me * n_t + t_me) * width, width, 1)
    return (
        seqs(oo),
        seqs(xx),
        gs[0, :, :576].reshape(rows, 3, 192),
        gs[0, :, 576:].T,
        gs[1],
        gs[2].T,
        mine[:10],
        mine[10:12],
    )


def solution(mesh):
    placed = (
        P("tensor", "dp", None),
        P("tensor", "dp", None),
        P("dp"),
        P("dp", None, "tensor"),
        P("tensor", "dp"),
        P("dp", "tensor"),
        P("tensor", "dp"),
        P(None, ("dp", "tensor")),
        P(None, ("dp", "tensor")),
    )
    return jax.shard_map(on_device, mesh=mesh, in_specs=placed, out_specs=placed[:2] + placed[3:], check_vma=False)
```

```python
import functools
import math

import jax
import jax.numpy as jnp
from jax import lax
from jax.experimental import pallas as pl
from jax.experimental.pallas import tpu as pltpu
from jax.sharding import PartitionSpec as P

f32=jnp.float32; bf16=jnp.bfloat16
L=1024; QB=256; NK=(512,512,768,1024)
C2=0.125*math.log2(math.e)
NEG=-1e30
def dotf(a,b): return jnp.dot(a,b,preferred_element_type=f32)
def dot_nt(a,b): return lax.dot_general(a,b,(((1,),(1,)),((),())),preferred_element_type=f32)
def masks(mask_ref, prefix):
    k=lax.broadcasted_iota(jnp.int32,(256,256),0); q=lax.broadcasted_iota(jnp.int32,(256,256),1)
    diag=k<=q
    mask_ref[0]=jnp.where(diag|(k<prefix),0.0,NEG)
    mask_ref[1]=jnp.where(k+256<prefix,0.0,NEG)+jnp.zeros((256,256),f32)
    mask_ref[2]=jnp.where(diag|(k+256<prefix),0.0,NEG)
    mask_ref[3]=jnp.where(diag,0.0,NEG)
MASKMAP={0:{0:0,1:1},1:{1:2},2:{2:3},3:{3:3}}
def masked(st,qb,mask_ref):
    parts=[]
    for kb in range(NK[qb]//256):
        p=st[kb*256:(kb+1)*256]
        mi=MASKMAP[qb].get(kb)
        parts.append(p if mi is None else p+mask_ref[mi])
    return jnp.concatenate(parts,0)
def fwd_kernel(prefix_ref,x_ref,w_ref,b_ref,proj_ref,projT_ref,heads_ref,ot_ref,lse_ref,zq_ref,mask_ref):
    masks(mask_ref,prefix_ref[0])
    proj=(dotf(x_ref[...],w_ref[:,:640])+b_ref[...]).astype(bf16)
    proj_ref[...]=proj
    projT_ref[...]=proj.T
    zq_ref[...]=jnp.zeros_like(zq_ref)
    for h in range(3):
        zq_ref[h,64+64*h:128+64*h,:]=projT_ref[64*h:64*h+64,:]
    ot_ref[...]=jnp.zeros_like(ot_ref)
    for h in range(3):
        for qb in range(4):
            nk=NK[qb]; qs=slice(qb*QB,qb*QB+QB)
            st=dotf(proj_ref[:nk,128:384],zq_ref[h,:,qs])
            st=masked(st,qb,mask_ref)
            m=jnp.max(st,axis=0,keepdims=True)
            p=jnp.exp2((st-m)*C2)
            l=jnp.sum(p,axis=0,keepdims=True)
            ot=dotf(projT_ref[384+64*h:448+64*h,:nk],p.astype(bf16))
            ot_ref[64+64*h:128+64*h,qs]=(ot/l).astype(bf16)
            lse_ref[h:h+1,qs]=m*C2+jnp.log2(l)
    heads_ref[...]=ot_ref[...].T
def attn_fwd(prefix,x,w1,bqkv):
    sq=pl.squeezed
    return pl.pallas_call(fwd_kernel,grid_spec=pltpu.PrefetchScalarGridSpec(num_scalar_prefetch=1,grid=(4,),
      in_specs=[pl.BlockSpec((L,768),lambda t,p:(0,0)),pl.BlockSpec((sq,768,768),lambda t,p:(t,0,0)),pl.BlockSpec((sq,1,640),lambda t,p:(t,0,0))],
      out_specs=[pl.BlockSpec((sq,L,640),lambda t,p:(t,0,0)),pl.BlockSpec((sq,640,L),lambda t,p:(t,0,0)),pl.BlockSpec((sq,L,256),lambda t,p:(t,0,0)),pl.BlockSpec((sq,256,L),lambda t,p:(t,0,0)),pl.BlockSpec((sq,8,L),lambda t,p:(t,0,0))],
      scratch_shapes=[pltpu.VMEM((3,256,L),bf16),pltpu.VMEM((4,256,256),f32)]),
      out_shape=[jax.ShapeDtypeStruct((4,L,640),bf16),jax.ShapeDtypeStruct((4,640,L),bf16),jax.ShapeDtypeStruct((4,L,256),bf16),jax.ShapeDtypeStruct((4,256,L),bf16),jax.ShapeDtypeStruct((4,8,L),f32)],
      compiler_params=pltpu.CompilerParams(vmem_limit_bytes=62<<20))(prefix,x,w1,bqkv)
def bwd_kernel(prefix_ref,g_ref,w_ref,proj_ref,projT_ref,ot_ref,lse_ref,gproj_ref,
               zq_ref,zdo_ref,qm_ref,dom_ref,pt_ref,ds_ref,mask_ref,gt_ref,dqt_ref):
    masks(mask_ref,prefix_ref[0])
    gh=dotf(g_ref[...],w_ref[:,512:768]).astype(bf16)
    gt_ref[...]=gh.T
    zq_ref[...]=jnp.zeros_like(zq_ref); zdo_ref[...]=jnp.zeros_like(zdo_ref)
    lane=lax.broadcasted_iota(jnp.int32,(1,256),1)
    for h in range(3):
        zq_ref[h,64+64*h:128+64*h,:]=projT_ref[64*h:64*h+64,:]
        zdo_ref[h,64*h:64*h+64,:]=gt_ref[64+64*h:128+64*h,:]*0.125
        sel=(lane>=64*h)&(lane<64*h+64)
        qm_ref[h]=jnp.where(sel,proj_ref[:,0:256],0)
        sel2=(lane>=64*h+64)&(lane<64*h+128)
        dom_ref[h]=jnp.where(sel2,gh,0)
    for h in range(3):
        d=jnp.sum(gt_ref[64+64*h:128+64*h,:].astype(f32)*ot_ref[64+64*h:128+64*h,:].astype(f32),axis=0,keepdims=True)*0.125
        for qb in range(4):
            nk=NK[qb]; qs=slice(qb*QB,qb*QB+QB)
            st=dotf(proj_ref[:nk,128:384],zq_ref[h,:,qs])
            st=masked(st,qb,mask_ref)
            p=jnp.exp2(st*C2-lse_ref[h:h+1,qs])
            dp=dotf(proj_ref[:nk,384:640],zdo_ref[h,:,qs])
            ds=(p*(dp-d[:,qs])).astype(bf16)
            pt_ref[h,:nk,qs]=p.astype(bf16)
            ds_ref[h,:nk,qs]=ds
            dqt_ref[64*h:64*h+64,qs]=dotf(projT_ref[192+64*h:256+64*h,:nk],ds).astype(bf16)
    gproj_ref[:,0:192]=dqt_ref[...].T
    for (k0,k1,q0) in ((0,512,0),(512,768,512),(768,1024,768)):
        dk=jnp.zeros((k1-k0,256),f32); dv=jnp.zeros((k1-k0,256),f32)
        for h in range(3):
            dk=dk+dotf(ds_ref[h,k0:k1,q0:],qm_ref[h,q0:,:])
            dv=dv+dotf(pt_ref[h,k0:k1,q0:],dom_ref[h,q0:,:])
        gproj_ref[k0:k1,192:384]=dk[:,0:192].astype(bf16)
        gproj_ref[k0:k1,384:576]=dv[:,64:256].astype(bf16)
    gproj_ref[:,576:640]=jnp.zeros((L,64),bf16)
def attn_bwd(prefix,g,w1,proj,projT,ot,lse):
    sq=pl.squeezed
    sp=lambda *s: pl.BlockSpec((sq,)+s,lambda t,p:(t,0,0))
    return pl.pallas_call(functools.partial(bwd_kernel),grid_spec=pltpu.PrefetchScalarGridSpec(num_scalar_prefetch=1,grid=(4,),
      in_specs=[pl.BlockSpec((L,768),lambda t,p:(0,0)),sp(768,768),sp(L,640),sp(640,L),sp(256,L),sp(8,L)],
      out_specs=sp(L,640),
      scratch_shapes=[pltpu.VMEM((3,256,L),bf16),pltpu.VMEM((3,256,L),bf16),pltpu.VMEM((3,L,256),bf16),pltpu.VMEM((3,L,256),bf16),pltpu.VMEM((3,L,L),bf16),pltpu.VMEM((3,L,L),bf16),pltpu.VMEM((4,256,256),f32),pltpu.VMEM((256,L),bf16),pltpu.VMEM((192,L),bf16)]),
      out_shape=jax.ShapeDtypeStruct((4,L,640),bf16),
      compiler_params=pltpu.CompilerParams(vmem_limit_bytes=62<<20))(prefix,g,w1,proj,projT,ot,lse)
MESH=pl.DeviceIdType.MESH
class Place:
    def __init__(self):
        dp=lax.axis_index("dp"); t=lax.axis_index("tensor")
        self.dp,self.t=dp,t
        self.z,self.x,self.y,self.c=dp//2,dp%2,t//2,t%2
    def peer(self,dim,j=1):
        return {'x':lambda:(self.dp^1,self.t),'z':lambda:(self.dp^(2*j),self.t),'y':lambda:(self.dp,self.t^2),'c':lambda:(self.dp,self.t^1)}[dim]()
    def peers_all(self):
        return [self.peer('x'),self.peer('y'),self.peer('c'),self.peer('z',1),self.peer('z',2),self.peer('z',3),(self.dp,self.t^3)]
def barrier(peers):
    b=pltpu.get_barrier_semaphore()
    for p in peers: pl.semaphore_signal(b,inc=1,device_id=p,device_id_type=MESH)
    pl.semaphore_wait(b,len(peers))
class Sems:
    def __init__(self,send,recv): self.s,self.r,self.n=send,recv,0
    def take(self):
        i=self.n; self.n+=1
        return self.s.at[i],self.r.at[i]
def rcopy(src,dst,sems,dev):
    a,b=sems.take()
    return pltpu.make_async_remote_copy(src_ref=src,dst_ref=dst,send_sem=a,recv_sem=b,device_id=dev,device_id_type=MESH)
def local(src,dst,sem):
    k=pltpu.make_async_copy(src,dst,sem); k.start(); return k
def exchange(pc,src,dst,sems):
    out=[]
    for j in (2,3,1):
        p=(pc.dp,pc.t^j)
        k=rcopy(src.at[pc.t^j],dst.at[pc.t],sems,p); k.start(); out.append(k)
    return out
HBM=pl.BlockSpec(memory_space=pltpu.HBM); VM=pl.BlockSpec(memory_space=pltpu.VMEM)
def point(steps, k, h):
    for kk in range(4):
        todo = steps.get((kk, h))
        if todo:
            @pl.when(k == kk)
            def _(todo=todo):
                for step in todo:
                    step()


def add_into(dst, src, n, pick_dst, pick_src):
    def body(j, _):
        a, b = pick_dst(j), pick_src(j)
        dst[a] = (dst[a].astype(f32) + src[b].astype(f32)).astype(bf16)
        return 0
    lax.fori_loop(0, n, body, 0)


class Reduce:
    def __init__(self, pc, d_ref, half, lc, rc, r1, r2, r3, sems, lsem):
        self.pc, self.lc, self.rc, self.r1, self.r2, self.r3 = pc, lc, rc, r1, r2, r3
        rows = pl.ds(48 * half, 48)
        self.own = pltpu.make_async_copy(d_ref.at[:, pc.c, :, :, rows], lc, lsem)
        self.q0 = rcopy(d_ref.at[:, 1 - pc.c, :, :, rows], rc, sems, pc.peer("c"))
        self.q1 = rcopy(lc.at[:, :, 1 - pc.x], r1, sems, pc.peer("x"))
        self.q2 = [rcopy(lc.at[:, pc.z ^ j, pc.x], r2.at[j - 1], sems, pc.peer("z", j)) for j in (3, 2, 1)]
        self.q3 = rcopy(lc.at[1 - pc.y, pc.z, pc.x], r3, sems, pc.peer("y"))

    def s0(self):
        self.own.start()
        self.q0.start()

    def s1(self):
        self.own.wait()
        self.q0.wait_recv()
        at = lambda j: (j // 8, (j // 2) % 4, j % 2)
        add_into(self.lc, self.rc, 16, at, at)
        self.q1.start()

    def s2(self):
        self.q1.wait_recv()
        add_into(self.lc, self.r1, 8, lambda j: (j // 4, j % 4, self.pc.x), lambda j: (j // 4, j % 4))
        for q in self.q2:
            q.start()

    def s3(self):
        pc = self.pc
        for q in self.q2:
            q.wait_recv()
        for y in range(2):
            at = (y, pc.z, pc.x)
            total = (self.lc[at].astype(f32) + self.r2[0, y].astype(f32)) + (self.r2[1, y].astype(f32) + self.r2[2, y].astype(f32))
            self.lc[at] = total.astype(bf16)
        self.q3.start()

    def s4(self, out_ref, rows):
        pc = self.pc
        self.q3.wait_recv()
        out_ref[rows] = self.lc[pc.y, pc.z, pc.x].astype(f32) + self.r3[...].astype(f32)

    def end(self):
        for q in [self.q0, self.q1, self.q3] + self.q2:
            q.wait_send()


N_C = 4 * 6 + 1 + 1 + 1 + 2 + 6 + 6 + 6


def back_kernel(
    prefix_ref, x_ref, g_ref, gf_ref, w_ref, proj_ref, projT_ref, ot_ref, lse_ref, dout_ref, d_ref, v_ref, out_ref,
    gs_ref, vs_ref, oo_ref, xo_ref,
    xT, gl, dxa, w_b, proj_b, projT_b, ot_b, lse_b, dout_b,
    zq, zdo, qm, dom, pt, ds, mask_ref, gt, dqt, dkb, dvb, gproj,
    lc, rc, r1, r2, r3, dwb, cr, yr, xr, zr, vb, vr, xst, ss, rs, ls, ins,
):
    pc = Place()
    sems = Sems(ss, rs)
    w1 = w_ref.at[0]
    lane = lax.broadcasted_iota(jnp.int32, (1, 256), 1)

    def loads(k, slot):
        t = pc.t ^ (3 - k)
        pairs = [
            (w1.at[t // 2, t % 2], w_b), (proj_ref.at[t], proj_b), (projT_ref.at[t], projT_b),
            (ot_ref.at[t], ot_b), (lse_ref.at[t], lse_b), (dout_ref.at[t], dout_b),
        ]
        return [pltpu.make_async_copy(a, b.at[slot], ins.at[slot, n]) for n, (a, b) in enumerate(pairs)]

    first = loads(0, 0)
    for q in first:
        q.start()
    l_x = local(x_ref, xst, ls.at[4])
    l_g = local(g_ref, gl, ls.at[5])
    l_f = local(gf_ref, dxa, ls.at[6])
    barrier(pc.peers_all())
    red = {}
    for n, (g, i) in enumerate(((1, 0), (1, 1), (0, 0), (0, 1))):
        red[n] = Reduce(pc, d_ref.at[g], i, lc.at[n], rc.at[n], r1.at[n], r2.at[n], r3.at[n], sems, ls.at[n])
        red[n].s0()
    ox = exchange(pc, out_ref, oo_ref, sems)
    l_o = [local(out_ref.at[pc.t], oo_ref.at[pc.t], ls.at[7])]
    q_c0 = rcopy(dwb.at[0], cr.at[0], sems, pc.peer("c"))
    q_y = rcopy(dwb.at[1], yr, sems, pc.peer("y"))
    q_c1 = rcopy(dwb.at[2], cr.at[1], sems, pc.peer("c"))
    half = [pl.ds(48 * i, 48) for i in range(2)]
    q_x = [rcopy(dwb.at[3, :, 1 - pc.x, half[i]], xr.at[i], sems, pc.peer("x")) for i in range(2)]
    q_z = [[rcopy(dwb.at[3, pc.z ^ j, pc.x, half[i]], zr.at[i, j - 1], sems, pc.peer("z", j)) for j in (3, 2, 1)] for i in range(2)]
    steps = {
        (0, 1): [red[0].s1], (0, 2): [red[1].s1], (0, 3): [red[2].s1], (1, 1): [red[3].s1],
        (1, 3): [red[0].s2], (2, 3): [red[1].s2], (3, 0): [red[0].s3], (3, 3): [red[2].s2],
    }
    masks(mask_ref, prefix_ref[0])
    zq[...] = jnp.zeros_like(zq)
    zdo[...] = jnp.zeros_like(zdo)
    gproj[:, 576:640] = jnp.zeros((L, 64), bf16)
    vb[0] = v_ref[...]
    l_x.wait()
    xT[...] = xst[...].reshape(L, 768).T
    l_g.wait()
    l_f.wait()

    def group(k, _):
        slot = k % 2
        for q in loads(k, slot):
            q.wait()

        @pl.when(k < 3)
        def _():
            for q in loads(k + 1, 1 - slot):
                q.start()

        t = pc.t ^ (3 - k)
        w, pj, pjT, o_t, lse = w_b.at[slot], proj_b.at[slot], projT_b.at[slot], ot_b.at[slot], lse_b.at[slot]
        gh = dotf(gl[...], w[...].reshape(768, 768)[:, 512:768]).astype(bf16)
        gt[...] = gh.T
        for h in range(3):
            point(steps, k, h)
            own = slice(64 + 64 * h, 128 + 64 * h)
            zq[h, own, :] = pjT[64 * h : 64 * h + 64, :]
            zdo[h, 64 * h : 64 * h + 64, :] = gt[own, :] * 0.125
            qm[...] = jnp.where((lane >= 64 * h) & (lane < 64 * h + 64), pj[:, 0:256], 0)
            dom[...] = jnp.where((lane >= 64 * h + 64) & (lane < 64 * h + 128), gh, 0)
            d = jnp.sum(gt[own, :].astype(f32) * o_t[own, :].astype(f32), axis=0, keepdims=True) * 0.125
            for qb in range(4):
                nk = NK[qb]
                qs = slice(qb * QB, qb * QB + QB)
                st = masked(dotf(pj[:nk, 128:384], zq[h, :, qs]), qb, mask_ref)
                p = jnp.exp2(st * C2 - lse[h : h + 1, qs])
                dp = dotf(pj[:nk, 384:640], zdo[h, :, qs])
                dsv = (p * (dp - d[:, qs])).astype(bf16)
                pt[:nk, qs] = p.astype(bf16)
                ds[:nk, qs] = dsv
                dqt[64 * h : 64 * h + 64, qs] = dotf(pjT[192 + 64 * h : 256 + 64 * h, :nk], dsv).astype(bf16)
            for k0, k1, q0 in ((0, 512, 0), (512, 768, 512), (768, 1024, 768)):
                dk = dotf(ds[k0:k1, q0:], qm[q0:, :]).astype(bf16)
                dv = dotf(pt[k0:k1, q0:], dom[q0:, :]).astype(bf16)
                dkb[k0:k1] = dk if h == 0 else dkb[k0:k1] + dk
                dvb[k0:k1] = dv if h == 0 else dvb[k0:k1] + dv
        point(steps, k, 3)
        gproj[:, 0:192] = dqt[...].T
        gproj[:, 192:384] = dkb[:, 0:192]
        gproj[:, 384:576] = dvb[:, 64:256]
        vb[0, pl.ds(16 + 2 * t, 1), 0:256] = jnp.sum(gproj[:, 0:256].astype(f32), axis=0, keepdims=True)
        vb[0, pl.ds(17 + 2 * t, 1), 0:256] = jnp.sum(gproj[:, 384:640].astype(f32), axis=0, keepdims=True)
        dw = dotf(xT[...], gproj[...])
        do = dout_b[slot].astype(f32)
        shape = lambda a: a.astype(bf16).reshape(4, 2, 96, a.shape[1])
        dwb[k, :, :, :, 0:512] = shape(dw[:, 0:512])
        dwb[k, :, :, :, 512:640] = shape(dw[:, 512:640] + do[:, 0:128])
        dwb[k, :, :, :, 640:768] = shape(do[:, 128:256])

        @pl.when(k == 0)
        def _():
            q_c0.start()

        @pl.when(k == 1)
        def _():
            q_c0.wait_recv()
            add_into(dwb.at[1], cr.at[0], 8, lambda j: (j // 2, j % 2), lambda j: (j // 2, j % 2))
            q_y.start()

        @pl.when(k == 2)
        def _():
            q_c1.start()

        @pl.when(k == 3)
        def _():
            q_c1.wait_recv()
            add_into(dwb.at[3], cr.at[1], 8, lambda j: (j // 2, j % 2), lambda j: (j // 2, j % 2))
            q_y.wait_recv()
            add_into(dwb.at[3], yr, 8, lambda j: (j // 2, j % 2), lambda j: (j // 2, j % 2))
            for q in q_x:
                q.start()

        dxa[...] += dot_nt(gproj[...], w[...].reshape(768, 768)[:, 0:640])
        return 0

    lax.fori_loop(0, 4, group, 0)
    xst[...] = dxa[...].astype(bf16).reshape(4, 256, 768)
    v_q = [rcopy(vb.at[0], vr.at[0], sems, pc.peer("c"))]
    v_q[0].start()
    xx = exchange(pc, xst, xo_ref, sems)
    l_o.append(local(xst.at[pc.t], xo_ref.at[pc.t], ls.at[8]))

    def vstep(n, dim):
        v_q[n].wait_recv()
        vb[n + 1] = vb[n] + vr[n]
        v_q.append(rcopy(vb.at[n + 1], vr.at[n + 1], sems, pc.peer(dim)))
        v_q[n + 1].start()

    vstep(0, "x")
    red[1].s3()
    for i in range(2):
        q_x[i].wait_recv()
        for z in range(4):
            dwb[3, z, pc.x, half[i]] = (dwb[3, z, pc.x, half[i]].astype(f32) + xr[i, z].astype(f32)).astype(bf16)
        for q in q_z[i]:
            q.start()
    vstep(1, "y")
    red[3].s2()
    red[2].s3()
    v_q[2].wait_recv()
    vb[3] = vb[2] + vr[2]
    v_z = [rcopy(vb.at[3], vr.at[2 + j], sems, pc.peer("z", j)) for j in (3, 2, 1)]
    for q in v_z:
        q.start()
    red[0].s4(gs_ref.at[2], slice(0, 48))
    red[1].s4(gs_ref.at[2], slice(48, 96))
    red[3].s3()
    for i in range(2):
        for q in q_z[i]:
            q.wait_recv()
        gs_ref[0, 48 * i : 48 * i + 48] = (dwb[3, pc.z, pc.x, half[i]].astype(f32) + zr[i, 0].astype(f32)) + (zr[i, 1].astype(f32) + zr[i, 2].astype(f32))
    red[2].s4(gs_ref.at[1], slice(0, 48))
    for q in v_z:
        q.wait_recv()
    vs_ref[...] = (vb[3] + vr[3]) + (vr[4] + vr[5])
    red[3].s4(gs_ref.at[1], slice(48, 96))
    for q in l_o:
        q.wait()
    for q in ox + xx:
        q.wait()
    for n in range(4):
        red[n].end()
    for q in [q_c0, q_y, q_c1] + q_x + q_z[0] + q_z[1] + v_q + v_z:
        q.wait_send()


def back(prefix, x, g1low, g1, g, proj, projT, ot, lse, doutw, d, v, out4):
    v_ = pltpu.VMEM
    dma = pltpu.SemaphoreType.DMA
    sd = jax.ShapeDtypeStruct
    return pl.pallas_call(
        back_kernel,
        out_shape=[sd((3, 96, 768), f32), sd((24, 768), f32), sd((4, 256, 768), bf16), sd((4, 256, 768), bf16)],
        in_specs=[pl.BlockSpec(memory_space=pltpu.SMEM)] + [HBM] * 10 + [VM, HBM],
        out_specs=[VM, VM, HBM, HBM],
        scratch_shapes=[
            v_((768, L), bf16), v_((L, 768), bf16), v_((L, 768), f32),
            v_((2, 4, 2, 96, 768), bf16), v_((2, L, 640), bf16), v_((2, 640, L), bf16), v_((2, 256, L), bf16), v_((2, 8, L), f32), v_((2, 768, 256), bf16),
            v_((3, 256, L), bf16), v_((3, 256, L), bf16), v_((L, 256), bf16), v_((L, 256), bf16), v_((L, L), bf16), v_((L, L), bf16),
            v_((4, 256, 256), f32), v_((256, L), bf16), v_((192, L), bf16), v_((L, 256), bf16), v_((L, 256), bf16), v_((L, 640), bf16),
            v_((4, 2, 4, 2, 48, 768), bf16), v_((4, 2, 4, 2, 48, 768), bf16), v_((4, 2, 4, 48, 768), bf16), v_((4, 3, 2, 48, 768), bf16), v_((4, 48, 768), bf16),
            v_((4, 4, 2, 96, 768), bf16), v_((2, 4, 2, 96, 768), bf16), v_((4, 2, 96, 768), bf16), v_((2, 4, 48, 768), bf16), v_((2, 3, 48, 768), bf16),
            v_((4, 24, 768), f32), v_((6, 24, 768), f32), v_((4, 256, 768), bf16),
            dma((N_C,)), dma((N_C,)), dma((9,)), dma((2, 6)),
        ],
        compiler_params=pltpu.CompilerParams(collective_id=1, has_side_effects=True, vmem_limit_bytes=67043328),
    )(prefix, x, g1low, g1, g, proj, projT, ot, lse, doutw, d, v, out4)


class Gather:
    def __init__(self, pc, src, dst, rows, order, sems):
        self.pc, self.src, self.dst, self.rows, self.order, self.sems = pc, src, dst, rows, order, sems
        self.full, self.sent, self.core = set(), [], []
        self.plan()

    def at(self, over, full):
        pc = self.pc
        ix = {d: over.get(d, slice(None) if d in full else getattr(pc, d)) for d in "yzx"}
        return self.dst.at[(ix["y"], pc.c, ix["z"], ix["x"]) + ((pl.ds(*self.rows),) if self.rows else ())]

    def plan(self):
        pc = self.pc
        src = self.src.at[pl.ds(*self.rows)] if self.rows else self.src
        mine = self.at({}, set())
        self.core.append(rcopy(src, mine, self.sems, pc.peer("c")))
        self.phases = []
        full = set()
        for d in self.order:
            ks = []
            for j in (1, 2, 3) if d == "z" else (1,):
                here = self.at({}, full)
                ks.append(rcopy(here if full else src, here, self.sems, pc.peer(d, j)))
                there = self.at({d: getattr(pc, d) ^ j}, full)
                self.core.append(rcopy(there, there, self.sems, pc.peer("c")))
            self.phases.append(ks)
            full = full | {d}
        self.first = [1]
        for ks in self.phases:
            self.first.append(self.first[-1] + len(ks))

    def start(self):
        self.core[0].start()
        for k in self.phases[0]:
            k.start()

    def arrive(self, p):
        for n, k in enumerate(self.phases[p]):
            k.wait_recv()
            self.core[self.first[p] + n].start()

    def next(self, p):
        self.arrive(p - 1)
        for k in self.phases[p]:
            k.start()

    def from_core(self, a, b):
        for k in self.core[a:b]:
            k.wait_recv()

    def end(self):
        for k in self.core + sum(self.phases, []):
            k.wait_send()


N_A = 6 * 11 + 6


def front_kernel(
    prefix_ref, s_ref, h_ref, c_ref, b_ref,
    g_ref, x_ref, co_ref, vec_ref, proj_ref, projT_ref, heads_ref, ot_ref, lse_ref,
    bv, sv, xv, cst, wv, proj_b, projT_b, heads_b, ot_b, lse_b, zq, mask_ref, ss, rs, ls, os_,
):
    pc = Place()
    sems = Sems(ss, rs)
    own = (pc.y, pc.c, pc.z, pc.x)
    l_s = local(s_ref, sv, ls.at[0])
    l_h = local(h_ref.at[pc.t], xv.at[pc.t], ls.at[1])
    l_c = local(c_ref.at[pc.t], cst, ls.at[2])
    l_b = local(b_ref, bv.at[own], ls.at[9])
    barrier(pc.peers_all())
    bias = Gather(pc, b_ref, bv, None, "zxy", sems)
    w1 = Gather(pc, s_ref.at[0], g_ref.at[0], None, "zxy", sems)
    w2 = [Gather(pc, s_ref.at[1], g_ref.at[1], (48 * i, 48), "yzx", sems) for i in range(2)]
    w3 = [Gather(pc, s_ref.at[2], g_ref.at[2], (48 * i, 48), "yzx", sems) for i in range(2)]
    bias.start()
    w1.start()
    w2[0].start()
    w2[1].start()
    hx = exchange(pc, h_ref, xv, sems)
    w3[0].start()
    w3[1].start()
    l_s.wait()
    l_g = [local(sv.at[g], g_ref.at[g].at[own], ls.at[3 + g]) for g in range(3)]
    l_c.wait()
    l_c2 = local(cst, co_ref.at[pc.t], ls.at[6])
    masks(mask_ref, prefix_ref[0])
    zq[...] = jnp.zeros_like(zq)
    ot_b[...] = jnp.zeros_like(ot_b)
    for q in l_g:
        q.wait()
    l_b.wait()
    w1.next(1)
    bias.next(1)
    w2[0].next(1)
    w1.next(2)
    bias.next(2)
    w2[1].next(1)
    bias.arrive(2)
    bias.from_core(0, len(bias.core))
    l_h.wait()
    for q in hx:
        q.wait_recv()
    l_x = local(xv, x_ref, ls.at[7])
    c_plan = [rcopy(c_ref.at[pc.t ^ j], co_ref.at[pc.t], sems, (pc.dp, pc.t ^ j)) for j in (2, 3, 1)]

    def load(k, slot):
        t = pc.t ^ k
        return pltpu.make_async_copy(g_ref.at[0, t // 2, t % 2], wv.at[slot], ls.at[8])

    def start_cot():
        for q in c_plan:
            q.start()

    steps = {
        (0, 1): [lambda: w3[0].next(1), lambda: w3[1].next(1)],
        (0, 2): [lambda: w1.from_core(0, 5), lambda: load(1, 1).start()],
        (1, 0): [lambda: w2[0].next(2)],
        (1, 1): [start_cot],
        (1, 3): [lambda: w1.arrive(2), lambda: load(2, 0).start()],
        (2, 0): [lambda: w2[1].next(2)],
        (2, 2): [lambda: w1.from_core(5, 6), lambda: load(3, 1).start()],
        (3, 2): [lambda: w3[0].next(2)],
    }
    load(0, 0).start()

    def outs(k, slot):
        t = pc.t ^ k
        pairs = [(proj_b, proj_ref), (projT_b, projT_ref), (heads_b, heads_ref), (ot_b, ot_ref), (lse_b, lse_ref)]
        return [pltpu.make_async_copy(a.at[slot], b.at[t], os_.at[slot, n]) for n, (a, b) in enumerate(pairs)]

    def group(k, _):
        slot = k % 2
        t = pc.t ^ k
        load(k, slot).wait()

        @pl.when(k >= 2)
        def _():
            for q in outs(k - 2, slot):
                q.wait()

        row = jnp.zeros((8, 256), f32)
        for i in range(8):
            piece = bv[(i // 2) % 2, i % 2, t, i // 4, 0:8, :]
            row = row + pltpu.roll(jnp.concatenate([piece, jnp.zeros((8, 128), f32)], 1), 24 * i, 1)
        brow = jnp.concatenate([row[0:1], jnp.zeros((1, 128), f32), row[1:2]], 1)
        pj, pjT, ot, lse = proj_b.at[slot], projT_b.at[slot], ot_b.at[slot], lse_b.at[slot]
        proj = (dotf(xv[...].reshape(L, 768), wv[slot].reshape(768, 768)[:, :640]) + brow).astype(bf16)
        pj[...] = proj
        pjT[...] = proj.T
        for h in range(3):
            point(steps, k, h)
            zq[h, 64 + 64 * h : 128 + 64 * h, :] = pjT[64 * h : 64 * h + 64, :]
            for qb in range(4):
                nk = NK[qb]
                qs = slice(qb * QB, qb * QB + QB)
                st = masked(dotf(pj[:nk, 128:384], zq[h, :, qs]), qb, mask_ref)
                m = jnp.max(st, axis=0, keepdims=True)
                p = jnp.exp2((st - m) * C2)
                l = jnp.sum(p, axis=0, keepdims=True)
                o = dotf(pjT[384 + 64 * h : 448 + 64 * h, :nk], p.astype(bf16))
                ot[64 + 64 * h : 128 + 64 * h, qs] = (o / l).astype(bf16)
                lse[h : h + 1, qs] = m * C2 + jnp.log2(l)
        point(steps, k, 3)
        heads_b[slot] = ot[...].T
        for q in outs(k, slot):
            q.start()
        return 0

    lax.fori_loop(0, 4, group, 0)
    w3[1].next(2)
    tiles = [jnp.zeros((16, 128), f32) for _ in range(6)]
    lane = lax.broadcasted_iota(jnp.int32, (1, 128), 1)
    for i in range(32):
        z, x, y, c = i // 8, (i // 4) % 2, (i // 2) % 2, i % 2
        j, r = (24 * i) // 128, (24 * i) % 128
        piece = pltpu.roll(bv[y, c, z, x], r, 1) if r else bv[y, c, z, x]
        tiles[j] = tiles[j] + (jnp.where(lane >= r, piece, 0.0) if r > 104 else piece)
        if r > 104:
            tiles[j + 1] = tiles[j + 1] + jnp.where(lane < r, piece, 0.0)
    for j in range(6):
        vec_ref[:, 128 * j : 128 * j + 128] = tiles[j]
    for g in w2 + w3:
        g.arrive(2)
    for g in w2 + w3:
        g.from_core(0, 6)
    for q in hx:
        q.wait_send()
    for q in c_plan:
        q.wait()
    l_x.wait()
    l_c2.wait()
    for k in (2, 3):
        for q in outs(k, k % 2):
            q.wait()
    for g in [bias, w1] + w2 + w3:
        g.end()


def front(prefix, s, h, c, b):
    v_ = pltpu.VMEM
    dma = pltpu.SemaphoreType.DMA
    sd = jax.ShapeDtypeStruct
    return pl.pallas_call(
        front_kernel,
        out_shape=[
            sd((3, 2, 2, 4, 2, 96, 768), bf16), sd((4, 256, 768), bf16), sd((4, 256, 768), bf16), sd((16, 768), f32),
            sd((4, L, 640), bf16), sd((4, 640, L), bf16), sd((4, L, 256), bf16), sd((4, 256, L), bf16), sd((4, 8, L), f32),
        ],
        in_specs=[pl.BlockSpec(memory_space=pltpu.SMEM)] + [HBM] * 3 + [VM],
        out_specs=[HBM] * 3 + [VM] + [HBM] * 5,
        scratch_shapes=[
            v_((2, 2, 4, 2, 16, 128), f32), v_((3, 96, 768), bf16), v_((4, 256, 768), bf16), v_((256, 768), bf16), v_((2, 4, 2, 96, 768), bf16),
            v_((2, L, 640), bf16), v_((2, 640, L), bf16), v_((2, L, 256), bf16), v_((2, 256, L), bf16), v_((2, 8, L), f32),
            v_((3, 256, L), bf16), v_((4, 256, 256), f32),
            dma((N_A,)), dma((N_A,)), dma((10,)), dma((2, 5)),
        ],
        compiler_params=pltpu.CompilerParams(collective_id=0, has_side_effects=True, vmem_limit_bytes=67043328),
    )(prefix, s, h, c, b)


EPSILON = 1e-12


def gelu_pair(v):
    cdf = 0.5 + 0.5 * lax.erf(v * math.sqrt(0.5))
    pdf = jnp.exp2(v * v * (-0.5 * math.log2(math.e))) * (1.0 / math.sqrt(2.0 * math.pi))
    return v * cdf, cdf + v * pdf


def row_mean(a):
    return jnp.sum(a, axis=-1, keepdims=True) * (1.0 / 768.0)


def mid_kernel(
    x_ref, c_ref, heads_ref, g_ref, vec_ref,
    out_ref, g1_ref, g1low_ref, dout_ref, d_ref, v_ref,
    xv, cv, hv, wo, w2, w3, xhat, inv, low, act, gd, acc, glow, lowT, gT, stage, dst, ls, ds_,
):
    l_x = local(x_ref, xv, ls.at[0])
    l_h = local(heads_ref, hv, ls.at[1])
    l_wo = [local(g_ref.at[0, y, c, :, :, :, pl.ds(512, 256)], wo.at[2 * y + c], ls.at[2 + 2 * y + c]) for y in range(2) for c in range(2)]
    l_w2 = local(g_ref.at[1], w2, ls.at[6])
    l_w3 = local(g_ref.at[2], w3, ls.at[7])
    l_c = local(c_ref, cv, ls.at[8])
    row = lambda n: vec_ref[n : n + 1, :]
    v_ref[...] = jnp.zeros_like(v_ref)

    def add_row(n, a):
        v_ref[n : n + 1, :] += jnp.sum(a, axis=0, keepdims=True)

    for q in [l_x, l_h] + l_wo:
        q.wait()

    def first(b, _):
        rows = pl.ds(pl.multiple_of(b * 256, 256), 256)
        r = xv[b].astype(f32) + row(2)
        for t in range(4):
            r = r + dot_nt(hv[t, rows, :], wo[t].reshape(768, 256))
        center = r - row_mean(r)
        iv = lax.rsqrt(row_mean(center * center) + EPSILON)
        xh = center * iv
        xhat[rows, :] = xh
        inv[rows, :] = jnp.broadcast_to(iv, (256, 128))
        normed = xh * row(10) + row(8)
        low[rows, :] = normed.astype(bf16)
        acc[rows, :] = normed + row(7)
        return 0

    lax.fori_loop(0, 4, first, 0)
    l_w2.wait()
    l_w3.wait()

    def up(n, _):
        t, b = n // 4, n % 4
        rows = pl.ds(pl.multiple_of(b * 256, 256), 256)
        pre = dotf(low[rows, :], w2[t // 2, t % 2].reshape(768, 768)) + vec_ref[pl.ds(3 + t, 1), :]
        a, d = gelu_pair(pre)
        a = a.astype(bf16)
        act[t, rows, :] = a
        gd[t, rows, :] = d.astype(bf16)
        acc[rows, :] += dot_nt(a, w3[t // 2, t % 2].reshape(768, 768))
        return 0

    lax.fori_loop(0, 16, up, 0)
    l_c.wait()

    def second(b, _):
        rows = pl.ds(pl.multiple_of(b * 256, 256), 256)
        r = acc[rows, :]
        center = r - row_mean(r)
        iv = lax.rsqrt(row_mean(center * center) + EPSILON)
        xh = center * iv
        stage[b] = (xh * row(11) + row(9)).astype(bf16)
        ct = cv[b].astype(f32)
        e = ct * row(11)
        g2 = (e - row_mean(e) - xh * row_mean(e * xh)) * iv
        acc[rows, :] = g2
        glow[rows, :] = g2.astype(bf16)
        add_row(11, ct * xh)
        add_row(9, ct)
        add_row(7, g2)
        return 0

    lax.fori_loop(0, 4, second, 0)
    l_o = local(stage, out_ref, ls.at[0])
    gT[...] = glow[...].T
    lowT[...] = low[...].T

    def sends(t):
        return [pltpu.make_async_copy(dst.at[t % 2, n], d_ref.at[n, t], ds_.at[t % 2, n]) for n in range(2)]

    def down(t, _):
        wt2, wt3 = w2.at[t // 2, t % 2], w3.at[t // 2, t % 2]

        @pl.when(t >= 2)
        def _():
            for q in sends(t - 2):
                q.wait()

        dst[t % 2, 1] = dotf(gT[...], act[t]).astype(bf16)
        for b in range(4):
            rows = slice(256 * b, 256 * b + 256)
            ga = dotf(glow[rows, :], wt3[...].reshape(768, 768))
            gp = (ga * gd[t, rows, :].astype(f32)).astype(bf16)
            gd[t, rows, :] = gp
            acc[rows, :] += dot_nt(gp, wt2[...].reshape(768, 768))
            v_ref[pl.ds(3 + t, 1), :] += jnp.sum(gp.astype(f32), axis=0, keepdims=True)
        dst[t % 2, 0] = dotf(lowT[...], gd[t]).astype(bf16)
        for q in sends(t):
            q.start()
        return 0

    lax.fori_loop(0, 4, down, 0)

    def last(b, _):
        rows = pl.ds(pl.multiple_of(b * 256, 256), 256)
        gn, xh = acc[rows, :], xhat[rows, :]
        e = gn * row(10)
        g1 = (e - row_mean(e) - xh * row_mean(e * xh)) * inv[rows, 0:1]
        acc[rows, :] = g1
        glow[rows, :] = g1.astype(bf16)
        add_row(10, gn * xh)
        add_row(8, gn)
        add_row(2, g1)
        return 0

    lax.fori_loop(0, 4, last, 0)
    l_g = [local(acc, g1_ref, ls.at[1]), local(glow, g1low_ref, ls.at[2])]
    gT[...] = glow[...].T
    for q in sends(2) + sends(3):
        q.wait()
    for t in range(4):
        dst[t // 2, t % 2, :, 0:256] = dotf(gT[...], hv[t]).astype(bf16)
    l_d = [local(dst.at[t // 2, t % 2, :, pl.ds(0, 256)], dout_ref.at[t], ls.at[3 + t]) for t in range(4)]
    for q in [l_o] + l_g + l_d:
        q.wait()


def mid(xs, cs, heads, g, vec):
    v_ = pltpu.VMEM
    dma = pltpu.SemaphoreType.DMA
    sd = jax.ShapeDtypeStruct
    wt = v_((2, 2, 4, 2, 96, 768), bf16)
    return pl.pallas_call(
        mid_kernel,
        out_shape=[sd((4, 256, 768), bf16), sd((L, 768), f32), sd((L, 768), bf16), sd((4, 768, 256), bf16), sd((2, 4, 768, 768), bf16), sd((24, 768), f32)],
        in_specs=[HBM] * 4 + [VM],
        out_specs=[HBM] * 5 + [VM],
        scratch_shapes=[
            v_((4, 256, 768), bf16), v_((4, 256, 768), bf16), v_((4, L, 256), bf16), v_((4, 4, 2, 96, 256), bf16), wt, wt,
            v_((L, 768), f32), v_((L, 128), f32), v_((L, 768), bf16), v_((4, L, 768), bf16), v_((4, L, 768), bf16), v_((L, 768), f32),
            v_((L, 768), bf16), v_((768, L), bf16), v_((768, L), bf16), v_((4, 256, 768), bf16), v_((2, 2, 768, 768), bf16),
            dma((9,)), dma((2, 2)),
        ],
        compiler_params=pltpu.CompilerParams(vmem_limit_bytes=67043328),
    )(xs, cs, heads, g, vec)


def norm_stats(r):
    center = r - jnp.mean(r, axis=-1, keepdims=True)
    inv = lax.rsqrt(jnp.mean(center * center, axis=-1, keepdims=True) + EPSILON)
    return center * inv, inv


def norm_back(cot, gain, xhat, inv):
    e = cot * gain
    grad = (e - jnp.mean(e, -1, keepdims=True) - xhat * jnp.mean(e * xhat, -1, keepdims=True)) * inv
    return grad, jnp.sum(cot * xhat, 0), jnp.sum(cot, 0)


def middle(x, cot, heads, w1, w2, w3, bias_o, bias_h, bias_d, shift1, shift2, gain1, gain2):
    ein = functools.partial(jnp.einsum, preferred_element_type=f32)
    hid = x.astype(f32)
    resid1 = hid + ein("tpw,tdw->pd", heads, w1[:, :, 512:]) + bias_o
    xhat1, inv1 = norm_stats(resid1)
    normed = xhat1 * gain1 + shift1
    low = normed.astype(bf16)
    pre = ein("pd,tdf->tpf", low, w2) + bias_h[:, None, :]
    act, gelu_back = jax.vjp(lambda v: jax.nn.gelu(v, approximate=False), pre)
    act = act.astype(bf16)
    resid2 = normed + ein("tpf,tdf->pd", act, w3) + bias_d
    xhat2, inv2 = norm_stats(resid2)
    out = (xhat2 * gain2 + shift2).astype(bf16)
    g2, dgain2, dshift2 = norm_back(cot.astype(f32), gain2, xhat2, inv2)
    g2low = g2.astype(bf16)
    d3 = ein("pd,tpf->tdf", g2low, act).astype(bf16)
    gpre = gelu_back(ein("pd,tdf->tpf", g2low, w3))[0].astype(bf16)
    d2 = ein("pd,tpf->tdf", low, gpre).astype(bf16)
    gn = g2 + ein("tpf,tdf->pd", gpre, w2)
    g1, dgain1, dshift1 = norm_back(gn, gain1, xhat1, inv1)
    g1low = g1.astype(bf16)
    dout = ein("pd,tpw->tdw", g1low, heads).astype(bf16)
    dbh = jnp.sum(gpre, 1, dtype=f32)
    return out, g1, g1low, dout, d2, d3, (dgain1, dgain2, dshift1, dshift2, jnp.sum(g1, 0), dbh, jnp.sum(g2, 0))


def on_device(hidden_in, cotangent, prefix, w_qkv, w_out, w_in, w_down, biases, gains):
    rows = w_qkv.shape[0]
    n_t = lax.axis_size("tensor")
    t_me, d_me = lax.axis_index("tensor"), lax.axis_index("dp")
    n_dev = n_t * lax.axis_size("dp")
    s = jnp.stack([jnp.concatenate([w_qkv.reshape(rows, -1), w_out.T], axis=1), w_in, w_down.T])
    vecs = jnp.concatenate([biases, gains], 0)
    width = vecs.shape[1]
    vecs = jnp.pad(vecs, ((0, 4), (0, 128 - width)))
    seqs = lambda a: jnp.transpose(a, (1, 0, 2))
    h, c = seqs(hidden_in), seqs(cotangent)
    my_prefix = lax.dynamic_slice_in_dim(prefix, t_me, 1, 0)
    if lax.axis_size("dp") == 8:
        g, xs, cs, vec, proj, projT, heads, ot, lse = front(my_prefix, s, h, c, vecs)
        out4, g1, g1low, doutw, d, v = mid(xs, cs, heads, g, vec)
        gs, vs, oo, xx = back(my_prefix, xs, g1low, g1, g, proj, projT, ot, lse, doutw, d.reshape(2, 2, 2, 4, 2, rows, 768), v, out4)
        qv = vs[16:24, :256].reshape(4, 2, 256)
        vs = jnp.concatenate([qv[:, 0, :192].reshape(1, 768), qv[:, 1, :192].reshape(1, 768), vs[2:16]])
    else:
        ein = functools.partial(jnp.einsum, preferred_element_type=f32)
        g = lax.all_gather(lax.all_gather(s, "dp", axis=1, tiled=True), "tensor", axis=1)
        x = lax.all_to_all(h, "tensor", 0, 0, tiled=True).reshape(1024, 768)
        cot = lax.all_to_all(c, "tensor", 0, 0, tiled=True).reshape(1024, 768)
        b = lax.all_gather(vecs, ("dp", "tensor"), axis=0)
        w1, w2, w3 = [a.reshape(n_t, 768, 768) for a in g]
        vec = b.reshape(n_dev, 16, 128)[:, :12, :width].transpose(1, 0, 2).reshape(12, 768)
        bqkv = jnp.pad(jnp.stack([vec[0].reshape(4, 192), jnp.zeros((4, 192), f32), vec[1].reshape(4, 192)], 1).reshape(4, 1, 576), ((0, 0), (0, 0), (0, 64)))
        proj, projT, heads, ot, lse = attn_fwd(my_prefix, x, w1, bqkv)
        out, g1, g1low, doutw, d2, d3, small = middle(
            x, cot, heads, w1, w2, w3, vec[2], vec[3:7].reshape(4, 768), vec[7], vec[8], vec[9], vec[10], vec[11]
        )
        dgain1, dgain2, dshift1, dshift2, dbo, dbh, dbd = small
        gproj = attn_bwd(my_prefix, g1low, w1, proj, projT, ot, lse)
        gp = gproj[:, :, :576]
        dqkv = ein("pd,tpc->tdc", x, gp).astype(bf16)
        x4 = (g1 + ein("tpc,tdc->pd", gp, w1[:, :, :576])).astype(bf16).reshape(4, 256, 768)
        dbq = jnp.sum(gp[:, :, :192], 1, dtype=f32).reshape(1, 768)
        dbv = jnp.sum(gp[:, :, 384:], 1, dtype=f32).reshape(1, 768)
        d = jnp.stack([jnp.concatenate([dqkv, doutw[:, :, 64:]], 2), d2, d3])
        part = lax.all_to_all(d, "tensor", 1, 1, tiled=True).astype(f32).sum(1)
        part = part.astype(bf16).reshape(3, -1, rows, 768)
        gs = lax.all_to_all(part, "dp", 1, 1, tiled=True).astype(f32).sum(1)
        vs = lax.psum(
            jnp.concatenate([dbq, dbv, dbo[None], dbh, jnp.stack([dbd, dshift1, dshift2, dgain1, dgain2]), jnp.zeros((4, 768), f32)]),
            ("dp", "tensor"),
        )
        oo = lax.all_to_all(out.reshape(4, 256, 768), "tensor", 0, 0, tiled=True)
        xx = lax.all_to_all(x4, "tensor", 0, 0, tiled=True)
    mine = lax.dynamic_slice_in_dim(vs, (d_me * n_t + t_me) * width, width, 1)
    return (
        seqs(oo),
        seqs(xx),
        gs[0, :, :576].reshape(rows, 3, 192),
        gs[0, :, 576:].T,
        gs[1],
        gs[2].T,
        mine[:10],
        mine[10:12],
    )


def solution(mesh):
    placed = (
        P("tensor", "dp", None),
        P("tensor", "dp", None),
        P("dp"),
        P("dp", None, "tensor"),
        P("tensor", "dp"),
        P("dp", "tensor"),
        P("tensor", "dp"),
        P(None, ("dp", "tensor")),
        P(None, ("dp", "tensor")),
    )
    return jax.shard_map(on_device, mesh=mesh, in_specs=placed, out_specs=placed[:2] + placed[3:], check_vma=False)
```

```python
import functools
import math

import jax
import jax.numpy as jnp
from jax import lax
from jax.experimental import pallas as pl
from jax.experimental.pallas import tpu as pltpu
from jax.sharding import PartitionSpec as P

f32=jnp.float32; bf16=jnp.bfloat16
L=1024; QB=256; NK=(512,512,768,1024)
C2=0.125*math.log2(math.e)
NEG=-1e30
def dotf(a,b): return jnp.dot(a,b,preferred_element_type=f32)
def dot_nt(a,b): return lax.dot_general(a,b,(((1,),(1,)),((),())),preferred_element_type=f32)
def masks(mask_ref, prefix):
    k=lax.broadcasted_iota(jnp.int32,(256,256),0); q=lax.broadcasted_iota(jnp.int32,(256,256),1)
    diag=k<=q
    mask_ref[0]=jnp.where(diag|(k<prefix),0.0,NEG)
    mask_ref[1]=jnp.where(k+256<prefix,0.0,NEG)+jnp.zeros((256,256),f32)
    mask_ref[2]=jnp.where(diag|(k+256<prefix),0.0,NEG)
    mask_ref[3]=jnp.where(diag,0.0,NEG)
MASKMAP={0:{0:0,1:1},1:{1:2},2:{2:3},3:{3:3}}
def masked(st,qb,mask_ref):
    parts=[]
    for kb in range(NK[qb]//256):
        p=st[kb*256:(kb+1)*256]
        mi=MASKMAP[qb].get(kb)
        parts.append(p if mi is None else p+mask_ref[mi])
    return jnp.concatenate(parts,0)
def fwd_kernel(prefix_ref,x_ref,w_ref,b_ref,proj_ref,projT_ref,heads_ref,ot_ref,lse_ref,zq_ref,mask_ref):
    masks(mask_ref,prefix_ref[0])
    proj=(dotf(x_ref[...],w_ref[:,:640])+b_ref[...]).astype(bf16)
    proj_ref[...]=proj
    projT_ref[...]=proj.T
    zq_ref[...]=jnp.zeros_like(zq_ref)
    for h in range(3):
        zq_ref[h,64+64*h:128+64*h,:]=projT_ref[64*h:64*h+64,:]
    ot_ref[...]=jnp.zeros_like(ot_ref)
    for h in range(3):
        for qb in range(4):
            nk=NK[qb]; qs=slice(qb*QB,qb*QB+QB)
            st=dotf(proj_ref[:nk,128:384],zq_ref[h,:,qs])
            st=masked(st,qb,mask_ref)
            m=jnp.max(st,axis=0,keepdims=True)
            p=jnp.exp2((st-m)*C2)
            l=jnp.sum(p,axis=0,keepdims=True)
            ot=dotf(projT_ref[384+64*h:448+64*h,:nk],p.astype(bf16))
            ot_ref[64+64*h:128+64*h,qs]=(ot/l).astype(bf16)
            lse_ref[h:h+1,qs]=m*C2+jnp.log2(l)
    heads_ref[...]=ot_ref[...].T
def attn_fwd(prefix,x,w1,bqkv):
    sq=pl.squeezed
    return pl.pallas_call(fwd_kernel,grid_spec=pltpu.PrefetchScalarGridSpec(num_scalar_prefetch=1,grid=(4,),
      in_specs=[pl.BlockSpec((L,768),lambda t,p:(0,0)),pl.BlockSpec((sq,768,768),lambda t,p:(t,0,0)),pl.BlockSpec((sq,1,640),lambda t,p:(t,0,0))],
      out_specs=[pl.BlockSpec((sq,L,640),lambda t,p:(t,0,0)),pl.BlockSpec((sq,640,L),lambda t,p:(t,0,0)),pl.BlockSpec((sq,L,256),lambda t,p:(t,0,0)),pl.BlockSpec((sq,256,L),lambda t,p:(t,0,0)),pl.BlockSpec((sq,8,L),lambda t,p:(t,0,0))],
      scratch_shapes=[pltpu.VMEM((3,256,L),bf16),pltpu.VMEM((4,256,256),f32)]),
      out_shape=[jax.ShapeDtypeStruct((4,L,640),bf16),jax.ShapeDtypeStruct((4,640,L),bf16),jax.ShapeDtypeStruct((4,L,256),bf16),jax.ShapeDtypeStruct((4,256,L),bf16),jax.ShapeDtypeStruct((4,8,L),f32)],
      compiler_params=pltpu.CompilerParams(vmem_limit_bytes=62<<20))(prefix,x,w1,bqkv)
def bwd_kernel(prefix_ref,g_ref,w_ref,proj_ref,projT_ref,ot_ref,lse_ref,gproj_ref,
               zq_ref,zdo_ref,qm_ref,dom_ref,pt_ref,ds_ref,mask_ref,gt_ref,dqt_ref):
    masks(mask_ref,prefix_ref[0])
    gh=dotf(g_ref[...],w_ref[:,512:768]).astype(bf16)
    gt_ref[...]=gh.T
    zq_ref[...]=jnp.zeros_like(zq_ref); zdo_ref[...]=jnp.zeros_like(zdo_ref)
    lane=lax.broadcasted_iota(jnp.int32,(1,256),1)
    for h in range(3):
        zq_ref[h,64+64*h:128+64*h,:]=projT_ref[64*h:64*h+64,:]
        zdo_ref[h,64*h:64*h+64,:]=gt_ref[64+64*h:128+64*h,:]*0.125
        sel=(lane>=64*h)&(lane<64*h+64)
        qm_ref[h]=jnp.where(sel,proj_ref[:,0:256],0)
        sel2=(lane>=64*h+64)&(lane<64*h+128)
        dom_ref[h]=jnp.where(sel2,gh,0)
    for h in range(3):
        d=jnp.sum(gt_ref[64+64*h:128+64*h,:].astype(f32)*ot_ref[64+64*h:128+64*h,:].astype(f32),axis=0,keepdims=True)*0.125
        for qb in range(4):
            nk=NK[qb]; qs=slice(qb*QB,qb*QB+QB)
            st=dotf(proj_ref[:nk,128:384],zq_ref[h,:,qs])
            st=masked(st,qb,mask_ref)
            p=jnp.exp2(st*C2-lse_ref[h:h+1,qs])
            dp=dotf(proj_ref[:nk,384:640],zdo_ref[h,:,qs])
            ds=(p*(dp-d[:,qs])).astype(bf16)
            pt_ref[h,:nk,qs]=p.astype(bf16)
            ds_ref[h,:nk,qs]=ds
            dqt_ref[64*h:64*h+64,qs]=dotf(projT_ref[192+64*h:256+64*h,:nk],ds).astype(bf16)
    gproj_ref[:,0:192]=dqt_ref[...].T
    for (k0,k1,q0) in ((0,512,0),(512,768,512),(768,1024,768)):
        dk=jnp.zeros((k1-k0,256),f32); dv=jnp.zeros((k1-k0,256),f32)
        for h in range(3):
            dk=dk+dotf(ds_ref[h,k0:k1,q0:],qm_ref[h,q0:,:])
            dv=dv+dotf(pt_ref[h,k0:k1,q0:],dom_ref[h,q0:,:])
        gproj_ref[k0:k1,192:384]=dk[:,0:192].astype(bf16)
        gproj_ref[k0:k1,384:576]=dv[:,64:256].astype(bf16)
    gproj_ref[:,576:640]=jnp.zeros((L,64),bf16)
def attn_bwd(prefix,g,w1,proj,projT,ot,lse):
    sq=pl.squeezed
    sp=lambda *s: pl.BlockSpec((sq,)+s,lambda t,p:(t,0,0))
    return pl.pallas_call(functools.partial(bwd_kernel),grid_spec=pltpu.PrefetchScalarGridSpec(num_scalar_prefetch=1,grid=(4,),
      in_specs=[pl.BlockSpec((L,768),lambda t,p:(0,0)),sp(768,768),sp(L,640),sp(640,L),sp(256,L),sp(8,L)],
      out_specs=sp(L,640),
      scratch_shapes=[pltpu.VMEM((3,256,L),bf16),pltpu.VMEM((3,256,L),bf16),pltpu.VMEM((3,L,256),bf16),pltpu.VMEM((3,L,256),bf16),pltpu.VMEM((3,L,L),bf16),pltpu.VMEM((3,L,L),bf16),pltpu.VMEM((4,256,256),f32),pltpu.VMEM((256,L),bf16),pltpu.VMEM((192,L),bf16)]),
      out_shape=jax.ShapeDtypeStruct((4,L,640),bf16),
      compiler_params=pltpu.CompilerParams(vmem_limit_bytes=62<<20))(prefix,g,w1,proj,projT,ot,lse)
MESH=pl.DeviceIdType.MESH
class Place:
    def __init__(self):
        dp=lax.axis_index("dp"); t=lax.axis_index("tensor")
        self.dp,self.t=dp,t
        self.z,self.x,self.y,self.c=dp//2,dp%2,t//2,t%2
    def peer(self,dim,j=1):
        return {'x':lambda:(self.dp^1,self.t),'z':lambda:(self.dp^(2*j),self.t),'y':lambda:(self.dp,self.t^2),'c':lambda:(self.dp,self.t^1)}[dim]()
    def peers_all(self):
        return [self.peer('x'),self.peer('y'),self.peer('c'),self.peer('z',1),self.peer('z',2),self.peer('z',3),(self.dp,self.t^3)]
def barrier(peers):
    b=pltpu.get_barrier_semaphore()
    for p in peers: pl.semaphore_signal(b,inc=1,device_id=p,device_id_type=MESH)
    pl.semaphore_wait(b,len(peers))
class Sems:
    def __init__(self,send,recv): self.s,self.r,self.n=send,recv,0
    def take(self):
        i=self.n; self.n+=1
        return self.s.at[i],self.r.at[i]
def rcopy(src,dst,sems,dev):
    a,b=sems.take()
    return pltpu.make_async_remote_copy(src_ref=src,dst_ref=dst,send_sem=a,recv_sem=b,device_id=dev,device_id_type=MESH)
def local(src,dst,sem):
    k=pltpu.make_async_copy(src,dst,sem); k.start(); return k
def exchange(pc,src,dst,sems):
    out=[]
    for j in (2,3,1):
        p=(pc.dp,pc.t^j)
        k=rcopy(src.at[pc.t^j],dst.at[pc.t],sems,p); k.start(); out.append(k)
    return out
HBM=pl.BlockSpec(memory_space=pltpu.HBM); VM=pl.BlockSpec(memory_space=pltpu.VMEM)
def point(steps, k, h):
    for kk in range(4):
        todo = steps.get((kk, h))
        if todo:
            @pl.when(k == kk)
            def _(todo=todo):
                for step in todo:
                    step()


def add_into(dst, src, n, pick_dst, pick_src):
    def body(j, _):
        a, b = pick_dst(j), pick_src(j)
        dst[a] = (dst[a].astype(f32) + src[b].astype(f32)).astype(bf16)
        return 0
    lax.fori_loop(0, n, body, 0)


class Reduce:
    def __init__(self, pc, d_ref, half, lc, rc, r1, r2, r3, sems, lsem):
        self.pc, self.lc, self.rc, self.r1, self.r2, self.r3 = pc, lc, rc, r1, r2, r3
        rows = pl.ds(48 * half, 48)
        self.own = pltpu.make_async_copy(d_ref.at[:, pc.c, :, :, rows], lc, lsem)
        self.q0 = rcopy(d_ref.at[:, 1 - pc.c, :, :, rows], rc, sems, pc.peer("c"))
        self.q1 = rcopy(lc.at[:, :, 1 - pc.x], r1, sems, pc.peer("x"))
        self.q2 = [rcopy(lc.at[:, pc.z ^ j, pc.x], r2.at[j - 1], sems, pc.peer("z", j)) for j in (3, 2, 1)]
        self.q3 = rcopy(lc.at[1 - pc.y, pc.z, pc.x], r3, sems, pc.peer("y"))

    def s0(self):
        self.own.start()
        self.q0.start()

    def s1(self):
        self.own.wait()
        self.q0.wait_recv()
        at = lambda j: (j // 8, (j // 2) % 4, j % 2)
        add_into(self.lc, self.rc, 16, at, at)
        self.q1.start()

    def s2(self):
        self.q1.wait_recv()
        add_into(self.lc, self.r1, 8, lambda j: (j // 4, j % 4, self.pc.x), lambda j: (j // 4, j % 4))
        for q in self.q2:
            q.start()

    def s3(self):
        pc = self.pc
        for q in self.q2:
            q.wait_recv()
        for y in range(2):
            at = (y, pc.z, pc.x)
            total = (self.lc[at].astype(f32) + self.r2[0, y].astype(f32)) + (self.r2[1, y].astype(f32) + self.r2[2, y].astype(f32))
            self.lc[at] = total.astype(bf16)
        self.q3.start()

    def s4(self, out_ref, rows):
        pc = self.pc
        self.q3.wait_recv()
        out_ref[rows] = self.lc[pc.y, pc.z, pc.x].astype(f32) + self.r3[...].astype(f32)

    def end(self):
        for q in [self.q0, self.q1, self.q3] + self.q2:
            q.wait_send()


N_C = 4 * 6 + 1 + 1 + 1 + 2 + 6 + 6 + 6


def back_kernel(
    prefix_ref, x_ref, g_ref, gf_ref, w_ref, proj_ref, projT_ref, ot_ref, lse_ref, dout_ref, d_ref, v_ref, out_ref,
    gs_ref, vs_ref, oo_ref, xo_ref,
    xT, gl, dxa, w_b, proj_b, projT_b, ot_b, lse_b, dout_b,
    zq, zdo, qm, dom, pt, ds, mask_ref, gt, dqt, dkb, dvb, gproj,
    lc, rc, r1, r2, r3, dwb, cr, yr, xr, zr, vb, vr, xst, ss, rs, ls, ins,
):
    pc = Place()
    sems = Sems(ss, rs)
    w1 = w_ref.at[0]
    lane = lax.broadcasted_iota(jnp.int32, (1, 256), 1)

    def loads(k, slot):
        t = pc.t ^ (3 - k)
        pairs = [
            (w1.at[t // 2, t % 2], w_b), (proj_ref.at[t], proj_b), (projT_ref.at[t], projT_b),
            (ot_ref.at[t], ot_b), (lse_ref.at[t], lse_b), (dout_ref.at[t], dout_b),
        ]
        return [pltpu.make_async_copy(a, b.at[slot], ins.at[slot, n]) for n, (a, b) in enumerate(pairs)]

    first = loads(0, 0)
    for q in first:
        q.start()
    l_x = local(x_ref, xst, ls.at[4])
    l_g = local(g_ref, gl, ls.at[5])
    l_f = local(gf_ref, dxa, ls.at[6])
    barrier(pc.peers_all())
    red = {}
    for n, (g, i) in enumerate(((1, 0), (1, 1), (0, 0), (0, 1))):
        red[n] = Reduce(pc, d_ref.at[g], i, lc.at[n], rc.at[n], r1.at[n], r2.at[n], r3.at[n], sems, ls.at[n])
        red[n].s0()
    ox = exchange(pc, out_ref, oo_ref, sems)
    l_o = [local(out_ref.at[pc.t], oo_ref.at[pc.t], ls.at[7])]
    q_c0 = rcopy(dwb.at[0], cr.at[0], sems, pc.peer("c"))
    q_y = rcopy(dwb.at[1], yr, sems, pc.peer("y"))
    q_c1 = rcopy(dwb.at[2], cr.at[1], sems, pc.peer("c"))
    half = [pl.ds(48 * i, 48) for i in range(2)]
    q_x = [rcopy(dwb.at[3, :, 1 - pc.x, half[i]], xr.at[i], sems, pc.peer("x")) for i in range(2)]
    q_z = [[rcopy(dwb.at[3, pc.z ^ j, pc.x, half[i]], zr.at[i, j - 1], sems, pc.peer("z", j)) for j in (3, 2, 1)] for i in range(2)]
    steps = {
        (0, 1): [red[0].s1], (0, 2): [red[1].s1], (0, 3): [red[2].s1], (1, 1): [red[3].s1],
        (1, 3): [red[0].s2], (2, 3): [red[1].s2], (3, 0): [red[0].s3], (3, 3): [red[2].s2],
    }
    masks(mask_ref, prefix_ref[0])
    zq[...] = jnp.zeros_like(zq)
    zdo[...] = jnp.zeros_like(zdo)
    gproj[:, 576:640] = jnp.zeros((L, 64), bf16)
    vb[0] = v_ref[...]
    l_x.wait()
    xT[...] = xst[...].reshape(L, 768).T
    l_g.wait()
    l_f.wait()

    def group(k, _):
        slot = k % 2
        for q in loads(k, slot):
            q.wait()

        @pl.when(k < 3)
        def _():
            for q in loads(k + 1, 1 - slot):
                q.start()

        t = pc.t ^ (3 - k)
        w, pj, pjT, o_t, lse = w_b.at[slot], proj_b.at[slot], projT_b.at[slot], ot_b.at[slot], lse_b.at[slot]
        gh = dotf(gl[...], w[...].reshape(768, 768)[:, 512:768]).astype(bf16)
        gt[...] = gh.T
        for h in range(3):
            point(steps, k, h)
            own = slice(64 + 64 * h, 128 + 64 * h)
            zq[h, own, :] = pjT[64 * h : 64 * h + 64, :]
            zdo[h, 64 * h : 64 * h + 64, :] = gt[own, :] * 0.125
            qm[...] = jnp.where((lane >= 64 * h) & (lane < 64 * h + 64), pj[:, 0:256], 0)
            dom[...] = jnp.where((lane >= 64 * h + 64) & (lane < 64 * h + 128), gh, 0)
            d = jnp.sum(gt[own, :].astype(f32) * o_t[own, :].astype(f32), axis=0, keepdims=True) * 0.125
            for qb in range(4):
                nk = NK[qb]
                qs = slice(qb * QB, qb * QB + QB)
                st = masked(dotf(pj[:nk, 128:384], zq[h, :, qs]), qb, mask_ref)
                p = jnp.exp2(st * C2 - lse[h : h + 1, qs])
                dp = dotf(pj[:nk, 384:640], zdo[h, :, qs])
                dsv = (p * (dp - d[:, qs])).astype(bf16)
                pt[:nk, qs] = p.astype(bf16)
                ds[:nk, qs] = dsv
                dqt[64 * h : 64 * h + 64, qs] = dotf(pjT[192 + 64 * h : 256 + 64 * h, :nk], dsv).astype(bf16)
            for k0, k1, q0 in ((0, 512, 0), (512, 768, 512), (768, 1024, 768)):
                dk = dotf(ds[k0:k1, q0:], qm[q0:, :]).astype(bf16)
                dv = dotf(pt[k0:k1, q0:], dom[q0:, :]).astype(bf16)
                dkb[k0:k1] = dk if h == 0 else dkb[k0:k1] + dk
                dvb[k0:k1] = dv if h == 0 else dvb[k0:k1] + dv
        point(steps, k, 3)
        gproj[:, 0:192] = dqt[...].T
        gproj[:, 192:384] = dkb[:, 0:192]
        gproj[:, 384:576] = dvb[:, 64:256]
        vb[0, pl.ds(16 + 2 * t, 1), 0:256] = jnp.sum(gproj[:, 0:256].astype(f32), axis=0, keepdims=True)
        vb[0, pl.ds(17 + 2 * t, 1), 0:256] = jnp.sum(gproj[:, 384:640].astype(f32), axis=0, keepdims=True)
        dw = dotf(xT[...], gproj[...])
        do = dout_b[slot].astype(f32)
        shape = lambda a: a.astype(bf16).reshape(4, 2, 96, a.shape[1])
        dwb[k, :, :, :, 0:512] = shape(dw[:, 0:512])
        dwb[k, :, :, :, 512:640] = shape(dw[:, 512:640] + do[:, 0:128])
        dwb[k, :, :, :, 640:768] = shape(do[:, 128:256])

        @pl.when(k == 0)
        def _():
            q_c0.start()

        @pl.when(k == 1)
        def _():
            q_c0.wait_recv()
            add_into(dwb.at[1], cr.at[0], 8, lambda j: (j // 2, j % 2), lambda j: (j // 2, j % 2))
            q_y.start()

        @pl.when(k == 2)
        def _():
            q_c1.start()

        @pl.when(k == 3)
        def _():
            q_c1.wait_recv()
            add_into(dwb.at[3], cr.at[1], 8, lambda j: (j // 2, j % 2), lambda j: (j // 2, j % 2))
            q_y.wait_recv()
            add_into(dwb.at[3], yr, 8, lambda j: (j // 2, j % 2), lambda j: (j // 2, j % 2))
            for q in q_x:
                q.start()

        dxa[...] += dot_nt(gproj[...], w[...].reshape(768, 768)[:, 0:640])
        return 0

    lax.fori_loop(0, 4, group, 0)
    xst[...] = dxa[...].astype(bf16).reshape(4, 256, 768)
    v_q = [rcopy(vb.at[0], vr.at[0], sems, pc.peer("c"))]
    v_q[0].start()
    xx = exchange(pc, xst, xo_ref, sems)
    l_o.append(local(xst.at[pc.t], xo_ref.at[pc.t], ls.at[8]))

    def vstep(n, dim):
        v_q[n].wait_recv()
        vb[n + 1] = vb[n] + vr[n]
        v_q.append(rcopy(vb.at[n + 1], vr.at[n + 1], sems, pc.peer(dim)))
        v_q[n + 1].start()

    vstep(0, "x")
    red[1].s3()
    for i in range(2):
        q_x[i].wait_recv()
        for z in range(4):
            dwb[3, z, pc.x, half[i]] = (dwb[3, z, pc.x, half[i]].astype(f32) + xr[i, z].astype(f32)).astype(bf16)
        for q in q_z[i]:
            q.start()
    vstep(1, "y")
    red[3].s2()
    red[2].s3()
    v_q[2].wait_recv()
    vb[3] = vb[2] + vr[2]
    v_z = [rcopy(vb.at[3], vr.at[2 + j], sems, pc.peer("z", j)) for j in (3, 2, 1)]
    for q in v_z:
        q.start()
    red[0].s4(gs_ref.at[2], slice(0, 48))
    red[1].s4(gs_ref.at[2], slice(48, 96))
    red[3].s3()
    for i in range(2):
        for q in q_z[i]:
            q.wait_recv()
        gs_ref[0, 48 * i : 48 * i + 48] = (dwb[3, pc.z, pc.x, half[i]].astype(f32) + zr[i, 0].astype(f32)) + (zr[i, 1].astype(f32) + zr[i, 2].astype(f32))
    red[2].s4(gs_ref.at[1], slice(0, 48))
    for q in v_z:
        q.wait_recv()
    vs_ref[...] = (vb[3] + vr[3]) + (vr[4] + vr[5])
    red[3].s4(gs_ref.at[1], slice(48, 96))
    for q in l_o:
        q.wait()
    for q in ox + xx:
        q.wait()
    for n in range(4):
        red[n].end()
    for q in [q_c0, q_y, q_c1] + q_x + q_z[0] + q_z[1] + v_q + v_z:
        q.wait_send()


def back(prefix, x, g1low, g1, g, proj, projT, ot, lse, doutw, d, v, out4):
    v_ = pltpu.VMEM
    dma = pltpu.SemaphoreType.DMA
    sd = jax.ShapeDtypeStruct
    return pl.pallas_call(
        back_kernel,
        out_shape=[sd((3, 96, 768), f32), sd((24, 768), f32), sd((4, 256, 768), bf16), sd((4, 256, 768), bf16)],
        in_specs=[pl.BlockSpec(memory_space=pltpu.SMEM)] + [HBM] * 10 + [VM, HBM],
        out_specs=[VM, VM, HBM, HBM],
        scratch_shapes=[
            v_((768, L), bf16), v_((L, 768), bf16), v_((L, 768), f32),
            v_((2, 4, 2, 96, 768), bf16), v_((2, L, 640), bf16), v_((2, 640, L), bf16), v_((2, 256, L), bf16), v_((2, 8, L), f32), v_((2, 768, 256), bf16),
            v_((3, 256, L), bf16), v_((3, 256, L), bf16), v_((L, 256), bf16), v_((L, 256), bf16), v_((L, L), bf16), v_((L, L), bf16),
            v_((4, 256, 256), f32), v_((256, L), bf16), v_((192, L), bf16), v_((L, 256), bf16), v_((L, 256), bf16), v_((L, 640), bf16),
            v_((4, 2, 4, 2, 48, 768), bf16), v_((4, 2, 4, 2, 48, 768), bf16), v_((4, 2, 4, 48, 768), bf16), v_((4, 3, 2, 48, 768), bf16), v_((4, 48, 768), bf16),
            v_((4, 4, 2, 96, 768), bf16), v_((2, 4, 2, 96, 768), bf16), v_((4, 2, 96, 768), bf16), v_((2, 4, 48, 768), bf16), v_((2, 3, 48, 768), bf16),
            v_((4, 24, 768), f32), v_((6, 24, 768), f32), v_((4, 256, 768), bf16),
            dma((N_C,)), dma((N_C,)), dma((9,)), dma((2, 6)),
        ],
        compiler_params=pltpu.CompilerParams(collective_id=1, has_side_effects=True, vmem_limit_bytes=67043328),
    )(prefix, x, g1low, g1, g, proj, projT, ot, lse, doutw, d, v, out4)


class Gather:
    def __init__(self, pc, src, dst, rows, order, sems):
        self.pc, self.src, self.dst, self.rows, self.order, self.sems = pc, src, dst, rows, order, sems
        self.full, self.sent, self.core = set(), [], []
        self.plan()

    def at(self, over, full):
        pc = self.pc
        ix = {d: over.get(d, slice(None) if d in full else getattr(pc, d)) for d in "yzx"}
        return self.dst.at[(ix["y"], pc.c, ix["z"], ix["x"]) + ((pl.ds(*self.rows),) if self.rows else ())]

    def plan(self):
        pc = self.pc
        src = self.src.at[pl.ds(*self.rows)] if self.rows else self.src
        mine = self.at({}, set())
        self.core.append(rcopy(src, mine, self.sems, pc.peer("c")))
        self.phases = []
        full = set()
        for d in self.order:
            ks = []
            for j in (1, 2, 3) if d == "z" else (1,):
                here = self.at({}, full)
                ks.append(rcopy(here if full else src, here, self.sems, pc.peer(d, j)))
                there = self.at({d: getattr(pc, d) ^ j}, full)
                self.core.append(rcopy(there, there, self.sems, pc.peer("c")))
            self.phases.append(ks)
            full = full | {d}
        self.first = [1]
        for ks in self.phases:
            self.first.append(self.first[-1] + len(ks))

    def start(self):
        self.core[0].start()
        for k in self.phases[0]:
            k.start()

    def arrive(self, p):
        for n, k in enumerate(self.phases[p]):
            k.wait_recv()
            self.core[self.first[p] + n].start()

    def next(self, p):
        self.arrive(p - 1)
        for k in self.phases[p]:
            k.start()

    def from_core(self, a, b):
        for k in self.core[a:b]:
            k.wait_recv()

    def end(self):
        for k in self.core + sum(self.phases, []):
            k.wait_send()


class Slabs:
    def __init__(self, pc, src, dst, kind, rows, sems):
        src = src.at[rows]
        at = lambda y, z, x: dst.at[y, pc.c, z, x, rows]
        every = slice(None)
        mine, other = pc.y, 1 - pc.y
        self.copy, self.fwd = {}, {}

        def add(name, dim, pairs, got):
            self.copy[name] = [rcopy(a, b, sems, pc.peer(dim, j)) for j, a, b in pairs]
            if got is not None:
                self.fwd[name] = rcopy(got, got, sems, pc.peer("c"))

        slab = at(mine, every, pc.x)
        add("z", "z", [(j, src, at(mine, pc.z, pc.x)) for j in (3, 2, 1)], slab)
        add("x", "x", [(1, slab, slab)], at(mine, every, 1 - pc.x))
        if kind == "A":
            whole = at(mine, every, every)
            add("y", "y", [(1, whole, whole)], at(other, every, every))
        else:
            add("y", "y", [(1, src, at(mine, pc.z, pc.x))], None)
            one, slab2 = at(other, pc.z, pc.x), at(other, every, pc.x)
            add("z2", "z", [(j, one, one) for j in (3, 2, 1)], slab2)
            add("x2", "x", [(1, slab2, slab2)], at(other, every, 1 - pc.x))

    def start(self, name):
        for k in self.copy[name]:
            k.start()

    def arrive(self, name):
        for k in self.copy[name]:
            k.wait_recv()
        if name in self.fwd:
            self.fwd[name].start()

    def from_core(self, *names):
        for n in names:
            self.fwd[n].wait_recv()

    def end(self):
        for ks in self.copy.values():
            for k in ks:
                k.wait_send()
        for k in self.fwd.values():
            k.wait_send()


N_A = 3 * 8 + 3 * 13 + 11 + 3


def front_kernel(
    prefix_ref, s_ref, h_ref, b_ref,
    g_ref, x_ref, vec_ref, proj_ref, projT_ref, heads_ref, ot_ref, lse_ref,
    bv, sv, xv, wv, proj_b, projT_b, heads_b, ot_b, lse_b, zq, mask_ref, ss, rs, ls, os_,
):
    pc = Place()
    sems = Sems(ss, rs)
    own = (pc.y, pc.c, pc.z, pc.x)
    l_s = local(s_ref, sv, ls.at[0])
    l_h = local(h_ref.at[pc.t], xv.at[pc.t], ls.at[1])
    l_b = local(b_ref, bv.at[own], ls.at[9])
    barrier(pc.peers_all())
    bias = Gather(pc, b_ref, bv, None, "zxy", sems)
    w1a, w1b, w2a, w2b, w3a, w3b = every = [
        Slabs(pc, s_ref.at[n // 2], g_ref.at[n // 2], kind, pl.ds(48 * (n % 2), 48), sems) for n, kind in enumerate("ABAABB")
    ]
    bias.start()
    w1b.start("y")
    w1a.start("z")
    w1b.start("z")
    hx = exchange(pc, h_ref, xv, sems)
    w3a.start("y")
    w3b.start("y")
    l_s.wait()
    l_g = [local(sv.at[g], g_ref.at[g].at[own], ls.at[3 + g]) for g in range(3)]
    masks(mask_ref, prefix_ref[0])
    zq[...] = jnp.zeros_like(zq)
    ot_b[...] = jnp.zeros_like(ot_b)
    for q in l_g:
        q.wait()
    l_b.wait()
    w1b.arrive("y")
    w1b.start("z2")
    for g in (w2a, w2b, w3a):
        g.start("z")
    bias.next(1)
    w1a.arrive("z")
    w1a.start("x")
    bias.next(2)
    w1b.arrive("z")
    w1b.start("x")
    w1a.arrive("x")
    w1a.start("y")
    w1b.arrive("z2")
    w1b.start("x2")
    w1b.arrive("x")
    bias.arrive(2)
    bias.from_core(0, len(bias.core))
    l_h.wait()
    for q in hx:
        q.wait_recv()
    l_x = local(xv, x_ref, ls.at[7])

    def load(k, slot):
        t = pc.t ^ k
        return pltpu.make_async_copy(g_ref.at[0, t // 2, t % 2], wv.at[slot], ls.at[8])

    def go(g, got, then=None, then_g=None):
        def step():
            g.arrive(got)
            if then:
                (then_g or g).start(then)
        return step

    steps = {
        (0, 0): [go(w3a, "y", "z2"), lambda: w3b.start("z"), go(w3b, "y", "z2")],
        (0, 2): [go(w2a, "z", "x"), lambda: w1a.from_core("z", "x"), lambda: w1b.from_core("z", "x"), lambda: load(1, 1).start()],
        (0, 3): [go(w1b, "x2")],
        (1, 1): [go(w2b, "z", "x")],
        (1, 2): [go(w2a, "x", "y")],
        (1, 3): [go(w1a, "y"), lambda: load(2, 0).start()],
        (2, 1): [go(w3a, "z", "x"), go(w2b, "x", "y")],
        (2, 2): [lambda: w1a.from_core("y"), lambda: w1b.from_core("z2", "x2"), lambda: load(3, 1).start()],
        (3, 0): [go(w3a, "z2", "x2")],
        (3, 1): [go(w3a, "x"), go(w2a, "y")],
        (3, 3): [go(w3b, "z", "x")],
    }
    load(0, 0).start()

    def outs(k, slot):
        t = pc.t ^ k
        pairs = [(proj_b, proj_ref), (projT_b, projT_ref), (heads_b, heads_ref), (ot_b, ot_ref), (lse_b, lse_ref)]
        return [pltpu.make_async_copy(a.at[slot], b.at[t], os_.at[slot, n]) for n, (a, b) in enumerate(pairs)]

    def group(k, _):
        slot = k % 2
        t = pc.t ^ k
        load(k, slot).wait()

        @pl.when(k >= 2)
        def _():
            for q in outs(k - 2, slot):
                q.wait()

        row = jnp.zeros((8, 256), f32)
        for i in range(8):
            piece = bv[(i // 2) % 2, i % 2, t, i // 4, 0:8, :]
            row = row + pltpu.roll(jnp.concatenate([piece, jnp.zeros((8, 128), f32)], 1), 24 * i, 1)
        brow = jnp.concatenate([row[0:1], jnp.zeros((1, 128), f32), row[1:2]], 1)
        pj, pjT, ot, lse = proj_b.at[slot], projT_b.at[slot], ot_b.at[slot], lse_b.at[slot]
        proj = (dotf(xv[...].reshape(L, 768), wv[slot].reshape(768, 768)[:, :640]) + brow).astype(bf16)
        pj[...] = proj
        pjT[...] = proj.T
        for h in range(3):
            point(steps, k, h)
            zq[h, 64 + 64 * h : 128 + 64 * h, :] = pjT[64 * h : 64 * h + 64, :]
            for qb in range(4):
                nk = NK[qb]
                qs = slice(qb * QB, qb * QB + QB)
                st = masked(dotf(pj[:nk, 128:384], zq[h, :, qs]), qb, mask_ref)
                m = jnp.max(st, axis=0, keepdims=True)
                p = jnp.exp2((st - m) * C2)
                l = jnp.sum(p, axis=0, keepdims=True)
                o = dotf(pjT[384 + 64 * h : 448 + 64 * h, :nk], p.astype(bf16))
                ot[64 + 64 * h : 128 + 64 * h, qs] = (o / l).astype(bf16)
                lse[h : h + 1, qs] = m * C2 + jnp.log2(l)
        point(steps, k, 3)
        heads_b[slot] = ot[...].T
        for q in outs(k, slot):
            q.start()
        return 0

    lax.fori_loop(0, 4, group, 0)
    w3a.arrive("x2")
    w3b.arrive("z2")
    w3b.start("x2")
    tiles = [jnp.zeros((16, 128), f32) for _ in range(6)]
    lane = lax.broadcasted_iota(jnp.int32, (1, 128), 1)
    for i in range(32):
        z, x, y, c = i // 8, (i // 4) % 2, (i // 2) % 2, i % 2
        j, r = (24 * i) // 128, (24 * i) % 128
        piece = pltpu.roll(bv[y, c, z, x], r, 1) if r else bv[y, c, z, x]
        tiles[j] = tiles[j] + (jnp.where(lane >= r, piece, 0.0) if r > 104 else piece)
        if r > 104:
            tiles[j + 1] = tiles[j + 1] + jnp.where(lane < r, piece, 0.0)
    for j in range(6):
        vec_ref[:, 128 * j : 128 * j + 128] = tiles[j]
    w2b.arrive("y")
    w3b.arrive("x")
    w3b.arrive("x2")
    for g in (w2a, w2b):
        g.from_core("z", "x", "y")
    for g in (w3a, w3b):
        g.from_core("z", "x", "z2", "x2")
    for q in hx:
        q.wait_send()
    l_x.wait()
    for k in (2, 3):
        for q in outs(k, k % 2):
            q.wait()
    bias.end()
    for g in every:
        g.end()


def front(prefix, s, h, b):
    v_ = pltpu.VMEM
    dma = pltpu.SemaphoreType.DMA
    sd = jax.ShapeDtypeStruct
    return pl.pallas_call(
        front_kernel,
        out_shape=[
            sd((3, 2, 2, 4, 2, 96, 768), bf16), sd((4, 256, 768), bf16), sd((16, 768), f32),
            sd((4, L, 640), bf16), sd((4, 640, L), bf16), sd((4, L, 256), bf16), sd((4, 256, L), bf16), sd((4, 8, L), f32),
        ],
        in_specs=[pl.BlockSpec(memory_space=pltpu.SMEM)] + [HBM] * 2 + [VM],
        out_specs=[HBM] * 2 + [VM] + [HBM] * 5,
        scratch_shapes=[
            v_((2, 2, 4, 2, 16, 128), f32), v_((3, 96, 768), bf16), v_((4, 256, 768), bf16), v_((2, 4, 2, 96, 768), bf16),
            v_((2, L, 640), bf16), v_((2, 640, L), bf16), v_((2, L, 256), bf16), v_((2, 256, L), bf16), v_((2, 8, L), f32),
            v_((3, 256, L), bf16), v_((4, 256, 256), f32),
            dma((N_A,)), dma((N_A,)), dma((10,)), dma((2, 5)),
        ],
        compiler_params=pltpu.CompilerParams(collective_id=0, has_side_effects=True, vmem_limit_bytes=67043328),
    )(prefix, s, h, b)


EPSILON = 1e-12


def gelu_pair(v):
    cdf = 0.5 + 0.5 * lax.erf(v * math.sqrt(0.5))
    pdf = jnp.exp2(v * v * (-0.5 * math.log2(math.e))) * (1.0 / math.sqrt(2.0 * math.pi))
    return v * cdf, cdf + v * pdf


def row_mean(a):
    return jnp.sum(a, axis=-1, keepdims=True) * (1.0 / 768.0)


def mid_kernel(
    x_ref, c_ref, heads_ref, g_ref, vec_ref,
    out_ref, g1_ref, g1low_ref, dout_ref, d_ref, v_ref,
    xv, cv, hv, wo, w2, w3, xhat, inv, low, act, gd, acc, glow, lowT, gT, stage, dst, ls, ds_, ss, rs,
):
    pc = Place()
    sems = Sems(ss, rs)
    l_x = local(x_ref, xv, ls.at[0])
    l_h = local(heads_ref, hv, ls.at[1])
    l_wo = [local(g_ref.at[0, y, c, :, :, :, pl.ds(512, 256)], wo.at[2 * y + c], ls.at[2 + 2 * y + c]) for y in range(2) for c in range(2)]
    l_w2 = local(g_ref.at[1], w2, ls.at[6])
    l_w3 = local(g_ref.at[2], w3, ls.at[7])
    l_c = local(c_ref.at[pc.t], cv.at[pc.t], ls.at[8])
    barrier([(pc.dp, pc.t ^ j) for j in (1, 2, 3)])
    cx = exchange(pc, c_ref, cv, sems)
    row = lambda n: vec_ref[n : n + 1, :]
    v_ref[...] = jnp.zeros_like(v_ref)

    def add_row(n, a):
        v_ref[n : n + 1, :] += jnp.sum(a, axis=0, keepdims=True)

    for q in [l_x, l_h] + l_wo:
        q.wait()

    def first(b, _):
        rows = pl.ds(pl.multiple_of(b * 256, 256), 256)
        r = xv[b].astype(f32) + row(2)
        for t in range(4):
            r = r + dot_nt(hv[t, rows, :], wo[t].reshape(768, 256))
        center = r - row_mean(r)
        iv = lax.rsqrt(row_mean(center * center) + EPSILON)
        xh = center * iv
        xhat[rows, :] = xh
        inv[rows, :] = jnp.broadcast_to(iv, (256, 128))
        normed = xh * row(10) + row(8)
        low[rows, :] = normed.astype(bf16)
        acc[rows, :] = normed + row(7)
        return 0

    lax.fori_loop(0, 4, first, 0)
    l_w2.wait()
    l_w3.wait()

    def up(n, _):
        t, b = n // 4, n % 4
        rows = pl.ds(pl.multiple_of(b * 256, 256), 256)
        pre = dotf(low[rows, :], w2[t // 2, t % 2].reshape(768, 768)) + vec_ref[pl.ds(3 + t, 1), :]
        a, d = gelu_pair(pre)
        a = a.astype(bf16)
        act[t, rows, :] = a
        gd[t, rows, :] = d.astype(bf16)
        acc[rows, :] += dot_nt(a, w3[t // 2, t % 2].reshape(768, 768))
        return 0

    lax.fori_loop(0, 16, up, 0)
    l_c.wait()
    for q in cx:
        q.wait()

    def second(b, _):
        rows = pl.ds(pl.multiple_of(b * 256, 256), 256)
        r = acc[rows, :]
        center = r - row_mean(r)
        iv = lax.rsqrt(row_mean(center * center) + EPSILON)
        xh = center * iv
        stage[b] = (xh * row(11) + row(9)).astype(bf16)
        ct = cv[b].astype(f32)
        e = ct * row(11)
        g2 = (e - row_mean(e) - xh * row_mean(e * xh)) * iv
        acc[rows, :] = g2
        glow[rows, :] = g2.astype(bf16)
        add_row(11, ct * xh)
        add_row(9, ct)
        add_row(7, g2)
        return 0

    lax.fori_loop(0, 4, second, 0)
    l_o = local(stage, out_ref, ls.at[0])
    gT[...] = glow[...].T
    lowT[...] = low[...].T

    def sends(t):
        return [pltpu.make_async_copy(dst.at[t % 2, n], d_ref.at[n, t], ds_.at[t % 2, n]) for n in range(2)]

    def down(t, _):
        wt2, wt3 = w2.at[t // 2, t % 2], w3.at[t // 2, t % 2]

        @pl.when(t >= 2)
        def _():
            for q in sends(t - 2):
                q.wait()

        dst[t % 2, 1] = dotf(gT[...], act[t]).astype(bf16)
        for b in range(4):
            rows = slice(256 * b, 256 * b + 256)
            ga = dotf(glow[rows, :], wt3[...].reshape(768, 768))
            gp = (ga * gd[t, rows, :].astype(f32)).astype(bf16)
            gd[t, rows, :] = gp
            acc[rows, :] += dot_nt(gp, wt2[...].reshape(768, 768))
            v_ref[pl.ds(3 + t, 1), :] += jnp.sum(gp.astype(f32), axis=0, keepdims=True)
        dst[t % 2, 0] = dotf(lowT[...], gd[t]).astype(bf16)
        for q in sends(t):
            q.start()
        return 0

    lax.fori_loop(0, 4, down, 0)

    def last(b, _):
        rows = pl.ds(pl.multiple_of(b * 256, 256), 256)
        gn, xh = acc[rows, :], xhat[rows, :]
        e = gn * row(10)
        g1 = (e - row_mean(e) - xh * row_mean(e * xh)) * inv[rows, 0:1]
        acc[rows, :] = g1
        glow[rows, :] = g1.astype(bf16)
        add_row(10, gn * xh)
        add_row(8, gn)
        add_row(2, g1)
        return 0

    lax.fori_loop(0, 4, last, 0)
    l_g = [local(acc, g1_ref, ls.at[1]), local(glow, g1low_ref, ls.at[2])]
    gT[...] = glow[...].T
    for q in sends(2) + sends(3):
        q.wait()
    for t in range(4):
        dst[t // 2, t % 2, :, 0:256] = dotf(gT[...], hv[t]).astype(bf16)
    l_d = [local(dst.at[t // 2, t % 2, :, pl.ds(0, 256)], dout_ref.at[t], ls.at[3 + t]) for t in range(4)]
    for q in [l_o] + l_g + l_d:
        q.wait()


def mid(xs, cs, heads, g, vec):
    v_ = pltpu.VMEM
    dma = pltpu.SemaphoreType.DMA
    sd = jax.ShapeDtypeStruct
    wt = v_((2, 2, 4, 2, 96, 768), bf16)
    return pl.pallas_call(
        mid_kernel,
        out_shape=[sd((4, 256, 768), bf16), sd((L, 768), f32), sd((L, 768), bf16), sd((4, 768, 256), bf16), sd((2, 4, 768, 768), bf16), sd((24, 768), f32)],
        in_specs=[HBM] * 4 + [VM],
        out_specs=[HBM] * 5 + [VM],
        scratch_shapes=[
            v_((4, 256, 768), bf16), v_((4, 256, 768), bf16), v_((4, L, 256), bf16), v_((4, 4, 2, 96, 256), bf16), wt, wt,
            v_((L, 768), f32), v_((L, 128), f32), v_((L, 768), bf16), v_((4, L, 768), bf16), v_((4, L, 768), bf16), v_((L, 768), f32),
            v_((L, 768), bf16), v_((768, L), bf16), v_((768, L), bf16), v_((4, 256, 768), bf16), v_((2, 2, 768, 768), bf16),
            dma((9,)), dma((2, 2)), dma((3,)), dma((3,)),
        ],
        compiler_params=pltpu.CompilerParams(collective_id=2, has_side_effects=True, vmem_limit_bytes=67043328),
    )(xs, cs, heads, g, vec)


def norm_stats(r):
    center = r - jnp.mean(r, axis=-1, keepdims=True)
    inv = lax.rsqrt(jnp.mean(center * center, axis=-1, keepdims=True) + EPSILON)
    return center * inv, inv


def norm_back(cot, gain, xhat, inv):
    e = cot * gain
    grad = (e - jnp.mean(e, -1, keepdims=True) - xhat * jnp.mean(e * xhat, -1, keepdims=True)) * inv
    return grad, jnp.sum(cot * xhat, 0), jnp.sum(cot, 0)


def middle(x, cot, heads, w1, w2, w3, bias_o, bias_h, bias_d, shift1, shift2, gain1, gain2):
    ein = functools.partial(jnp.einsum, preferred_element_type=f32)
    hid = x.astype(f32)
    resid1 = hid + ein("tpw,tdw->pd", heads, w1[:, :, 512:]) + bias_o
    xhat1, inv1 = norm_stats(resid1)
    normed = xhat1 * gain1 + shift1
    low = normed.astype(bf16)
    pre = ein("pd,tdf->tpf", low, w2) + bias_h[:, None, :]
    act, gelu_back = jax.vjp(lambda v: jax.nn.gelu(v, approximate=False), pre)
    act = act.astype(bf16)
    resid2 = normed + ein("tpf,tdf->pd", act, w3) + bias_d
    xhat2, inv2 = norm_stats(resid2)
    out = (xhat2 * gain2 + shift2).astype(bf16)
    g2, dgain2, dshift2 = norm_back(cot.astype(f32), gain2, xhat2, inv2)
    g2low = g2.astype(bf16)
    d3 = ein("pd,tpf->tdf", g2low, act).astype(bf16)
    gpre = gelu_back(ein("pd,tdf->tpf", g2low, w3))[0].astype(bf16)
    d2 = ein("pd,tpf->tdf", low, gpre).astype(bf16)
    gn = g2 + ein("tpf,tdf->pd", gpre, w2)
    g1, dgain1, dshift1 = norm_back(gn, gain1, xhat1, inv1)
    g1low = g1.astype(bf16)
    dout = ein("pd,tpw->tdw", g1low, heads).astype(bf16)
    dbh = jnp.sum(gpre, 1, dtype=f32)
    return out, g1, g1low, dout, d2, d3, (dgain1, dgain2, dshift1, dshift2, jnp.sum(g1, 0), dbh, jnp.sum(g2, 0))


def on_device(hidden_in, cotangent, prefix, w_qkv, w_out, w_in, w_down, biases, gains):
    rows = w_qkv.shape[0]
    n_t = lax.axis_size("tensor")
    t_me, d_me = lax.axis_index("tensor"), lax.axis_index("dp")
    n_dev = n_t * lax.axis_size("dp")
    s = jnp.stack([jnp.concatenate([w_qkv.reshape(rows, -1), w_out.T], axis=1), w_in, w_down.T])
    vecs = jnp.concatenate([biases, gains], 0)
    width = vecs.shape[1]
    vecs = jnp.pad(vecs, ((0, 4), (0, 128 - width)))
    seqs = lambda a: jnp.transpose(a, (1, 0, 2))
    h, c = seqs(hidden_in), seqs(cotangent)
    my_prefix = lax.dynamic_slice_in_dim(prefix, t_me, 1, 0)
    if lax.axis_size("dp") == 8:
        g, xs, vec, proj, projT, heads, ot, lse = front(my_prefix, s, h, vecs)
        out4, g1, g1low, doutw, d, v = mid(xs, c, heads, g, vec)
        gs, vs, oo, xx = back(my_prefix, xs, g1low, g1, g, proj, projT, ot, lse, doutw, d.reshape(2, 2, 2, 4, 2, rows, 768), v, out4)
        qv = vs[16:24, :256].reshape(4, 2, 256)
        vs = jnp.concatenate([qv[:, 0, :192].reshape(1, 768), qv[:, 1, :192].reshape(1, 768), vs[2:16]])
    else:
        ein = functools.partial(jnp.einsum, preferred_element_type=f32)
        g = lax.all_gather(lax.all_gather(s, "dp", axis=1, tiled=True), "tensor", axis=1)
        x = lax.all_to_all(h, "tensor", 0, 0, tiled=True).reshape(1024, 768)
        cot = lax.all_to_all(c, "tensor", 0, 0, tiled=True).reshape(1024, 768)
        b = lax.all_gather(vecs, ("dp", "tensor"), axis=0)
        w1, w2, w3 = [a.reshape(n_t, 768, 768) for a in g]
        vec = b.reshape(n_dev, 16, 128)[:, :12, :width].transpose(1, 0, 2).reshape(12, 768)
        bqkv = jnp.pad(jnp.stack([vec[0].reshape(4, 192), jnp.zeros((4, 192), f32), vec[1].reshape(4, 192)], 1).reshape(4, 1, 576), ((0, 0), (0, 0), (0, 64)))
        proj, projT, heads, ot, lse = attn_fwd(my_prefix, x, w1, bqkv)
        out, g1, g1low, doutw, d2, d3, small = middle(
            x, cot, heads, w1, w2, w3, vec[2], vec[3:7].reshape(4, 768), vec[7], vec[8], vec[9], vec[10], vec[11]
        )
        dgain1, dgain2, dshift1, dshift2, dbo, dbh, dbd = small
        gproj = attn_bwd(my_prefix, g1low, w1, proj, projT, ot, lse)
        gp = gproj[:, :, :576]
        dqkv = ein("pd,tpc->tdc", x, gp).astype(bf16)
        x4 = (g1 + ein("tpc,tdc->pd", gp, w1[:, :, :576])).astype(bf16).reshape(4, 256, 768)
        dbq = jnp.sum(gp[:, :, :192], 1, dtype=f32).reshape(1, 768)
        dbv = jnp.sum(gp[:, :, 384:], 1, dtype=f32).reshape(1, 768)
        d = jnp.stack([jnp.concatenate([dqkv, doutw[:, :, 64:]], 2), d2, d3])
        part = lax.all_to_all(d, "tensor", 1, 1, tiled=True).astype(f32).sum(1)
        part = part.astype(bf16).reshape(3, -1, rows, 768)
        gs = lax.all_to_all(part, "dp", 1, 1, tiled=True).astype(f32).sum(1)
        vs = lax.psum(
            jnp.concatenate([dbq, dbv, dbo[None], dbh, jnp.stack([dbd, dshift1, dshift2, dgain1, dgain2]), jnp.zeros((4, 768), f32)]),
            ("dp", "tensor"),
        )
        oo = lax.all_to_all(out.reshape(4, 256, 768), "tensor", 0, 0, tiled=True)
        xx = lax.all_to_all(x4, "tensor", 0, 0, tiled=True)
    mine = lax.dynamic_slice_in_dim(vs, (d_me * n_t + t_me) * width, width, 1)
    return (
        seqs(oo),
        seqs(xx),
        gs[0, :, :576].reshape(rows, 3, 192),
        gs[0, :, 576:].T,
        gs[1],
        gs[2].T,
        mine[:10],
        mine[10:12],
    )


def solution(mesh):
    placed = (
        P("tensor", "dp", None),
        P("tensor", "dp", None),
        P("dp"),
        P("dp", None, "tensor"),
        P("tensor", "dp"),
        P("dp", "tensor"),
        P("tensor", "dp"),
        P(None, ("dp", "tensor")),
        P(None, ("dp", "tensor")),
    )
    return jax.shard_map(on_device, mesh=mesh, in_specs=placed, out_specs=placed[:2] + placed[3:], check_vma=False)
```

```python
import functools
import math

import jax
import jax.numpy as jnp
from jax import lax
from jax.experimental import pallas as pl
from jax.experimental.pallas import tpu as pltpu
from jax.sharding import PartitionSpec as P

f32=jnp.float32; bf16=jnp.bfloat16
L=1024; QB=256; NK=(512,512,768,1024)
C2=0.125*math.log2(math.e)
NEG=-1e30
def dotf(a,b): return jnp.dot(a,b,preferred_element_type=f32)
def dot_nt(a,b): return lax.dot_general(a,b,(((1,),(1,)),((),())),preferred_element_type=f32)
def masks(mask_ref, prefix):
    k=lax.broadcasted_iota(jnp.int32,(256,256),0); q=lax.broadcasted_iota(jnp.int32,(256,256),1)
    diag=k<=q
    mask_ref[0]=jnp.where(diag|(k<prefix),0.0,NEG)
    mask_ref[1]=jnp.where(k+256<prefix,0.0,NEG)+jnp.zeros((256,256),f32)
    mask_ref[2]=jnp.where(diag|(k+256<prefix),0.0,NEG)
    mask_ref[3]=jnp.where(diag,0.0,NEG)
MASKMAP={0:{0:0,1:1},1:{1:2},2:{2:3},3:{3:3}}
def masked(st,qb,mask_ref):
    parts=[]
    for kb in range(NK[qb]//256):
        p=st[kb*256:(kb+1)*256]
        mi=MASKMAP[qb].get(kb)
        parts.append(p if mi is None else p+mask_ref[mi])
    return jnp.concatenate(parts,0)
def fwd_kernel(prefix_ref,x_ref,w_ref,b_ref,proj_ref,projT_ref,heads_ref,ot_ref,lse_ref,zq_ref,mask_ref):
    masks(mask_ref,prefix_ref[0])
    proj=(dotf(x_ref[...],w_ref[:,:640])+b_ref[...]).astype(bf16)
    proj_ref[...]=proj
    projT_ref[...]=proj.T
    zq_ref[...]=jnp.zeros_like(zq_ref)
    for h in range(3):
        zq_ref[h,64+64*h:128+64*h,:]=projT_ref[64*h:64*h+64,:]
    ot_ref[...]=jnp.zeros_like(ot_ref)
    for h in range(3):
        for qb in range(4):
            nk=NK[qb]; qs=slice(qb*QB,qb*QB+QB)
            st=dotf(proj_ref[:nk,128:384],zq_ref[h,:,qs])
            st=masked(st,qb,mask_ref)
            m=jnp.max(st,axis=0,keepdims=True)
            p=jnp.exp2((st-m)*C2)
            l=jnp.sum(p,axis=0,keepdims=True)
            ot=dotf(projT_ref[384+64*h:448+64*h,:nk],p.astype(bf16))
            ot_ref[64+64*h:128+64*h,qs]=(ot/l).astype(bf16)
            lse_ref[h:h+1,qs]=m*C2+jnp.log2(l)
    heads_ref[...]=ot_ref[...].T
def attn_fwd(prefix,x,w1,bqkv):
    sq=pl.squeezed
    return pl.pallas_call(fwd_kernel,grid_spec=pltpu.PrefetchScalarGridSpec(num_scalar_prefetch=1,grid=(4,),
      in_specs=[pl.BlockSpec((L,768),lambda t,p:(0,0)),pl.BlockSpec((sq,768,768),lambda t,p:(t,0,0)),pl.BlockSpec((sq,1,640),lambda t,p:(t,0,0))],
      out_specs=[pl.BlockSpec((sq,L,640),lambda t,p:(t,0,0)),pl.BlockSpec((sq,640,L),lambda t,p:(t,0,0)),pl.BlockSpec((sq,L,256),lambda t,p:(t,0,0)),pl.BlockSpec((sq,256,L),lambda t,p:(t,0,0)),pl.BlockSpec((sq,8,L),lambda t,p:(t,0,0))],
      scratch_shapes=[pltpu.VMEM((3,256,L),bf16),pltpu.VMEM((4,256,256),f32)]),
      out_shape=[jax.ShapeDtypeStruct((4,L,640),bf16),jax.ShapeDtypeStruct((4,640,L),bf16),jax.ShapeDtypeStruct((4,L,256),bf16),jax.ShapeDtypeStruct((4,256,L),bf16),jax.ShapeDtypeStruct((4,8,L),f32)],
      compiler_params=pltpu.CompilerParams(vmem_limit_bytes=62<<20))(prefix,x,w1,bqkv)
def bwd_kernel(prefix_ref,g_ref,w_ref,proj_ref,projT_ref,ot_ref,lse_ref,gproj_ref,
               zq_ref,zdo_ref,qm_ref,dom_ref,pt_ref,ds_ref,mask_ref,gt_ref,dqt_ref):
    masks(mask_ref,prefix_ref[0])
    gh=dotf(g_ref[...],w_ref[:,512:768]).astype(bf16)
    gt_ref[...]=gh.T
    zq_ref[...]=jnp.zeros_like(zq_ref); zdo_ref[...]=jnp.zeros_like(zdo_ref)
    lane=lax.broadcasted_iota(jnp.int32,(1,256),1)
    for h in range(3):
        zq_ref[h,64+64*h:128+64*h,:]=projT_ref[64*h:64*h+64,:]
        zdo_ref[h,64*h:64*h+64,:]=gt_ref[64+64*h:128+64*h,:]*0.125
        sel=(lane>=64*h)&(lane<64*h+64)
        qm_ref[h]=jnp.where(sel,proj_ref[:,0:256],0)
        sel2=(lane>=64*h+64)&(lane<64*h+128)
        dom_ref[h]=jnp.where(sel2,gh,0)
    for h in range(3):
        d=jnp.sum(gt_ref[64+64*h:128+64*h,:].astype(f32)*ot_ref[64+64*h:128+64*h,:].astype(f32),axis=0,keepdims=True)*0.125
        for qb in range(4):
            nk=NK[qb]; qs=slice(qb*QB,qb*QB+QB)
            st=dotf(proj_ref[:nk,128:384],zq_ref[h,:,qs])
            st=masked(st,qb,mask_ref)
            p=jnp.exp2(st*C2-lse_ref[h:h+1,qs])
            dp=dotf(proj_ref[:nk,384:640],zdo_ref[h,:,qs])
            ds=(p*(dp-d[:,qs])).astype(bf16)
            pt_ref[h,:nk,qs]=p.astype(bf16)
            ds_ref[h,:nk,qs]=ds
            dqt_ref[64*h:64*h+64,qs]=dotf(projT_ref[192+64*h:256+64*h,:nk],ds).astype(bf16)
    gproj_ref[:,0:192]=dqt_ref[...].T
    for (k0,k1,q0) in ((0,512,0),(512,768,512),(768,1024,768)):
        dk=jnp.zeros((k1-k0,256),f32); dv=jnp.zeros((k1-k0,256),f32)
        for h in range(3):
            dk=dk+dotf(ds_ref[h,k0:k1,q0:],qm_ref[h,q0:,:])
            dv=dv+dotf(pt_ref[h,k0:k1,q0:],dom_ref[h,q0:,:])
        gproj_ref[k0:k1,192:384]=dk[:,0:192].astype(bf16)
        gproj_ref[k0:k1,384:576]=dv[:,64:256].astype(bf16)
    gproj_ref[:,576:640]=jnp.zeros((L,64),bf16)
def attn_bwd(prefix,g,w1,proj,projT,ot,lse):
    sq=pl.squeezed
    sp=lambda *s: pl.BlockSpec((sq,)+s,lambda t,p:(t,0,0))
    return pl.pallas_call(functools.partial(bwd_kernel),grid_spec=pltpu.PrefetchScalarGridSpec(num_scalar_prefetch=1,grid=(4,),
      in_specs=[pl.BlockSpec((L,768),lambda t,p:(0,0)),sp(768,768),sp(L,640),sp(640,L),sp(256,L),sp(8,L)],
      out_specs=sp(L,640),
      scratch_shapes=[pltpu.VMEM((3,256,L),bf16),pltpu.VMEM((3,256,L),bf16),pltpu.VMEM((3,L,256),bf16),pltpu.VMEM((3,L,256),bf16),pltpu.VMEM((3,L,L),bf16),pltpu.VMEM((3,L,L),bf16),pltpu.VMEM((4,256,256),f32),pltpu.VMEM((256,L),bf16),pltpu.VMEM((192,L),bf16)]),
      out_shape=jax.ShapeDtypeStruct((4,L,640),bf16),
      compiler_params=pltpu.CompilerParams(vmem_limit_bytes=62<<20))(prefix,g,w1,proj,projT,ot,lse)
MESH=pl.DeviceIdType.MESH
class Place:
    def __init__(self):
        dp=lax.axis_index("dp"); t=lax.axis_index("tensor")
        self.dp,self.t=dp,t
        self.z,self.x,self.y,self.c=dp//2,dp%2,t//2,t%2
    def peer(self,dim,j=1):
        return {'x':lambda:(self.dp^1,self.t),'z':lambda:(self.dp^(2*j),self.t),'y':lambda:(self.dp,self.t^2),'c':lambda:(self.dp,self.t^1)}[dim]()
    def peers_all(self):
        return [self.peer('x'),self.peer('y'),self.peer('c'),self.peer('z',1),self.peer('z',2),self.peer('z',3),(self.dp,self.t^3)]
def barrier(peers):
    b=pltpu.get_barrier_semaphore()
    for p in peers: pl.semaphore_signal(b,inc=1,device_id=p,device_id_type=MESH)
    pl.semaphore_wait(b,len(peers))
class Sems:
    def __init__(self,send,recv): self.s,self.r,self.n=send,recv,0
    def take(self):
        i=self.n; self.n+=1
        return self.s.at[i],self.r.at[i]
def rcopy(src,dst,sems,dev):
    a,b=sems.take()
    return pltpu.make_async_remote_copy(src_ref=src,dst_ref=dst,send_sem=a,recv_sem=b,device_id=dev,device_id_type=MESH)
def local(src,dst,sem):
    k=pltpu.make_async_copy(src,dst,sem); k.start(); return k
def exchange(pc,src,dst,sems):
    out=[]
    for j in (2,3,1):
        p=(pc.dp,pc.t^j)
        k=rcopy(src.at[pc.t^j],dst.at[pc.t],sems,p); k.start(); out.append(k)
    return out
HBM=pl.BlockSpec(memory_space=pltpu.HBM); VM=pl.BlockSpec(memory_space=pltpu.VMEM)
def point(steps, k, h):
    for kk in range(4):
        todo = steps.get((kk, h))
        if todo:
            @pl.when(k == kk)
            def _(todo=todo):
                for step in todo:
                    step()


def add_into(dst, src, n, pick_dst, pick_src):
    def body(j, _):
        a, b = pick_dst(j), pick_src(j)
        dst[a] = (dst[a].astype(f32) + src[b].astype(f32)).astype(bf16)
        return 0
    lax.fori_loop(0, n, body, 0)


class Reduce:
    def __init__(self, pc, kind, d_ref, half, lc, rc, r1, r2, r3, sems, lsem):
        self.pc, self.kind, self.lc, self.rc, self.r1, self.r2, self.r3 = pc, kind, lc, rc, r1, r2, r3
        rows = pl.ds(48 * half, 48)
        self.own = pltpu.make_async_copy(d_ref.at[:, pc.c, :, :, rows], lc, lsem)
        self.q0 = rcopy(d_ref.at[:, 1 - pc.c, :, :, rows], rc, sems, pc.peer("c"))
        if kind == "x":
            self.q1 = rcopy(lc.at[:, :, 1 - pc.x], r1, sems, pc.peer("x"))
            self.q2 = [rcopy(lc.at[:, pc.z ^ j, pc.x], r2.at[j - 1], sems, pc.peer("z", j)) for j in (3, 2, 1)]
            self.q3 = [rcopy(lc.at[1 - pc.y, pc.z, pc.x], r3.at[0], sems, pc.peer("y"))]
        else:
            self.q1 = rcopy(lc.at[1 - pc.y], r1, sems, pc.peer("y"))
            self.q2 = [rcopy(lc.at[pc.y, :, 1 - pc.x], r2, sems, pc.peer("x"))]
            self.q3 = [rcopy(lc.at[pc.y, pc.z ^ j, pc.x], r3.at[j - 1], sems, pc.peer("z", j)) for j in (3, 2, 1)]

    def s0(self):
        self.own.start()
        self.q0.start()

    def s1(self):
        self.own.wait()
        self.q0.wait_recv()
        at = lambda j: (j // 8, (j // 2) % 4, j % 2)
        add_into(self.lc, self.rc, 16, at, at)
        self.q1.start()

    def s2(self):
        self.q1.wait_recv()
        if self.kind == "x":
            add_into(self.lc, self.r1, 8, lambda j: (j // 4, j % 4, self.pc.x), lambda j: (j // 4, j % 4))
        else:
            add_into(self.lc, self.r1, 8, lambda j: (self.pc.y, j // 2, j % 2), lambda j: (j // 2, j % 2))
        for q in self.q2:
            q.start()

    def s3(self):
        pc = self.pc
        for q in self.q2:
            q.wait_recv()
        if self.kind == "x":
            for y in range(2):
                at = (y, pc.z, pc.x)
                total = (self.lc[at].astype(f32) + self.r2[0, y].astype(f32)) + (self.r2[1, y].astype(f32) + self.r2[2, y].astype(f32))
                self.lc[at] = total.astype(bf16)
        else:
            add_into(self.lc, self.r2, 4, lambda j: (pc.y, j, pc.x), lambda j: (j,))
        for q in self.q3:
            q.start()

    def s4(self, out_ref, rows):
        pc = self.pc
        for q in self.q3:
            q.wait_recv()
        total = self.lc[pc.y, pc.z, pc.x].astype(f32) + self.r3[0].astype(f32)
        if self.kind == "y":
            total = total + (self.r3[1].astype(f32) + self.r3[2].astype(f32))
        out_ref[rows] = total

    def end(self):
        for q in [self.q0, self.q1] + self.q2 + self.q3:
            q.wait_send()


N_C = 4 * 6 + 3 + 3 + 8 + 6 + 6


def back_kernel(
    prefix_ref, x_ref, g_ref, gf_ref, w_ref, proj_ref, projT_ref, ot_ref, lse_ref, dout_ref, d_ref, v_ref,
    gs_ref, vs_ref, xo_ref,
    xT, gl, dxa, w_b, proj_b, projT_b, ot_b, lse_b, dout_b,
    zq, zdo, qm, dom, pt, ds, mask_ref, gt, dqt, dkb, dvb, gproj,
    lc, rc, yx1, yx2, yx3, yy1, yy2, yy3, dwb, cr, yr, xr, zr, vb, vr, xst, ss, rs, ls, ins,
):
    pc = Place()
    sems = Sems(ss, rs)
    w1 = w_ref.at[0]
    lane = lax.broadcasted_iota(jnp.int32, (1, 256), 1)

    def loads(k, slot):
        t = pc.t ^ (3 - k)
        pairs = [
            (w1.at[t // 2, t % 2], w_b), (proj_ref.at[t], proj_b), (projT_ref.at[t], projT_b),
            (ot_ref.at[t], ot_b), (lse_ref.at[t], lse_b), (dout_ref.at[t], dout_b),
        ]
        return [pltpu.make_async_copy(a, b.at[slot], ins.at[slot, n]) for n, (a, b) in enumerate(pairs)]

    first = loads(0, 0)
    for q in first:
        q.start()
    l_x = local(x_ref, xst, ls.at[4])
    l_g = local(g_ref, gl, ls.at[5])
    l_f = local(gf_ref, dxa, ls.at[6])
    barrier(pc.peers_all())
    red = []
    for n, (kind, g, i) in enumerate((("y", 1, 0), ("x", 1, 1), ("y", 0, 0), ("x", 0, 1))):
        r1, r2, r3 = [r.at[n // 2] for r in ((yy1, yy2, yy3) if kind == "y" else (yx1, yx2, yx3))]
        red.append(Reduce(pc, kind, d_ref.at[g], i, lc.at[n], rc.at[n], r1, r2, r3, sems, ls.at[n]))
        red[n].s0()
    q_c0 = rcopy(dwb.at[0], cr.at[0], sems, pc.peer("c"))
    q_y = rcopy(dwb.at[1], yr, sems, pc.peer("y"))
    q_c1 = rcopy(dwb.at[2], cr.at[1], sems, pc.peer("c"))
    half = [pl.ds(48 * i, 48) for i in range(2)]
    q_x = [rcopy(dwb.at[3, pc.z ^ j, 1 - pc.x, half[i]], xr.at[i, pc.z ^ j], sems, pc.peer("x")) for i in range(2) for j in (3, 2, 1, 0)]
    q_z = [rcopy(dwb.at[3, pc.z ^ j, pc.x, half[i]], zr.at[i, j - 1], sems, pc.peer("z", j)) for i in range(2) for j in (3, 2, 1)]
    v_q = [rcopy(vb.at[n], vr.at[n], sems, pc.peer(dim)) for n, dim in enumerate("cxy")]
    v_z = [rcopy(vb.at[3], vr.at[2 + j], sems, pc.peer("z", j)) for j in (3, 2, 1)]

    def vstep(n):
        v_q[n].wait_recv()
        vb[n + 1] = vb[n] + vr[n]
        for q in [v_q[n + 1]] if n < 2 else v_z:
            q.start()

    steps = {
        (0, 0): [red[0].s1], (0, 1): [red[1].s1], (0, 2): [red[2].s1], (0, 3): [red[3].s1],
        (1, 1): [red[1].s2], (1, 2): [red[0].s2], (2, 1): [red[3].s2, red[2].s2], (2, 2): [red[1].s3],
        (3, 0): [red[0].s3], (3, 1): [red[3].s3], (3, 2): [red[2].s3],
    }
    masks(mask_ref, prefix_ref[0])
    zq[...] = jnp.zeros_like(zq)
    zdo[...] = jnp.zeros_like(zdo)
    gproj[:, 576:640] = jnp.zeros((L, 64), bf16)
    vb[0] = v_ref[...]
    l_x.wait()
    xT[...] = xst[...].reshape(L, 768).T
    l_g.wait()
    l_f.wait()

    def group(k, _):
        slot = k % 2
        for q in loads(k, slot):
            q.wait()

        @pl.when(k < 3)
        def _():
            for q in loads(k + 1, 1 - slot):
                q.start()

        t = pc.t ^ (3 - k)
        w, pj, pjT, o_t, lse = w_b.at[slot], proj_b.at[slot], projT_b.at[slot], ot_b.at[slot], lse_b.at[slot]
        gh = dotf(gl[...], w[...].reshape(768, 768)[:, 512:768]).astype(bf16)
        gt[...] = gh.T
        for h in range(3):
            point(steps, k, h)
            own = slice(64 + 64 * h, 128 + 64 * h)
            zq[h, own, :] = pjT[64 * h : 64 * h + 64, :]
            zdo[h, 64 * h : 64 * h + 64, :] = gt[own, :] * 0.125
            qm[...] = jnp.where((lane >= 64 * h) & (lane < 64 * h + 64), pj[:, 0:256], 0)
            dom[...] = jnp.where((lane >= 64 * h + 64) & (lane < 64 * h + 128), gh, 0)
            d = jnp.sum(gt[own, :].astype(f32) * o_t[own, :].astype(f32), axis=0, keepdims=True) * 0.125
            for qb in range(4):
                nk = NK[qb]
                qs = slice(qb * QB, qb * QB + QB)
                st = masked(dotf(pj[:nk, 128:384], zq[h, :, qs]), qb, mask_ref)
                p = jnp.exp2(st * C2 - lse[h : h + 1, qs])
                dp = dotf(pj[:nk, 384:640], zdo[h, :, qs])
                dsv = (p * (dp - d[:, qs])).astype(bf16)
                pt[:nk, qs] = p.astype(bf16)
                ds[:nk, qs] = dsv
                dqt[64 * h : 64 * h + 64, qs] = dotf(pjT[192 + 64 * h : 256 + 64 * h, :nk], dsv).astype(bf16)
            for k0, k1, q0 in ((0, 512, 0), (512, 768, 512), (768, 1024, 768)):
                dk = dotf(ds[k0:k1, q0:], qm[q0:, :]).astype(bf16)
                dv = dotf(pt[k0:k1, q0:], dom[q0:, :]).astype(bf16)
                dkb[k0:k1] = dk if h == 0 else dkb[k0:k1] + dk
                dvb[k0:k1] = dv if h == 0 else dvb[k0:k1] + dv
        point(steps, k, 3)
        gproj[:, 0:192] = dqt[...].T
        gproj[:, 192:384] = dkb[:, 0:192]
        gproj[:, 384:576] = dvb[:, 64:256]
        vb[0, pl.ds(16 + 2 * t, 1), 0:256] = jnp.sum(gproj[:, 0:256].astype(f32), axis=0, keepdims=True)
        vb[0, pl.ds(17 + 2 * t, 1), 0:256] = jnp.sum(gproj[:, 384:640].astype(f32), axis=0, keepdims=True)

        @pl.when(k == 3)
        def _():
            v_q[0].start()

        dw = dotf(xT[...], gproj[...])
        do = dout_b[slot].astype(f32)
        shape = lambda a: a.astype(bf16).reshape(4, 2, 96, a.shape[1])
        dwb[k, :, :, :, 0:512] = shape(dw[:, 0:512])
        dwb[k, :, :, :, 512:640] = shape(dw[:, 512:640] + do[:, 0:128])
        dwb[k, :, :, :, 640:768] = shape(do[:, 128:256])

        @pl.when(k == 0)
        def _():
            q_c0.start()

        @pl.when(k == 1)
        def _():
            q_c0.wait_recv()
            add_into(dwb.at[1], cr.at[0], 8, lambda j: (j // 2, j % 2), lambda j: (j // 2, j % 2))
            q_y.start()

        @pl.when(k == 2)
        def _():
            q_c1.start()

        @pl.when(k == 3)
        def _():
            vstep(0)
            q_c1.wait_recv()
            add_into(dwb.at[3], cr.at[1], 8, lambda j: (j // 2, j % 2), lambda j: (j // 2, j % 2))
            q_y.wait_recv()
            add_into(dwb.at[3], yr, 8, lambda j: (j // 2, j % 2), lambda j: (j // 2, j % 2))
            for q in q_x:
                q.start()

        dxa[...] += dot_nt(gproj[...], w[...].reshape(768, 768)[:, 0:640])
        return 0

    lax.fori_loop(0, 4, group, 0)
    vstep(1)
    xst[...] = dxa[...].astype(bf16).reshape(4, 256, 768)
    xx = exchange(pc, xst, xo_ref, sems)
    l_o = local(xst.at[pc.t], xo_ref.at[pc.t], ls.at[7])
    vstep(2)

    def arrive(n, j):
        i, z = n // 4, pc.z ^ j
        q_x[n].wait_recv()
        dwb[3, z, pc.x, half[i]] = (dwb[3, z, pc.x, half[i]].astype(f32) + xr[i, z].astype(f32)).astype(bf16)

    for n in range(8):
        j = 3 - n % 4
        arrive(n, j)
        if j:
            q_z[n - n // 4].start()
        if n == 1:
            red[0].s4(gs_ref.at[2], slice(0, 48))
        if n == 3:
            red[2].s4(gs_ref.at[1], slice(0, 48))
    red[1].s4(gs_ref.at[2], slice(48, 96))
    red[3].s4(gs_ref.at[1], slice(48, 96))
    for q in v_z:
        q.wait_recv()
    vs_ref[...] = (vb[3] + vr[3]) + (vr[4] + vr[5])
    for i in range(2):
        for q in q_z[3 * i : 3 * i + 3]:
            q.wait_recv()
        gs_ref[0, 48 * i : 48 * i + 48] = (dwb[3, pc.z, pc.x, half[i]].astype(f32) + zr[i, 0].astype(f32)) + (zr[i, 1].astype(f32) + zr[i, 2].astype(f32))
    l_o.wait()
    for q in xx:
        q.wait()
    for r in red:
        r.end()
    for q in [q_c0, q_y, q_c1] + q_x + q_z + v_q + v_z:
        q.wait_send()


def back(prefix, x, g1low, g1, g, proj, projT, ot, lse, doutw, d, v):
    v_ = pltpu.VMEM
    dma = pltpu.SemaphoreType.DMA
    sd = jax.ShapeDtypeStruct
    return pl.pallas_call(
        back_kernel,
        out_shape=[sd((3, 96, 768), f32), sd((24, 768), f32), sd((4, 256, 768), bf16)],
        in_specs=[pl.BlockSpec(memory_space=pltpu.SMEM)] + [HBM] * 10 + [VM],
        out_specs=[VM, VM, HBM],
        scratch_shapes=[
            v_((768, L), bf16), v_((L, 768), bf16), v_((L, 768), f32),
            v_((2, 4, 2, 96, 768), bf16), v_((2, L, 640), bf16), v_((2, 640, L), bf16), v_((2, 256, L), bf16), v_((2, 8, L), f32), v_((2, 768, 256), bf16),
            v_((3, 256, L), bf16), v_((3, 256, L), bf16), v_((L, 256), bf16), v_((L, 256), bf16), v_((L, L), bf16), v_((L, L), bf16),
            v_((4, 256, 256), f32), v_((256, L), bf16), v_((192, L), bf16), v_((L, 256), bf16), v_((L, 256), bf16), v_((L, 640), bf16),
            v_((4, 2, 4, 2, 48, 768), bf16), v_((4, 2, 4, 2, 48, 768), bf16),
            v_((2, 2, 4, 48, 768), bf16), v_((2, 3, 2, 48, 768), bf16), v_((2, 1, 48, 768), bf16),
            v_((2, 4, 2, 48, 768), bf16), v_((2, 4, 48, 768), bf16), v_((2, 3, 48, 768), bf16),
            v_((4, 4, 2, 96, 768), bf16), v_((2, 4, 2, 96, 768), bf16), v_((4, 2, 96, 768), bf16), v_((2, 4, 48, 768), bf16), v_((2, 3, 48, 768), bf16),
            v_((4, 24, 768), f32), v_((6, 24, 768), f32), v_((4, 256, 768), bf16),
            dma((N_C,)), dma((N_C,)), dma((8,)), dma((2, 6)),
        ],
        compiler_params=pltpu.CompilerParams(collective_id=1, has_side_effects=True, vmem_limit_bytes=67043328),
    )(prefix, x, g1low, g1, g, proj, projT, ot, lse, doutw, d, v)


class Gather:
    def __init__(self, pc, src, dst, rows, order, sems):
        self.pc, self.src, self.dst, self.rows, self.order, self.sems = pc, src, dst, rows, order, sems
        self.full, self.sent, self.core = set(), [], []
        self.plan()

    def at(self, over, full):
        pc = self.pc
        ix = {d: over.get(d, slice(None) if d in full else getattr(pc, d)) for d in "yzx"}
        return self.dst.at[(ix["y"], pc.c, ix["z"], ix["x"]) + ((pl.ds(*self.rows),) if self.rows else ())]

    def plan(self):
        pc = self.pc
        src = self.src.at[pl.ds(*self.rows)] if self.rows else self.src
        mine = self.at({}, set())
        self.core.append(rcopy(src, mine, self.sems, pc.peer("c")))
        self.phases = []
        full = set()
        for d in self.order:
            ks = []
            for j in (1, 2, 3) if d == "z" else (1,):
                here = self.at({}, full)
                ks.append(rcopy(here if full else src, here, self.sems, pc.peer(d, j)))
                there = self.at({d: getattr(pc, d) ^ j}, full)
                self.core.append(rcopy(there, there, self.sems, pc.peer("c")))
            self.phases.append(ks)
            full = full | {d}
        self.first = [1]
        for ks in self.phases:
            self.first.append(self.first[-1] + len(ks))

    def start(self):
        self.core[0].start()
        for k in self.phases[0]:
            k.start()

    def arrive(self, p):
        for n, k in enumerate(self.phases[p]):
            k.wait_recv()
            self.core[self.first[p] + n].start()

    def next(self, p):
        self.arrive(p - 1)
        for k in self.phases[p]:
            k.start()

    def from_core(self, a, b):
        for k in self.core[a:b]:
            k.wait_recv()

    def end(self):
        for k in self.core + sum(self.phases, []):
            k.wait_send()


class Slabs:
    def __init__(self, pc, src, dst, kind, rows, sems):
        src = src.at[rows]
        at = lambda y, z, x: dst.at[y, pc.c, z, x, rows]
        every = slice(None)
        mine, other = pc.y, 1 - pc.y
        self.copy, self.fwd = {}, {}

        def add(name, dim, pairs, got):
            self.copy[name] = [rcopy(a, b, sems, pc.peer(dim, j)) for j, a, b in pairs]
            if got is not None:
                self.fwd[name] = rcopy(got, got, sems, pc.peer("c"))

        slab = at(mine, every, pc.x)
        add("z", "z", [(j, src, at(mine, pc.z, pc.x)) for j in (3, 2, 1)], slab)
        add("x", "x", [(1, slab, slab)], at(mine, every, 1 - pc.x))
        if kind == "A":
            whole = at(mine, every, every)
            add("y", "y", [(1, whole, whole)], at(other, every, every))
        else:
            add("y", "y", [(1, src, at(mine, pc.z, pc.x))], None)
            one, slab2 = at(other, pc.z, pc.x), at(other, every, pc.x)
            add("z2", "z", [(j, one, one) for j in (3, 2, 1)], slab2)
            add("x2", "x", [(1, slab2, slab2)], at(other, every, 1 - pc.x))

    def start(self, name):
        for k in self.copy[name]:
            k.start()

    def arrive(self, name):
        for k in self.copy[name]:
            k.wait_recv()
        if name in self.fwd:
            self.fwd[name].start()

    def from_core(self, *names):
        for n in names:
            self.fwd[n].wait_recv()

    def end(self):
        for ks in self.copy.values():
            for k in ks:
                k.wait_send()
        for k in self.fwd.values():
            k.wait_send()


N_A = 3 * 8 + 3 * 13 + 11 + 3


def front_kernel(
    prefix_ref, s_ref, h_ref, b_ref,
    g_ref, x_ref, vec_ref, proj_ref, projT_ref, heads_ref, ot_ref, lse_ref,
    bv, sv, xv, wv, proj_b, projT_b, heads_b, ot_b, lse_b, zq, mask_ref, ss, rs, ls, os_,
):
    pc = Place()
    sems = Sems(ss, rs)
    own = (pc.y, pc.c, pc.z, pc.x)
    l_s = local(s_ref, sv, ls.at[0])
    l_h = local(h_ref.at[pc.t], xv.at[pc.t], ls.at[1])
    l_b = local(b_ref, bv.at[own], ls.at[9])
    barrier(pc.peers_all())
    bias = Gather(pc, b_ref, bv, None, "zxy", sems)
    w1a, w1b, w2a, w2b, w3a, w3b = every = [
        Slabs(pc, s_ref.at[n // 2], g_ref.at[n // 2], kind, pl.ds(48 * (n % 2), 48), sems) for n, kind in enumerate("ABAABB")
    ]
    bias.start()
    w1b.start("y")
    w1a.start("z")
    w1b.start("z")
    hx = exchange(pc, h_ref, xv, sems)
    w3a.start("y")
    w3b.start("y")
    l_s.wait()
    l_g = [local(sv.at[g], g_ref.at[g].at[own], ls.at[3 + g]) for g in range(3)]
    masks(mask_ref, prefix_ref[0])
    zq[...] = jnp.zeros_like(zq)
    ot_b[...] = jnp.zeros_like(ot_b)
    for q in l_g:
        q.wait()
    l_b.wait()
    w1b.arrive("y")
    w1b.start("z2")
    for g in (w2a, w2b, w3a):
        g.start("z")
    bias.next(1)
    w1a.arrive("z")
    w1a.start("x")
    bias.next(2)
    w1b.arrive("z")
    w1b.start("x")
    w1a.arrive("x")
    w1a.start("y")
    w1b.arrive("z2")
    w1b.start("x2")
    w1b.arrive("x")
    bias.arrive(2)
    bias.from_core(0, len(bias.core))
    l_h.wait()
    for q in hx:
        q.wait_recv()
    l_x = local(xv, x_ref, ls.at[7])

    def load(k, slot):
        t = pc.t ^ k
        return pltpu.make_async_copy(g_ref.at[0, t // 2, t % 2], wv.at[slot], ls.at[8])

    def go(g, got, then=None, then_g=None):
        def step():
            g.arrive(got)
            if then:
                (then_g or g).start(then)
        return step

    steps = {
        (0, 0): [go(w3a, "y", "z2"), lambda: w3b.start("z"), go(w3b, "y", "z2")],
        (0, 2): [go(w2a, "z", "x"), lambda: w1a.from_core("z", "x"), lambda: w1b.from_core("z", "x"), lambda: load(1, 1).start()],
        (0, 3): [go(w1b, "x2")],
        (1, 1): [go(w2b, "z", "x")],
        (1, 2): [go(w2a, "x", "y")],
        (1, 3): [go(w1a, "y"), lambda: load(2, 0).start()],
        (2, 1): [go(w3a, "z", "x"), go(w2b, "x", "y")],
        (2, 2): [lambda: w1a.from_core("y"), lambda: w1b.from_core("z2", "x2"), lambda: load(3, 1).start()],
        (3, 0): [go(w3a, "z2", "x2")],
        (3, 1): [go(w3a, "x"), go(w2a, "y")],
        (3, 3): [go(w3b, "z", "x")],
    }
    load(0, 0).start()

    def outs(k, slot):
        t = pc.t ^ k
        pairs = [(proj_b, proj_ref), (projT_b, projT_ref), (heads_b, heads_ref), (ot_b, ot_ref), (lse_b, lse_ref)]
        return [pltpu.make_async_copy(a.at[slot], b.at[t], os_.at[slot, n]) for n, (a, b) in enumerate(pairs)]

    def group(k, _):
        slot = k % 2
        t = pc.t ^ k
        load(k, slot).wait()

        @pl.when(k >= 2)
        def _():
            for q in outs(k - 2, slot):
                q.wait()

        row = jnp.zeros((8, 256), f32)
        for i in range(8):
            piece = bv[(i // 2) % 2, i % 2, t, i // 4, 0:8, :]
            row = row + pltpu.roll(jnp.concatenate([piece, jnp.zeros((8, 128), f32)], 1), 24 * i, 1)
        brow = jnp.concatenate([row[0:1], jnp.zeros((1, 128), f32), row[1:2]], 1)
        pj, pjT, ot, lse = proj_b.at[slot], projT_b.at[slot], ot_b.at[slot], lse_b.at[slot]
        proj = (dotf(xv[...].reshape(L, 768), wv[slot].reshape(768, 768)[:, :640]) + brow).astype(bf16)
        pj[...] = proj
        pjT[...] = proj.T
        for h in range(3):
            point(steps, k, h)
            zq[h, 64 + 64 * h : 128 + 64 * h, :] = pjT[64 * h : 64 * h + 64, :]
            for qb in range(4):
                nk = NK[qb]
                qs = slice(qb * QB, qb * QB + QB)
                st = masked(dotf(pj[:nk, 128:384], zq[h, :, qs]), qb, mask_ref)
                m = jnp.max(st, axis=0, keepdims=True)
                p = jnp.exp2((st - m) * C2)
                l = jnp.sum(p, axis=0, keepdims=True)
                o = dotf(pjT[384 + 64 * h : 448 + 64 * h, :nk], p.astype(bf16))
                ot[64 + 64 * h : 128 + 64 * h, qs] = (o / l).astype(bf16)
                lse[h : h + 1, qs] = m * C2 + jnp.log2(l)
        point(steps, k, 3)
        heads_b[slot] = ot[...].T
        for q in outs(k, slot):
            q.start()
        return 0

    lax.fori_loop(0, 4, group, 0)
    w3a.arrive("x2")
    w3b.arrive("z2")
    w3b.start("x2")
    tiles = [jnp.zeros((16, 128), f32) for _ in range(6)]
    lane = lax.broadcasted_iota(jnp.int32, (1, 128), 1)
    for i in range(32):
        z, x, y, c = i // 8, (i // 4) % 2, (i // 2) % 2, i % 2
        j, r = (24 * i) // 128, (24 * i) % 128
        piece = pltpu.roll(bv[y, c, z, x], r, 1) if r else bv[y, c, z, x]
        tiles[j] = tiles[j] + (jnp.where(lane >= r, piece, 0.0) if r > 104 else piece)
        if r > 104:
            tiles[j + 1] = tiles[j + 1] + jnp.where(lane < r, piece, 0.0)
    for j in range(6):
        vec_ref[:, 128 * j : 128 * j + 128] = tiles[j]
    w2b.arrive("y")
    w3b.arrive("x")
    w3b.arrive("x2")
    for g in (w2a, w2b):
        g.from_core("z", "x", "y")
    for g in (w3a, w3b):
        g.from_core("z", "x", "z2", "x2")
    for q in hx:
        q.wait_send()
    l_x.wait()
    for k in (2, 3):
        for q in outs(k, k % 2):
            q.wait()
    bias.end()
    for g in every:
        g.end()


def front(prefix, s, h, b):
    v_ = pltpu.VMEM
    dma = pltpu.SemaphoreType.DMA
    sd = jax.ShapeDtypeStruct
    return pl.pallas_call(
        front_kernel,
        out_shape=[
            sd((3, 2, 2, 4, 2, 96, 768), bf16), sd((4, 256, 768), bf16), sd((16, 768), f32),
            sd((4, L, 640), bf16), sd((4, 640, L), bf16), sd((4, L, 256), bf16), sd((4, 256, L), bf16), sd((4, 8, L), f32),
        ],
        in_specs=[pl.BlockSpec(memory_space=pltpu.SMEM)] + [HBM] * 2 + [VM],
        out_specs=[HBM] * 2 + [VM] + [HBM] * 5,
        scratch_shapes=[
            v_((2, 2, 4, 2, 16, 128), f32), v_((3, 96, 768), bf16), v_((4, 256, 768), bf16), v_((2, 4, 2, 96, 768), bf16),
            v_((2, L, 640), bf16), v_((2, 640, L), bf16), v_((2, L, 256), bf16), v_((2, 256, L), bf16), v_((2, 8, L), f32),
            v_((3, 256, L), bf16), v_((4, 256, 256), f32),
            dma((N_A,)), dma((N_A,)), dma((10,)), dma((2, 5)),
        ],
        compiler_params=pltpu.CompilerParams(collective_id=0, has_side_effects=True, vmem_limit_bytes=67043328),
    )(prefix, s, h, b)


EPSILON = 1e-12


def gelu_pair(v):
    cdf = 0.5 + 0.5 * lax.erf(v * math.sqrt(0.5))
    pdf = jnp.exp2(v * v * (-0.5 * math.log2(math.e))) * (1.0 / math.sqrt(2.0 * math.pi))
    return v * cdf, cdf + v * pdf


def row_mean(a):
    return jnp.sum(a, axis=-1, keepdims=True) * (1.0 / 768.0)


def mid_kernel(
    x_ref, c_ref, heads_ref, g_ref, vec_ref,
    oo_ref, g1_ref, g1low_ref, dout_ref, d_ref, v_ref,
    xv, cv, hv, wo, w2, w3, xhat, inv, low, act, gd, acc, glow, lowT, gT, stage, dst, ls, ds_, ss, rs,
):
    pc = Place()
    sems = Sems(ss, rs)
    l_x = local(x_ref, xv, ls.at[0])
    l_h = local(heads_ref, hv, ls.at[1])
    l_wo = [local(g_ref.at[0, y, c, :, :, :, pl.ds(512, 256)], wo.at[2 * y + c], ls.at[2 + 2 * y + c]) for y in range(2) for c in range(2)]
    l_w2 = local(g_ref.at[1], w2, ls.at[6])
    l_w3 = local(g_ref.at[2], w3, ls.at[7])
    l_c = local(c_ref.at[pc.t], cv.at[pc.t], ls.at[8])
    barrier([(pc.dp, pc.t ^ j) for j in (1, 2, 3)])
    cx = exchange(pc, c_ref, cv, sems)
    row = lambda n: vec_ref[n : n + 1, :]
    v_ref[...] = jnp.zeros_like(v_ref)

    def add_row(n, a):
        v_ref[n : n + 1, :] += jnp.sum(a, axis=0, keepdims=True)

    for q in [l_x, l_h] + l_wo:
        q.wait()

    def first(b, _):
        rows = pl.ds(pl.multiple_of(b * 256, 256), 256)
        r = xv[b].astype(f32) + row(2)
        for t in range(4):
            r = r + dot_nt(hv[t, rows, :], wo[t].reshape(768, 256))
        center = r - row_mean(r)
        iv = lax.rsqrt(row_mean(center * center) + EPSILON)
        xh = center * iv
        xhat[rows, :] = xh
        inv[rows, :] = jnp.broadcast_to(iv, (256, 128))
        normed = xh * row(10) + row(8)
        low[rows, :] = normed.astype(bf16)
        acc[rows, :] = normed + row(7)
        return 0

    lax.fori_loop(0, 4, first, 0)
    l_w2.wait()
    l_w3.wait()

    def up(n, _):
        t, b = n // 4, n % 4
        rows = pl.ds(pl.multiple_of(b * 256, 256), 256)
        pre = dotf(low[rows, :], w2[t // 2, t % 2].reshape(768, 768)) + vec_ref[pl.ds(3 + t, 1), :]
        a, d = gelu_pair(pre)
        a = a.astype(bf16)
        act[t, rows, :] = a
        gd[t, rows, :] = d.astype(bf16)
        acc[rows, :] += dot_nt(a, w3[t // 2, t % 2].reshape(768, 768))
        return 0

    lax.fori_loop(0, 16, up, 0)
    l_c.wait()
    for q in cx:
        q.wait()

    def second(b, _):
        rows = pl.ds(pl.multiple_of(b * 256, 256), 256)
        r = acc[rows, :]
        center = r - row_mean(r)
        iv = lax.rsqrt(row_mean(center * center) + EPSILON)
        xh = center * iv
        stage[b] = (xh * row(11) + row(9)).astype(bf16)
        ct = cv[b].astype(f32)
        e = ct * row(11)
        g2 = (e - row_mean(e) - xh * row_mean(e * xh)) * iv
        acc[rows, :] = g2
        glow[rows, :] = g2.astype(bf16)
        add_row(11, ct * xh)
        add_row(9, ct)
        add_row(7, g2)
        return 0

    lax.fori_loop(0, 4, second, 0)
    ox = exchange(pc, stage, oo_ref, sems)
    l_o = local(stage.at[pc.t], oo_ref.at[pc.t], ls.at[0])
    gT[...] = glow[...].T
    lowT[...] = low[...].T

    def sends(t):
        return [pltpu.make_async_copy(dst.at[t % 2, n], d_ref.at[n, t], ds_.at[t % 2, n]) for n in range(2)]

    def down(t, _):
        wt2, wt3 = w2.at[t // 2, t % 2], w3.at[t // 2, t % 2]

        @pl.when(t >= 2)
        def _():
            for q in sends(t - 2):
                q.wait()

        dst[t % 2, 1] = dotf(gT[...], act[t]).astype(bf16)
        for b in range(4):
            rows = slice(256 * b, 256 * b + 256)
            ga = dotf(glow[rows, :], wt3[...].reshape(768, 768))
            gp = (ga * gd[t, rows, :].astype(f32)).astype(bf16)
            gd[t, rows, :] = gp
            acc[rows, :] += dot_nt(gp, wt2[...].reshape(768, 768))
            v_ref[pl.ds(3 + t, 1), :] += jnp.sum(gp.astype(f32), axis=0, keepdims=True)
        dst[t % 2, 0] = dotf(lowT[...], gd[t]).astype(bf16)
        for q in sends(t):
            q.start()
        return 0

    lax.fori_loop(0, 4, down, 0)

    def last(b, _):
        rows = pl.ds(pl.multiple_of(b * 256, 256), 256)
        gn, xh = acc[rows, :], xhat[rows, :]
        e = gn * row(10)
        g1 = (e - row_mean(e) - xh * row_mean(e * xh)) * inv[rows, 0:1]
        acc[rows, :] = g1
        glow[rows, :] = g1.astype(bf16)
        add_row(10, gn * xh)
        add_row(8, gn)
        add_row(2, g1)
        return 0

    lax.fori_loop(0, 4, last, 0)
    l_g = [local(acc, g1_ref, ls.at[1]), local(glow, g1low_ref, ls.at[2])]
    gT[...] = glow[...].T
    for q in sends(2) + sends(3):
        q.wait()
    for t in range(4):
        dst[t // 2, t % 2, :, 0:256] = dotf(gT[...], hv[t]).astype(bf16)
    l_d = [local(dst.at[t // 2, t % 2, :, pl.ds(0, 256)], dout_ref.at[t], ls.at[3 + t]) for t in range(4)]
    for q in [l_o] + l_g + l_d + ox:
        q.wait()


def mid(xs, cs, heads, g, vec):
    v_ = pltpu.VMEM
    dma = pltpu.SemaphoreType.DMA
    sd = jax.ShapeDtypeStruct
    wt = v_((2, 2, 4, 2, 96, 768), bf16)
    return pl.pallas_call(
        mid_kernel,
        out_shape=[sd((4, 256, 768), bf16), sd((L, 768), f32), sd((L, 768), bf16), sd((4, 768, 256), bf16), sd((2, 4, 768, 768), bf16), sd((24, 768), f32)],
        in_specs=[HBM] * 4 + [VM],
        out_specs=[HBM] * 5 + [VM],
        scratch_shapes=[
            v_((4, 256, 768), bf16), v_((4, 256, 768), bf16), v_((4, L, 256), bf16), v_((4, 4, 2, 96, 256), bf16), wt, wt,
            v_((L, 768), f32), v_((L, 128), f32), v_((L, 768), bf16), v_((4, L, 768), bf16), v_((4, L, 768), bf16), v_((L, 768), f32),
            v_((L, 768), bf16), v_((768, L), bf16), v_((768, L), bf16), v_((4, 256, 768), bf16), v_((2, 2, 768, 768), bf16),
            dma((9,)), dma((2, 2)), dma((6,)), dma((6,)),
        ],
        compiler_params=pltpu.CompilerParams(collective_id=2, has_side_effects=True, vmem_limit_bytes=67043328),
    )(xs, cs, heads, g, vec)


def norm_stats(r):
    center = r - jnp.mean(r, axis=-1, keepdims=True)
    inv = lax.rsqrt(jnp.mean(center * center, axis=-1, keepdims=True) + EPSILON)
    return center * inv, inv


def norm_back(cot, gain, xhat, inv):
    e = cot * gain
    grad = (e - jnp.mean(e, -1, keepdims=True) - xhat * jnp.mean(e * xhat, -1, keepdims=True)) * inv
    return grad, jnp.sum(cot * xhat, 0), jnp.sum(cot, 0)


def middle(x, cot, heads, w1, w2, w3, bias_o, bias_h, bias_d, shift1, shift2, gain1, gain2):
    ein = functools.partial(jnp.einsum, preferred_element_type=f32)
    hid = x.astype(f32)
    resid1 = hid + ein("tpw,tdw->pd", heads, w1[:, :, 512:]) + bias_o
    xhat1, inv1 = norm_stats(resid1)
    normed = xhat1 * gain1 + shift1
    low = normed.astype(bf16)
    pre = ein("pd,tdf->tpf", low, w2) + bias_h[:, None, :]
    act, gelu_back = jax.vjp(lambda v: jax.nn.gelu(v, approximate=False), pre)
    act = act.astype(bf16)
    resid2 = normed + ein("tpf,tdf->pd", act, w3) + bias_d
    xhat2, inv2 = norm_stats(resid2)
    out = (xhat2 * gain2 + shift2).astype(bf16)
    g2, dgain2, dshift2 = norm_back(cot.astype(f32), gain2, xhat2, inv2)
    g2low = g2.astype(bf16)
    d3 = ein("pd,tpf->tdf", g2low, act).astype(bf16)
    gpre = gelu_back(ein("pd,tdf->tpf", g2low, w3))[0].astype(bf16)
    d2 = ein("pd,tpf->tdf", low, gpre).astype(bf16)
    gn = g2 + ein("tpf,tdf->pd", gpre, w2)
    g1, dgain1, dshift1 = norm_back(gn, gain1, xhat1, inv1)
    g1low = g1.astype(bf16)
    dout = ein("pd,tpw->tdw", g1low, heads).astype(bf16)
    dbh = jnp.sum(gpre, 1, dtype=f32)
    return out, g1, g1low, dout, d2, d3, (dgain1, dgain2, dshift1, dshift2, jnp.sum(g1, 0), dbh, jnp.sum(g2, 0))


def on_device(hidden_in, cotangent, prefix, w_qkv, w_out, w_in, w_down, biases, gains):
    rows = w_qkv.shape[0]
    n_t = lax.axis_size("tensor")
    t_me, d_me = lax.axis_index("tensor"), lax.axis_index("dp")
    n_dev = n_t * lax.axis_size("dp")
    s = jnp.stack([jnp.concatenate([w_qkv.reshape(rows, -1), w_out.T], axis=1), w_in, w_down.T])
    vecs = jnp.concatenate([biases, gains], 0)
    width = vecs.shape[1]
    vecs = jnp.pad(vecs, ((0, 4), (0, 128 - width)))
    seqs = lambda a: jnp.transpose(a, (1, 0, 2))
    h, c = seqs(hidden_in), seqs(cotangent)
    my_prefix = lax.dynamic_slice_in_dim(prefix, t_me, 1, 0)
    if lax.axis_size("dp") == 8:
        g, xs, vec, proj, projT, heads, ot, lse = front(my_prefix, s, h, vecs)
        oo, g1, g1low, doutw, d, v = mid(xs, c, heads, g, vec)
        gs, vs, xx = back(my_prefix, xs, g1low, g1, g, proj, projT, ot, lse, doutw, d.reshape(2, 2, 2, 4, 2, rows, 768), v)
        qv = vs[16:24, :256].reshape(4, 2, 256)
        vs = jnp.concatenate([qv[:, 0, :192].reshape(1, 768), qv[:, 1, :192].reshape(1, 768), vs[2:16]])
    else:
        ein = functools.partial(jnp.einsum, preferred_element_type=f32)
        g = lax.all_gather(lax.all_gather(s, "dp", axis=1, tiled=True), "tensor", axis=1)
        x = lax.all_to_all(h, "tensor", 0, 0, tiled=True).reshape(1024, 768)
        cot = lax.all_to_all(c, "tensor", 0, 0, tiled=True).reshape(1024, 768)
        b = lax.all_gather(vecs, ("dp", "tensor"), axis=0)
        w1, w2, w3 = [a.reshape(n_t, 768, 768) for a in g]
        vec = b.reshape(n_dev, 16, 128)[:, :12, :width].transpose(1, 0, 2).reshape(12, 768)
        bqkv = jnp.pad(jnp.stack([vec[0].reshape(4, 192), jnp.zeros((4, 192), f32), vec[1].reshape(4, 192)], 1).reshape(4, 1, 576), ((0, 0), (0, 0), (0, 64)))
        proj, projT, heads, ot, lse = attn_fwd(my_prefix, x, w1, bqkv)
        out, g1, g1low, doutw, d2, d3, small = middle(
            x, cot, heads, w1, w2, w3, vec[2], vec[3:7].reshape(4, 768), vec[7], vec[8], vec[9], vec[10], vec[11]
        )
        dgain1, dgain2, dshift1, dshift2, dbo, dbh, dbd = small
        gproj = attn_bwd(my_prefix, g1low, w1, proj, projT, ot, lse)
        gp = gproj[:, :, :576]
        dqkv = ein("pd,tpc->tdc", x, gp).astype(bf16)
        x4 = (g1 + ein("tpc,tdc->pd", gp, w1[:, :, :576])).astype(bf16).reshape(4, 256, 768)
        dbq = jnp.sum(gp[:, :, :192], 1, dtype=f32).reshape(1, 768)
        dbv = jnp.sum(gp[:, :, 384:], 1, dtype=f32).reshape(1, 768)
        d = jnp.stack([jnp.concatenate([dqkv, doutw[:, :, 64:]], 2), d2, d3])
        part = lax.all_to_all(d, "tensor", 1, 1, tiled=True).astype(f32).sum(1)
        part = part.astype(bf16).reshape(3, -1, rows, 768)
        gs = lax.all_to_all(part, "dp", 1, 1, tiled=True).astype(f32).sum(1)
        vs = lax.psum(
            jnp.concatenate([dbq, dbv, dbo[None], dbh, jnp.stack([dbd, dshift1, dshift2, dgain1, dgain2]), jnp.zeros((4, 768), f32)]),
            ("dp", "tensor"),
        )
        oo = lax.all_to_all(out.reshape(4, 256, 768), "tensor", 0, 0, tiled=True)
        xx = lax.all_to_all(x4, "tensor", 0, 0, tiled=True)
    mine = lax.dynamic_slice_in_dim(vs, (d_me * n_t + t_me) * width, width, 1)
    return (
        seqs(oo),
        seqs(xx),
        gs[0, :, :576].reshape(rows, 3, 192),
        gs[0, :, 576:].T,
        gs[1],
        gs[2].T,
        mine[:10],
        mine[10:12],
    )


def solution(mesh):
    placed = (
        P("tensor", "dp", None),
        P("tensor", "dp", None),
        P("dp"),
        P("dp", None, "tensor"),
        P("tensor", "dp"),
        P("dp", "tensor"),
        P("tensor", "dp"),
        P(None, ("dp", "tensor")),
        P(None, ("dp", "tensor")),
    )
    return jax.shard_map(on_device, mesh=mesh, in_specs=placed, out_specs=placed[:2] + placed[3:], check_vma=False)
```

```python
import functools
import math

import jax
import jax.numpy as jnp
from jax import lax
from jax.experimental import pallas as pl
from jax.experimental.pallas import tpu as pltpu
from jax.sharding import PartitionSpec as P

f32=jnp.float32; bf16=jnp.bfloat16
L=1024; QB=256; NK=(512,512,768,1024)
C2=0.125*math.log2(math.e)
NEG=-1e30
def dotf(a,b): return jnp.dot(a,b,preferred_element_type=f32)
def dot_nt(a,b): return lax.dot_general(a,b,(((1,),(1,)),((),())),preferred_element_type=f32)
def masks(mask_ref, prefix):
    k=lax.broadcasted_iota(jnp.int32,(256,256),0); q=lax.broadcasted_iota(jnp.int32,(256,256),1)
    diag=k<=q
    mask_ref[0]=jnp.where(diag|(k<prefix),0.0,NEG)
    mask_ref[1]=jnp.where(k+256<prefix,0.0,NEG)+jnp.zeros((256,256),f32)
    mask_ref[2]=jnp.where(diag|(k+256<prefix),0.0,NEG)
    mask_ref[3]=jnp.where(diag,0.0,NEG)
MASKMAP={0:{0:0,1:1},1:{1:2},2:{2:3},3:{3:3}}
def masked(st,qb,mask_ref):
    parts=[]
    for kb in range(NK[qb]//256):
        p=st[kb*256:(kb+1)*256]
        mi=MASKMAP[qb].get(kb)
        parts.append(p if mi is None else p+mask_ref[mi])
    return jnp.concatenate(parts,0)
def fwd_kernel(prefix_ref,x_ref,w_ref,b_ref,proj_ref,projT_ref,heads_ref,ot_ref,lse_ref,zq_ref,mask_ref):
    masks(mask_ref,prefix_ref[0])
    proj=(dotf(x_ref[...],w_ref[:,:640])+b_ref[...]).astype(bf16)
    proj_ref[...]=proj
    projT_ref[...]=proj.T
    zq_ref[...]=jnp.zeros_like(zq_ref)
    for h in range(3):
        zq_ref[h,64+64*h:128+64*h,:]=projT_ref[64*h:64*h+64,:]
    ot_ref[...]=jnp.zeros_like(ot_ref)
    for h in range(3):
        for qb in range(4):
            nk=NK[qb]; qs=slice(qb*QB,qb*QB+QB)
            st=dotf(proj_ref[:nk,128:384],zq_ref[h,:,qs])
            st=masked(st,qb,mask_ref)
            m=jnp.max(st,axis=0,keepdims=True)
            p=jnp.exp2((st-m)*C2)
            l=jnp.sum(p,axis=0,keepdims=True)
            ot=dotf(projT_ref[384+64*h:448+64*h,:nk],p.astype(bf16))
            ot_ref[64+64*h:128+64*h,qs]=(ot/l).astype(bf16)
            lse_ref[h:h+1,qs]=m*C2+jnp.log2(l)
    heads_ref[...]=ot_ref[...].T
def attn_fwd(prefix,x,w1,bqkv):
    sq=pl.squeezed
    return pl.pallas_call(fwd_kernel,grid_spec=pltpu.PrefetchScalarGridSpec(num_scalar_prefetch=1,grid=(4,),
      in_specs=[pl.BlockSpec((L,768),lambda t,p:(0,0)),pl.BlockSpec((sq,768,768),lambda t,p:(t,0,0)),pl.BlockSpec((sq,1,640),lambda t,p:(t,0,0))],
      out_specs=[pl.BlockSpec((sq,L,640),lambda t,p:(t,0,0)),pl.BlockSpec((sq,640,L),lambda t,p:(t,0,0)),pl.BlockSpec((sq,L,256),lambda t,p:(t,0,0)),pl.BlockSpec((sq,256,L),lambda t,p:(t,0,0)),pl.BlockSpec((sq,8,L),lambda t,p:(t,0,0))],
      scratch_shapes=[pltpu.VMEM((3,256,L),bf16),pltpu.VMEM((4,256,256),f32)]),
      out_shape=[jax.ShapeDtypeStruct((4,L,640),bf16),jax.ShapeDtypeStruct((4,640,L),bf16),jax.ShapeDtypeStruct((4,L,256),bf16),jax.ShapeDtypeStruct((4,256,L),bf16),jax.ShapeDtypeStruct((4,8,L),f32)],
      compiler_params=pltpu.CompilerParams(vmem_limit_bytes=62<<20))(prefix,x,w1,bqkv)
def bwd_kernel(prefix_ref,g_ref,w_ref,proj_ref,projT_ref,ot_ref,lse_ref,gproj_ref,
               zq_ref,zdo_ref,qm_ref,dom_ref,pt_ref,ds_ref,mask_ref,gt_ref,dqt_ref):
    masks(mask_ref,prefix_ref[0])
    gh=dotf(g_ref[...],w_ref[:,512:768]).astype(bf16)
    gt_ref[...]=gh.T
    zq_ref[...]=jnp.zeros_like(zq_ref); zdo_ref[...]=jnp.zeros_like(zdo_ref)
    lane=lax.broadcasted_iota(jnp.int32,(1,256),1)
    for h in range(3):
        zq_ref[h,64+64*h:128+64*h,:]=projT_ref[64*h:64*h+64,:]
        zdo_ref[h,64*h:64*h+64,:]=gt_ref[64+64*h:128+64*h,:]*0.125
        sel=(lane>=64*h)&(lane<64*h+64)
        qm_ref[h]=jnp.where(sel,proj_ref[:,0:256],0)
        sel2=(lane>=64*h+64)&(lane<64*h+128)
        dom_ref[h]=jnp.where(sel2,gh,0)
    for h in range(3):
        d=jnp.sum(gt_ref[64+64*h:128+64*h,:].astype(f32)*ot_ref[64+64*h:128+64*h,:].astype(f32),axis=0,keepdims=True)*0.125
        for qb in range(4):
            nk=NK[qb]; qs=slice(qb*QB,qb*QB+QB)
            st=dotf(proj_ref[:nk,128:384],zq_ref[h,:,qs])
            st=masked(st,qb,mask_ref)
            p=jnp.exp2(st*C2-lse_ref[h:h+1,qs])
            dp=dotf(proj_ref[:nk,384:640],zdo_ref[h,:,qs])
            ds=(p*(dp-d[:,qs])).astype(bf16)
            pt_ref[h,:nk,qs]=p.astype(bf16)
            ds_ref[h,:nk,qs]=ds
            dqt_ref[64*h:64*h+64,qs]=dotf(projT_ref[192+64*h:256+64*h,:nk],ds).astype(bf16)
    gproj_ref[:,0:192]=dqt_ref[...].T
    for (k0,k1,q0) in ((0,512,0),(512,768,512),(768,1024,768)):
        dk=jnp.zeros((k1-k0,256),f32); dv=jnp.zeros((k1-k0,256),f32)
        for h in range(3):
            dk=dk+dotf(ds_ref[h,k0:k1,q0:],qm_ref[h,q0:,:])
            dv=dv+dotf(pt_ref[h,k0:k1,q0:],dom_ref[h,q0:,:])
        gproj_ref[k0:k1,192:384]=dk[:,0:192].astype(bf16)
        gproj_ref[k0:k1,384:576]=dv[:,64:256].astype(bf16)
    gproj_ref[:,576:640]=jnp.zeros((L,64),bf16)
def attn_bwd(prefix,g,w1,proj,projT,ot,lse):
    sq=pl.squeezed
    sp=lambda *s: pl.BlockSpec((sq,)+s,lambda t,p:(t,0,0))
    return pl.pallas_call(functools.partial(bwd_kernel),grid_spec=pltpu.PrefetchScalarGridSpec(num_scalar_prefetch=1,grid=(4,),
      in_specs=[pl.BlockSpec((L,768),lambda t,p:(0,0)),sp(768,768),sp(L,640),sp(640,L),sp(256,L),sp(8,L)],
      out_specs=sp(L,640),
      scratch_shapes=[pltpu.VMEM((3,256,L),bf16),pltpu.VMEM((3,256,L),bf16),pltpu.VMEM((3,L,256),bf16),pltpu.VMEM((3,L,256),bf16),pltpu.VMEM((3,L,L),bf16),pltpu.VMEM((3,L,L),bf16),pltpu.VMEM((4,256,256),f32),pltpu.VMEM((256,L),bf16),pltpu.VMEM((192,L),bf16)]),
      out_shape=jax.ShapeDtypeStruct((4,L,640),bf16),
      compiler_params=pltpu.CompilerParams(vmem_limit_bytes=62<<20))(prefix,g,w1,proj,projT,ot,lse)
MESH=pl.DeviceIdType.MESH
class Place:
    def __init__(self):
        dp=lax.axis_index("dp"); t=lax.axis_index("tensor")
        self.dp,self.t=dp,t
        self.z,self.x,self.y,self.c=dp//2,dp%2,t//2,t%2
    def peer(self,dim,j=1):
        return {'x':lambda:(self.dp^1,self.t),'z':lambda:(self.dp^(2*j),self.t),'y':lambda:(self.dp,self.t^2),'c':lambda:(self.dp,self.t^1)}[dim]()
    def peers_all(self):
        return [self.peer('x'),self.peer('y'),self.peer('c'),self.peer('z',1),self.peer('z',2),self.peer('z',3),(self.dp,self.t^3)]
def barrier(peers):
    b=pltpu.get_barrier_semaphore()
    for p in peers: pl.semaphore_signal(b,inc=1,device_id=p,device_id_type=MESH)
    pl.semaphore_wait(b,len(peers))
class Sems:
    def __init__(self,send,recv): self.s,self.r,self.n=send,recv,0
    def take(self):
        i=self.n; self.n+=1
        return self.s.at[i],self.r.at[i]
def rcopy(src,dst,sems,dev):
    a,b=sems.take()
    return pltpu.make_async_remote_copy(src_ref=src,dst_ref=dst,send_sem=a,recv_sem=b,device_id=dev,device_id_type=MESH)
def local(src,dst,sem):
    k=pltpu.make_async_copy(src,dst,sem); k.start(); return k
def exchange(pc,src,dst,sems):
    out=[]
    for j in (2,3,1):
        p=(pc.dp,pc.t^j)
        k=rcopy(src.at[pc.t^j],dst.at[pc.t],sems,p); k.start(); out.append(k)
    return out
HBM=pl.BlockSpec(memory_space=pltpu.HBM); VM=pl.BlockSpec(memory_space=pltpu.VMEM)
def point(steps, k, h):
    for kk in range(4):
        todo = steps.get((kk, h))
        if todo:
            @pl.when(k == kk)
            def _(todo=todo):
                for step in todo:
                    step()


def add_into(dst, src, n, pick_dst, pick_src):
    def body(j, _):
        a, b = pick_dst(j), pick_src(j)
        dst[a] = (dst[a].astype(f32) + src[b].astype(f32)).astype(bf16)
        return 0
    lax.fori_loop(0, n, body, 0)


class Reduce:
    def __init__(self, pc, kind, d_ref, half, lc, rc, r1, r2, r3, sems, lsem):
        self.pc, self.kind, self.lc, self.rc, self.r1, self.r2, self.r3 = pc, kind, lc, rc, r1, r2, r3
        rows = pl.ds(48 * half, 48)
        self.own = pltpu.make_async_copy(d_ref.at[:, pc.c, :, :, rows], lc, lsem)
        self.q0 = rcopy(d_ref.at[:, 1 - pc.c, :, :, rows], rc, sems, pc.peer("c"))
        if kind == "x":
            self.q1 = rcopy(lc.at[:, :, 1 - pc.x], r1, sems, pc.peer("x"))
            self.q2 = [rcopy(lc.at[:, pc.z ^ j, pc.x], r2.at[j - 1], sems, pc.peer("z", j)) for j in (3, 2, 1)]
            self.q3 = [rcopy(lc.at[1 - pc.y, pc.z, pc.x], r3.at[0], sems, pc.peer("y"))]
        else:
            self.q1 = rcopy(lc.at[1 - pc.y], r1, sems, pc.peer("y"))
            self.q2 = [rcopy(lc.at[pc.y, :, 1 - pc.x], r2, sems, pc.peer("x"))]
            self.q3 = [rcopy(lc.at[pc.y, pc.z ^ j, pc.x], r3.at[j - 1], sems, pc.peer("z", j)) for j in (3, 2, 1)]

    def s0(self):
        self.own.start()
        self.q0.start()

    def s1(self):
        self.own.wait()
        self.q0.wait_recv()
        at = lambda j: (j // 8, (j // 2) % 4, j % 2)
        add_into(self.lc, self.rc, 16, at, at)
        self.q1.start()

    def s2(self):
        self.q1.wait_recv()
        if self.kind == "x":
            add_into(self.lc, self.r1, 8, lambda j: (j // 4, j % 4, self.pc.x), lambda j: (j // 4, j % 4))
        else:
            add_into(self.lc, self.r1, 8, lambda j: (self.pc.y, j // 2, j % 2), lambda j: (j // 2, j % 2))
        for q in self.q2:
            q.start()

    def s3(self):
        pc = self.pc
        for q in self.q2:
            q.wait_recv()
        if self.kind == "x":
            for y in range(2):
                at = (y, pc.z, pc.x)
                total = (self.lc[at].astype(f32) + self.r2[0, y].astype(f32)) + (self.r2[1, y].astype(f32) + self.r2[2, y].astype(f32))
                self.lc[at] = total.astype(bf16)
        else:
            add_into(self.lc, self.r2, 4, lambda j: (pc.y, j, pc.x), lambda j: (j,))
        for q in self.q3:
            q.start()

    def s4(self, out_ref, rows):
        pc = self.pc
        for q in self.q3:
            q.wait_recv()
        total = self.lc[pc.y, pc.z, pc.x].astype(f32) + self.r3[0].astype(f32)
        if self.kind == "y":
            total = total + (self.r3[1].astype(f32) + self.r3[2].astype(f32))
        out_ref[rows] = total

    def end(self):
        for q in [self.q0, self.q1] + self.q2 + self.q3:
            q.wait_send()


N_C = 4 * 6 + 3 + 3 + 8 + 6 + 6


def back_kernel(
    prefix_ref, x_ref, g_ref, gf_ref, w_ref, proj_ref, projT_ref, ot_ref, lse_ref, dout_ref, d_ref, v_ref,
    gs_ref, vs_ref, xo_ref,
    xT, gl, dxa, w_b, proj_b, projT_b, ot_b, lse_b, dout_b,
    zq, zdo, qm, dom, pt, ds, mask_ref, gt, dqt, dkb, dvb, gproj,
    lc, rc, yx1, yx2, yx3, yy1, yy2, yy3, dwb, cr, yr, xr, zr, vb, vr, xst, ss, rs, ls, ins,
):
    pc = Place()
    sems = Sems(ss, rs)
    w1 = w_ref.at[0]
    lane = lax.broadcasted_iota(jnp.int32, (1, 256), 1)

    def loads(k, slot):
        t = pc.t ^ (3 - k)
        pairs = [
            (w1.at[t // 2, t % 2], w_b), (proj_ref.at[t], proj_b), (projT_ref.at[t], projT_b),
            (ot_ref.at[t], ot_b), (lse_ref.at[t], lse_b), (dout_ref.at[t], dout_b),
        ]
        return [pltpu.make_async_copy(a, b.at[slot], ins.at[slot, n]) for n, (a, b) in enumerate(pairs)]

    first = loads(0, 0)
    for q in first:
        q.start()
    l_x = local(x_ref, xst, ls.at[4])
    l_g = local(g_ref, gl, ls.at[5])
    l_f = local(gf_ref, dxa, ls.at[6])
    barrier(pc.peers_all())
    red = []
    for n, (kind, g, i) in enumerate((("y", 1, 0), ("x", 1, 1), ("y", 0, 0), ("x", 0, 1))):
        r1, r2, r3 = [r.at[n // 2] for r in ((yy1, yy2, yy3) if kind == "y" else (yx1, yx2, yx3))]
        red.append(Reduce(pc, kind, d_ref.at[g], i, lc.at[n], rc.at[n], r1, r2, r3, sems, ls.at[n]))
        red[n].s0()
    q_c0 = rcopy(dwb.at[0], cr.at[0], sems, pc.peer("c"))
    q_y = rcopy(dwb.at[1], yr, sems, pc.peer("y"))
    q_c1 = rcopy(dwb.at[2], cr.at[1], sems, pc.peer("c"))
    half = [pl.ds(48 * i, 48) for i in range(2)]
    q_x = [rcopy(dwb.at[3, pc.z ^ j, 1 - pc.x, half[i]], xr.at[i, pc.z ^ j], sems, pc.peer("x")) for i in range(2) for j in (3, 2, 1, 0)]
    q_z = [rcopy(dwb.at[3, pc.z ^ j, pc.x, half[i]], zr.at[i, j - 1], sems, pc.peer("z", j)) for i in range(2) for j in (3, 2, 1)]
    v_q = [rcopy(vb.at[n], vr.at[n], sems, pc.peer(dim)) for n, dim in enumerate("cxy")]
    v_z = [rcopy(vb.at[3], vr.at[2 + j], sems, pc.peer("z", j)) for j in (3, 2, 1)]

    def vstep(n):
        v_q[n].wait_recv()
        vb[n + 1] = vb[n] + vr[n]
        for q in [v_q[n + 1]] if n < 2 else v_z:
            q.start()

    steps = {
        (0, 0): [red[0].s1], (0, 1): [red[1].s1], (0, 2): [red[2].s1], (0, 3): [red[3].s1],
        (1, 1): [red[1].s2], (1, 2): [red[0].s2], (2, 1): [red[3].s2, red[2].s2], (2, 2): [red[1].s3],
        (3, 0): [red[0].s3], (3, 1): [red[3].s3], (3, 2): [red[2].s3],
    }
    masks(mask_ref, prefix_ref[pc.t])
    zq[...] = jnp.zeros_like(zq)
    zdo[...] = jnp.zeros_like(zdo)
    gproj[:, 576:640] = jnp.zeros((L, 64), bf16)
    vb[0] = v_ref[...]
    l_x.wait()
    xT[...] = xst[...].reshape(L, 768).T
    l_g.wait()
    l_f.wait()

    def chip_sum(i, z, x):
        return dwb[3, z, x, half[i]].astype(f32) + (cr[1, z, x, half[i]].astype(f32) + yr[z, x, half[i]].astype(f32))

    def group(k, _):
        slot = k % 2
        for q in loads(k, slot):
            q.wait()

        @pl.when(k < 3)
        def _():
            for q in loads(k + 1, 1 - slot):
                q.start()

        t = pc.t ^ (3 - k)
        w, pj, pjT, o_t, lse = w_b.at[slot], proj_b.at[slot], projT_b.at[slot], ot_b.at[slot], lse_b.at[slot]
        gh = dotf(gl[...], w[...].reshape(768, 768)[:, 512:768]).astype(bf16)
        gt[...] = gh.T
        for h in range(3):
            point(steps, k, h)
            own = slice(64 + 64 * h, 128 + 64 * h)
            zq[h, own, :] = pjT[64 * h : 64 * h + 64, :]
            zdo[h, 64 * h : 64 * h + 64, :] = gt[own, :] * 0.125
            qm[...] = jnp.where((lane >= 64 * h) & (lane < 64 * h + 64), pj[:, 0:256], 0)
            dom[...] = jnp.where((lane >= 64 * h + 64) & (lane < 64 * h + 128), gh, 0)
            d = jnp.sum(gt[own, :].astype(f32) * o_t[own, :].astype(f32), axis=0, keepdims=True) * 0.125
            for qb in range(4):
                nk = NK[qb]
                qs = slice(qb * QB, qb * QB + QB)
                st = masked(dotf(pj[:nk, 128:384], zq[h, :, qs]), qb, mask_ref)
                p = jnp.exp2(st * C2 - lse[h : h + 1, qs])
                dp = dotf(pj[:nk, 384:640], zdo[h, :, qs])
                dsv = (p * (dp - d[:, qs])).astype(bf16)
                pt[:nk, qs] = p.astype(bf16)
                ds[:nk, qs] = dsv
                dqt[64 * h : 64 * h + 64, qs] = dotf(pjT[192 + 64 * h : 256 + 64 * h, :nk], dsv).astype(bf16)
            for k0, k1, q0 in ((0, 512, 0), (512, 768, 512), (768, 1024, 768)):
                dk = dotf(ds[k0:k1, q0:], qm[q0:, :]).astype(bf16)
                dv = dotf(pt[k0:k1, q0:], dom[q0:, :]).astype(bf16)
                dkb[k0:k1] = dk if h == 0 else dkb[k0:k1] + dk
                dvb[k0:k1] = dv if h == 0 else dvb[k0:k1] + dv
        point(steps, k, 3)
        gproj[:, 0:192] = dqt[...].T
        gproj[:, 192:384] = dkb[:, 0:192]
        gproj[:, 384:576] = dvb[:, 64:256]
        vb[0, pl.ds(16 + 2 * t, 1), 0:256] = jnp.sum(gproj[:, 0:256].astype(f32), axis=0, keepdims=True)
        vb[0, pl.ds(17 + 2 * t, 1), 0:256] = jnp.sum(gproj[:, 384:640].astype(f32), axis=0, keepdims=True)

        @pl.when(k == 3)
        def _():
            v_q[0].start()

        dw = dotf(xT[...], gproj[...])
        do = dout_b[slot].astype(f32)
        shape = lambda a: a.astype(bf16).reshape(4, 2, 96, a.shape[1])
        dwb[k, :, :, :, 0:512] = shape(dw[:, 0:512])
        dwb[k, :, :, :, 512:640] = shape(dw[:, 512:640] + do[:, 0:128])
        dwb[k, :, :, :, 640:768] = shape(do[:, 128:256])

        @pl.when(k == 0)
        def _():
            q_c0.start()

        @pl.when(k == 1)
        def _():
            q_c0.wait_recv()
            add_into(dwb.at[1], cr.at[0], 8, lambda j: (j // 2, j % 2), lambda j: (j // 2, j % 2))
            q_y.start()

        @pl.when(k == 2)
        def _():
            q_c1.start()

        @pl.when(k == 3)
        def _():
            vstep(0)
            q_c1.wait_recv()
            q_y.wait_recv()
            for n, q in enumerate(q_x):
                i, z, x = n // 4, pc.z ^ (3 - n % 4), 1 - pc.x
                dwb[3, z, x, half[i]] = chip_sum(i, z, x).astype(bf16)
                q.start()

        dxa[...] += dot_nt(gproj[...], w[...].reshape(768, 768)[:, 0:640])
        return 0

    lax.fori_loop(0, 4, group, 0)
    vstep(1)
    xst[...] = dxa[...].astype(bf16).reshape(4, 256, 768)
    xx = exchange(pc, xst, xo_ref, sems)
    l_o = local(xst.at[pc.t], xo_ref.at[pc.t], ls.at[7])
    vstep(2)

    def arrive(n, j):
        i, z = n // 4, pc.z ^ j
        q_x[n].wait_recv()
        dwb[3, z, pc.x, half[i]] = (chip_sum(i, z, pc.x) + xr[i, z].astype(f32)).astype(bf16)

    for n in range(8):
        j = 3 - n % 4
        arrive(n, j)
        if j:
            q_z[n - n // 4].start()
        if n == 1:
            red[0].s4(gs_ref.at[2], slice(0, 48))
        if n == 3:
            red[2].s4(gs_ref.at[1], slice(0, 48))
    red[1].s4(gs_ref.at[2], slice(48, 96))
    red[3].s4(gs_ref.at[1], slice(48, 96))
    for q in v_z:
        q.wait_recv()
    vs_ref[...] = (vb[3] + vr[3]) + (vr[4] + vr[5])
    for i in range(2):
        for q in q_z[3 * i : 3 * i + 3]:
            q.wait_recv()
        gs_ref[0, 48 * i : 48 * i + 48] = (dwb[3, pc.z, pc.x, half[i]].astype(f32) + zr[i, 0].astype(f32)) + (zr[i, 1].astype(f32) + zr[i, 2].astype(f32))
    l_o.wait()
    for q in xx:
        q.wait()
    for r in red:
        r.end()
    for q in [q_c0, q_y, q_c1] + q_x + q_z + v_q + v_z:
        q.wait_send()


def back(prefix, x, g1low, g1, g, proj, projT, ot, lse, doutw, d, v):
    v_ = pltpu.VMEM
    dma = pltpu.SemaphoreType.DMA
    sd = jax.ShapeDtypeStruct
    return pl.pallas_call(
        back_kernel,
        out_shape=[sd((3, 96, 768), f32), sd((24, 768), f32), sd((4, 256, 768), bf16)],
        in_specs=[pl.BlockSpec(memory_space=pltpu.SMEM)] + [HBM] * 10 + [VM],
        out_specs=[VM, VM, HBM],
        scratch_shapes=[
            v_((768, L), bf16), v_((L, 768), bf16), v_((L, 768), f32),
            v_((2, 4, 2, 96, 768), bf16), v_((2, L, 640), bf16), v_((2, 640, L), bf16), v_((2, 256, L), bf16), v_((2, 8, L), f32), v_((2, 768, 256), bf16),
            v_((3, 256, L), bf16), v_((3, 256, L), bf16), v_((L, 256), bf16), v_((L, 256), bf16), v_((L, L), bf16), v_((L, L), bf16),
            v_((4, 256, 256), f32), v_((256, L), bf16), v_((192, L), bf16), v_((L, 256), bf16), v_((L, 256), bf16), v_((L, 640), bf16),
            v_((4, 2, 4, 2, 48, 768), bf16), v_((4, 2, 4, 2, 48, 768), bf16),
            v_((2, 2, 4, 48, 768), bf16), v_((2, 3, 2, 48, 768), bf16), v_((2, 1, 48, 768), bf16),
            v_((2, 4, 2, 48, 768), bf16), v_((2, 4, 48, 768), bf16), v_((2, 3, 48, 768), bf16),
            v_((4, 4, 2, 96, 768), bf16), v_((2, 4, 2, 96, 768), bf16), v_((4, 2, 96, 768), bf16), v_((2, 4, 48, 768), bf16), v_((2, 3, 48, 768), bf16),
            v_((4, 24, 768), f32), v_((6, 24, 768), f32), v_((4, 256, 768), bf16),
            dma((N_C,)), dma((N_C,)), dma((8,)), dma((2, 6)),
        ],
        compiler_params=pltpu.CompilerParams(collective_id=1, has_side_effects=True, vmem_limit_bytes=67043328),
    )(prefix, x, g1low, g1, g, proj, projT, ot, lse, doutw, d, v)


class Gather:
    def __init__(self, pc, src, dst, rows, order, sems):
        self.pc, self.src, self.dst, self.rows, self.order, self.sems = pc, src, dst, rows, order, sems
        self.full, self.sent, self.core = set(), [], []
        self.plan()

    def at(self, over, full):
        pc = self.pc
        ix = {d: over.get(d, slice(None) if d in full else getattr(pc, d)) for d in "yzx"}
        return self.dst.at[(ix["y"], pc.c, ix["z"], ix["x"]) + ((pl.ds(*self.rows),) if self.rows else ())]

    def plan(self):
        pc = self.pc
        src = self.src.at[pl.ds(*self.rows)] if self.rows else self.src
        mine = self.at({}, set())
        self.core.append(rcopy(src, mine, self.sems, pc.peer("c")))
        self.phases = []
        full = set()
        for d in self.order:
            ks = []
            for j in (1, 2, 3) if d == "z" else (1,):
                here = self.at({}, full)
                ks.append(rcopy(here if full else src, here, self.sems, pc.peer(d, j)))
                there = self.at({d: getattr(pc, d) ^ j}, full)
                self.core.append(rcopy(there, there, self.sems, pc.peer("c")))
            self.phases.append(ks)
            full = full | {d}
        self.first = [1]
        for ks in self.phases:
            self.first.append(self.first[-1] + len(ks))

    def start(self):
        self.core[0].start()
        for k in self.phases[0]:
            k.start()

    def arrive(self, p):
        for n, k in enumerate(self.phases[p]):
            k.wait_recv()
            self.core[self.first[p] + n].start()

    def next(self, p):
        self.arrive(p - 1)
        for k in self.phases[p]:
            k.start()

    def from_core(self, a, b):
        for k in self.core[a:b]:
            k.wait_recv()

    def end(self):
        for k in self.core + sum(self.phases, []):
            k.wait_send()


class Slabs:
    def __init__(self, pc, src, dst, kind, rows, sems):
        src = src.at[rows]
        at = lambda y, z, x: dst.at[y, pc.c, z, x, rows]
        every = slice(None)
        mine, other = pc.y, 1 - pc.y
        self.copy, self.fwd = {}, {}

        def add(name, dim, pairs, got):
            self.copy[name] = [rcopy(a, b, sems, pc.peer(dim, j)) for j, a, b in pairs]
            if got is not None:
                self.fwd[name] = rcopy(got, got, sems, pc.peer("c"))

        slab = at(mine, every, pc.x)
        add("z", "z", [(j, src, at(mine, pc.z, pc.x)) for j in (3, 2, 1)], slab)
        if kind in "AB":
            add("x", "x", [(1, slab, slab)], at(mine, every, 1 - pc.x))
        if kind == "A":
            whole = at(mine, every, every)
            add("y", "y", [(1, whole, whole)], at(other, every, every))
        if kind in "CE":
            add("y", "y", [(1, slab, slab)], at(other, every, pc.x))
        if kind == "E":
            whole = at(every, every, pc.x)
            add("x", "x", [(1, whole, whole)], at(every, every, 1 - pc.x))
        if kind == "B":
            add("y", "y", [(1, src, at(mine, pc.z, pc.x))], None)
            one, slab2 = at(other, pc.z, pc.x), at(other, every, pc.x)
            add("z2", "z", [(j, one, one) for j in (3, 2, 1)], slab2)
            add("x2", "x", [(1, slab2, slab2)], at(other, every, 1 - pc.x))

    def start(self, name):
        for k in self.copy[name]:
            k.start()

    def arrive(self, name):
        for k in self.copy[name]:
            k.wait_recv()
        if name in self.fwd:
            self.fwd[name].start()

    def from_core(self, *names):
        for n in names:
            self.fwd[n].wait_recv()

    def end(self):
        for ks in self.copy.values():
            for k in ks:
                k.wait_send()
        for k in self.fwd.values():
            k.wait_send()


N_A = 3 * 8 + 2 * 13 + 6 + 11 + 3


def front_kernel(
    prefix_ref, s_ref, h_ref, b_ref,
    g_ref, x_ref, vec_ref, proj_ref, projT_ref, heads_ref, ot_ref, lse_ref,
    bv, sv, xv, wv, proj_b, projT_b, heads_b, ot_b, lse_b, zq, mask_ref, ss, rs, ls, os_,
):
    pc = Place()
    sems = Sems(ss, rs)
    own = (pc.y, pc.c, pc.z, pc.x)
    l_s = local(s_ref, sv, ls.at[0])
    l_h = local(h_ref.at[pc.t], xv.at[pc.t], ls.at[1])
    l_b = local(b_ref, bv.at[own], ls.at[9])
    barrier(pc.peers_all())
    bias = Gather(pc, b_ref, bv, None, "zxy", sems)
    w1a, w1b, w2a, w2b, w3a, w3b = every = [
        Slabs(pc, s_ref.at[n // 2], g_ref.at[n // 2], kind, rows, sems)
        for n, (kind, rows) in enumerate(zip("ABABCE", [pl.ds(0, 48), pl.ds(48, 48)] * 3))
    ]
    bias.start()
    w1b.start("y")
    w1a.start("z")
    w1b.start("z")
    hx = exchange(pc, h_ref, xv, sems)
    w2b.start("y")
    l_s.wait()
    l_g = [local(sv.at[g], g_ref.at[g].at[own], ls.at[3 + g]) for g in range(3)]
    masks(mask_ref, prefix_ref[pc.t])
    zq[...] = jnp.zeros_like(zq)
    ot_b[...] = jnp.zeros_like(ot_b)
    for q in l_g:
        q.wait()
    l_b.wait()
    w1b.arrive("y")
    w1b.start("z2")
    bias.next(1)
    w1a.arrive("z")
    w1a.start("x")
    bias.next(2)
    w1b.arrive("z")
    w1b.start("x")
    w1a.arrive("x")
    w1a.start("y")
    w1b.arrive("z2")
    w1b.start("x2")
    w1b.arrive("x")
    for g in (w2a, w3b, w2b):
        g.start("z")
    bias.arrive(2)
    bias.from_core(0, len(bias.core))
    l_h.wait()
    for q in hx:
        q.wait_recv()
    l_x = local(xv, x_ref, ls.at[7])

    def load(k, slot):
        t = pc.t ^ k
        return pltpu.make_async_copy(g_ref.at[0, t // 2, t % 2], wv.at[slot], ls.at[8])

    def go(g, got, then=None, then_g=None):
        def step():
            g.arrive(got)
            if then:
                (then_g or g).start(then)
        return step

    steps = {
        (0, 0): [go(w2b, "y", "z2"), lambda: w3a.start("z")],
        (0, 2): [go(w2a, "z", "x"), lambda: w1a.from_core("z", "x"), lambda: w1b.from_core("z", "x"), lambda: load(1, 1).start()],
        (0, 3): [go(w1b, "x2")],
        (1, 1): [go(w3b, "z", "y")],
        (1, 2): [go(w2a, "x", "y")],
        (1, 3): [go(w1a, "y"), lambda: load(2, 0).start(), go(w2b, "z", "x")],
        (2, 1): [go(w3b, "y", "x")],
        (2, 2): [lambda: w1a.from_core("y"), lambda: w1b.from_core("z2", "x2"), lambda: load(3, 1).start(), go(w2b, "z2", "x2")],
        (3, 0): [go(w2b, "x"), go(w3a, "z", "y")],
        (3, 2): [go(w2a, "y")],
    }
    load(0, 0).start()

    def outs(k, slot):
        t = pc.t ^ k
        pairs = [(proj_b, proj_ref), (projT_b, projT_ref), (heads_b, heads_ref), (ot_b, ot_ref), (lse_b, lse_ref)]
        return [pltpu.make_async_copy(a.at[slot], b.at[t], os_.at[slot, n]) for n, (a, b) in enumerate(pairs)]

    def group(k, _):
        slot = k % 2
        t = pc.t ^ k
        load(k, slot).wait()

        @pl.when(k >= 2)
        def _():
            for q in outs(k - 2, slot):
                q.wait()

        row = jnp.zeros((8, 256), f32)
        for i in range(8):
            piece = bv[(i // 2) % 2, i % 2, t, i // 4, 0:8, :]
            row = row + pltpu.roll(jnp.concatenate([piece, jnp.zeros((8, 128), f32)], 1), 24 * i, 1)
        brow = jnp.concatenate([row[0:1], jnp.zeros((1, 128), f32), row[1:2]], 1)
        pj, pjT, ot, lse = proj_b.at[slot], projT_b.at[slot], ot_b.at[slot], lse_b.at[slot]
        proj = (dotf(xv[...].reshape(L, 768), wv[slot].reshape(768, 768)[:, :640]) + brow).astype(bf16)
        pj[...] = proj
        pjT[...] = proj.T
        for h in range(3):
            point(steps, k, h)
            zq[h, 64 + 64 * h : 128 + 64 * h, :] = pjT[64 * h : 64 * h + 64, :]
            for qb in range(4):
                nk = NK[qb]
                qs = slice(qb * QB, qb * QB + QB)
                st = masked(dotf(pj[:nk, 128:384], zq[h, :, qs]), qb, mask_ref)
                m = jnp.max(st, axis=0, keepdims=True)
                p = jnp.exp2((st - m) * C2)
                l = jnp.sum(p, axis=0, keepdims=True)
                o = dotf(pjT[384 + 64 * h : 448 + 64 * h, :nk], p.astype(bf16))
                ot[64 + 64 * h : 128 + 64 * h, qs] = (o / l).astype(bf16)
                lse[h : h + 1, qs] = m * C2 + jnp.log2(l)
        point(steps, k, 3)
        heads_b[slot] = ot[...].T
        for q in outs(k, slot):
            q.start()
        return 0

    lax.fori_loop(0, 4, group, 0)
    tiles = [jnp.zeros((16, 128), f32) for _ in range(6)]
    lane = lax.broadcasted_iota(jnp.int32, (1, 128), 1)
    for i in range(32):
        z, x, y, c = i // 8, (i // 4) % 2, (i // 2) % 2, i % 2
        j, r = (24 * i) // 128, (24 * i) % 128
        piece = pltpu.roll(bv[y, c, z, x], r, 1) if r else bv[y, c, z, x]
        tiles[j] = tiles[j] + (jnp.where(lane >= r, piece, 0.0) if r > 104 else piece)
        if r > 104:
            tiles[j + 1] = tiles[j + 1] + jnp.where(lane < r, piece, 0.0)
    for j in range(6):
        vec_ref[:, 128 * j : 128 * j + 128] = tiles[j]
    w3b.arrive("x")
    w2b.arrive("x2")
    w3a.arrive("y")
    w2a.from_core("z", "x", "y")
    w2b.from_core("z", "x", "z2", "x2")
    w3a.from_core("z", "y")
    w3b.from_core("z", "y", "x")
    for q in hx:
        q.wait_send()
    l_x.wait()
    for k in (2, 3):
        for q in outs(k, k % 2):
            q.wait()
    bias.end()
    for g in every:
        g.end()


def front(prefix, s, h, b):
    v_ = pltpu.VMEM
    dma = pltpu.SemaphoreType.DMA
    sd = jax.ShapeDtypeStruct
    return pl.pallas_call(
        front_kernel,
        out_shape=[
            sd((3, 2, 2, 4, 2, 96, 768), bf16), sd((4, 256, 768), bf16), sd((16, 768), f32),
            sd((4, L, 640), bf16), sd((4, 640, L), bf16), sd((4, L, 256), bf16), sd((4, 256, L), bf16), sd((4, 8, L), f32),
        ],
        in_specs=[pl.BlockSpec(memory_space=pltpu.SMEM)] + [HBM] * 2 + [VM],
        out_specs=[HBM] * 2 + [VM] + [HBM] * 5,
        scratch_shapes=[
            v_((2, 2, 4, 2, 16, 128), f32), v_((3, 96, 768), bf16), v_((4, 256, 768), bf16), v_((2, 4, 2, 96, 768), bf16),
            v_((2, L, 640), bf16), v_((2, 640, L), bf16), v_((2, L, 256), bf16), v_((2, 256, L), bf16), v_((2, 8, L), f32),
            v_((3, 256, L), bf16), v_((4, 256, 256), f32),
            dma((N_A,)), dma((N_A,)), dma((10,)), dma((2, 5)),
        ],
        compiler_params=pltpu.CompilerParams(collective_id=0, has_side_effects=True, vmem_limit_bytes=67043328),
    )(prefix, s, h, b)


EPSILON = 1e-12


def gelu_pair(v):
    cdf = 0.5 + 0.5 * lax.erf(v * math.sqrt(0.5))
    pdf = jnp.exp2(v * v * (-0.5 * math.log2(math.e))) * (1.0 / math.sqrt(2.0 * math.pi))
    return v * cdf, cdf + v * pdf


def row_mean(a):
    return jnp.sum(a, axis=-1, keepdims=True) * (1.0 / 768.0)


def mid_kernel(
    x_ref, c_ref, heads_ref, g_ref, vec_ref,
    oo_ref, g1_ref, g1low_ref, dout_ref, d_ref, v_ref,
    xv, cv, hv, wo, w2, w3, xhat, inv, low, act, gd, acc, glow, lowT, gT, stage, dst, ls, ds_, ss, rs,
):
    pc = Place()
    sems = Sems(ss, rs)
    l_x = local(x_ref, xv, ls.at[0])
    l_h = local(heads_ref, hv, ls.at[1])
    l_wo = [local(g_ref.at[0, y, c, :, :, :, pl.ds(512, 256)], wo.at[2 * y + c], ls.at[2 + 2 * y + c]) for y in range(2) for c in range(2)]
    l_w2 = local(g_ref.at[1], w2, ls.at[6])
    ra, rb = pl.ds(0, 48), pl.ds(48, 48)
    parts = lambda r: (r.at[:, :, :, pc.x, ra], r.at[:, :, :, :, rb])
    l_w3 = [local(a, b, ls.at[n]) for n, a, b in zip((7, 9), parts(g_ref.at[2]), parts(w3))]
    l_c = local(c_ref.at[pc.t], cv.at[pc.t], ls.at[8])
    barrier([(pc.dp, pc.t ^ j) for j in (1, 2, 3)] + [pc.peer("x")])
    came = w3.at[:, pc.c, :, 1 - pc.x, ra]
    wx = rcopy(g_ref.at[2, :, pc.c, :, pc.x, ra], w3.at[:, pc.c, :, pc.x, ra], sems, pc.peer("x"))
    wc = rcopy(came, came, sems, pc.peer("c"))
    wx.start()
    cx = exchange(pc, c_ref, cv, sems)
    row = lambda n: vec_ref[n : n + 1, :]
    v_ref[...] = jnp.zeros_like(v_ref)

    def add_row(n, a):
        v_ref[n : n + 1, :] += jnp.sum(a, axis=0, keepdims=True)

    for q in [l_x, l_h] + l_wo:
        q.wait()

    def first(b, _):
        rows = pl.ds(pl.multiple_of(b * 256, 256), 256)
        r = xv[b].astype(f32) + row(2)
        for t in range(4):
            r = r + dot_nt(hv[t, rows, :], wo[t].reshape(768, 256))
        center = r - row_mean(r)
        iv = lax.rsqrt(row_mean(center * center) + EPSILON)
        xh = center * iv
        xhat[rows, :] = xh
        inv[rows, :] = jnp.broadcast_to(iv, (256, 128))
        normed = xh * row(10) + row(8)
        low[rows, :] = normed.astype(bf16)
        acc[rows, :] = normed + row(7)
        return 0

    lax.fori_loop(0, 4, first, 0)
    l_w2.wait()

    def up(n, _):
        t, b = n // 4, n % 4
        rows = pl.ds(pl.multiple_of(b * 256, 256), 256)
        pre = dotf(low[rows, :], w2[t // 2, t % 2].reshape(768, 768)) + vec_ref[pl.ds(3 + t, 1), :]
        a, d = gelu_pair(pre)
        act[t, rows, :] = a.astype(bf16)
        gd[t, rows, :] = d.astype(bf16)

        @pl.when(n == 13)
        def _():
            wx.wait_recv()
            wc.start()

        return 0

    lax.fori_loop(0, 16, up, 0)
    wc.wait_recv()
    for q in l_w3:
        q.wait()

    def branch(b, _):
        rows = pl.ds(pl.multiple_of(b * 256, 256), 256)
        total = acc[rows, :]
        for t in range(4):
            total = total + dot_nt(act[t, rows, :], w3[t // 2, t % 2].reshape(768, 768))
        acc[rows, :] = total
        return 0

    lax.fori_loop(0, 4, branch, 0)
    for q in (wx, wc):
        q.wait_send()
    l_c.wait()
    for q in cx:
        q.wait()

    def second(b, _):
        rows = pl.ds(pl.multiple_of(b * 256, 256), 256)
        r = acc[rows, :]
        center = r - row_mean(r)
        iv = lax.rsqrt(row_mean(center * center) + EPSILON)
        xh = center * iv
        stage[b] = (xh * row(11) + row(9)).astype(bf16)
        ct = cv[b].astype(f32)
        e = ct * row(11)
        g2 = (e - row_mean(e) - xh * row_mean(e * xh)) * iv
        acc[rows, :] = g2
        glow[rows, :] = g2.astype(bf16)
        add_row(11, ct * xh)
        add_row(9, ct)
        add_row(7, g2)
        return 0

    lax.fori_loop(0, 4, second, 0)
    ox = exchange(pc, stage, oo_ref, sems)
    l_o = local(stage.at[pc.t], oo_ref.at[pc.t], ls.at[0])
    gT[...] = glow[...].T
    lowT[...] = low[...].T

    def sends(t):
        return [pltpu.make_async_copy(dst.at[t % 2, n], d_ref.at[n, t], ds_.at[t % 2, n]) for n in range(2)]

    def down(t, _):
        wt2, wt3 = w2.at[t // 2, t % 2], w3.at[t // 2, t % 2]

        @pl.when(t >= 2)
        def _():
            for q in sends(t - 2):
                q.wait()

        dst[t % 2, 1] = dotf(gT[...], act[t]).astype(bf16)
        for b in range(4):
            rows = slice(256 * b, 256 * b + 256)
            ga = dotf(glow[rows, :], wt3[...].reshape(768, 768))
            gp = (ga * gd[t, rows, :].astype(f32)).astype(bf16)
            gd[t, rows, :] = gp
            acc[rows, :] += dot_nt(gp, wt2[...].reshape(768, 768))
            v_ref[pl.ds(3 + t, 1), :] += jnp.sum(gp.astype(f32), axis=0, keepdims=True)
        dst[t % 2, 0] = dotf(lowT[...], gd[t]).astype(bf16)
        for q in sends(t):
            q.start()
        return 0

    lax.fori_loop(0, 4, down, 0)

    def last(b, _):
        rows = pl.ds(pl.multiple_of(b * 256, 256), 256)
        gn, xh = acc[rows, :], xhat[rows, :]
        e = gn * row(10)
        g1 = (e - row_mean(e) - xh * row_mean(e * xh)) * inv[rows, 0:1]
        acc[rows, :] = g1
        glow[rows, :] = g1.astype(bf16)
        add_row(10, gn * xh)
        add_row(8, gn)
        add_row(2, g1)
        return 0

    lax.fori_loop(0, 4, last, 0)
    l_g = [local(acc, g1_ref, ls.at[1]), local(glow, g1low_ref, ls.at[2])]
    gT[...] = glow[...].T
    for q in sends(2) + sends(3):
        q.wait()
    for t in range(4):
        dst[t // 2, t % 2, :, 0:256] = dotf(gT[...], hv[t]).astype(bf16)
    l_d = [local(dst.at[t // 2, t % 2, :, pl.ds(0, 256)], dout_ref.at[t], ls.at[3 + t]) for t in range(4)]
    for q in [l_o] + l_g + l_d + ox:
        q.wait()


def mid(xs, cs, heads, g, vec):
    v_ = pltpu.VMEM
    dma = pltpu.SemaphoreType.DMA
    sd = jax.ShapeDtypeStruct
    wt = v_((2, 2, 4, 2, 96, 768), bf16)
    return pl.pallas_call(
        mid_kernel,
        out_shape=[sd((4, 256, 768), bf16), sd((L, 768), f32), sd((L, 768), bf16), sd((4, 768, 256), bf16), sd((2, 4, 768, 768), bf16), sd((24, 768), f32)],
        in_specs=[HBM] * 4 + [VM],
        out_specs=[HBM] * 5 + [VM],
        scratch_shapes=[
            v_((4, 256, 768), bf16), v_((4, 256, 768), bf16), v_((4, L, 256), bf16), v_((4, 4, 2, 96, 256), bf16), wt, wt,
            v_((L, 768), f32), v_((L, 128), f32), v_((L, 768), bf16), v_((4, L, 768), bf16), v_((4, L, 768), bf16), v_((L, 768), f32),
            v_((L, 768), bf16), v_((768, L), bf16), v_((768, L), bf16), v_((4, 256, 768), bf16), v_((2, 2, 768, 768), bf16),
            dma((10,)), dma((2, 2)), dma((8,)), dma((8,)),
        ],
        compiler_params=pltpu.CompilerParams(collective_id=2, has_side_effects=True, vmem_limit_bytes=67043328),
    )(xs, cs, heads, g, vec)


def norm_stats(r):
    center = r - jnp.mean(r, axis=-1, keepdims=True)
    inv = lax.rsqrt(jnp.mean(center * center, axis=-1, keepdims=True) + EPSILON)
    return center * inv, inv


def norm_back(cot, gain, xhat, inv):
    e = cot * gain
    grad = (e - jnp.mean(e, -1, keepdims=True) - xhat * jnp.mean(e * xhat, -1, keepdims=True)) * inv
    return grad, jnp.sum(cot * xhat, 0), jnp.sum(cot, 0)


def middle(x, cot, heads, w1, w2, w3, bias_o, bias_h, bias_d, shift1, shift2, gain1, gain2):
    ein = functools.partial(jnp.einsum, preferred_element_type=f32)
    hid = x.astype(f32)
    resid1 = hid + ein("tpw,tdw->pd", heads, w1[:, :, 512:]) + bias_o
    xhat1, inv1 = norm_stats(resid1)
    normed = xhat1 * gain1 + shift1
    low = normed.astype(bf16)
    pre = ein("pd,tdf->tpf", low, w2) + bias_h[:, None, :]
    act, gelu_back = jax.vjp(lambda v: jax.nn.gelu(v, approximate=False), pre)
    act = act.astype(bf16)
    resid2 = normed + ein("tpf,tdf->pd", act, w3) + bias_d
    xhat2, inv2 = norm_stats(resid2)
    out = (xhat2 * gain2 + shift2).astype(bf16)
    g2, dgain2, dshift2 = norm_back(cot.astype(f32), gain2, xhat2, inv2)
    g2low = g2.astype(bf16)
    d3 = ein("pd,tpf->tdf", g2low, act).astype(bf16)
    gpre = gelu_back(ein("pd,tdf->tpf", g2low, w3))[0].astype(bf16)
    d2 = ein("pd,tpf->tdf", low, gpre).astype(bf16)
    gn = g2 + ein("tpf,tdf->pd", gpre, w2)
    g1, dgain1, dshift1 = norm_back(gn, gain1, xhat1, inv1)
    g1low = g1.astype(bf16)
    dout = ein("pd,tpw->tdw", g1low, heads).astype(bf16)
    dbh = jnp.sum(gpre, 1, dtype=f32)
    return out, g1, g1low, dout, d2, d3, (dgain1, dgain2, dshift1, dshift2, jnp.sum(g1, 0), dbh, jnp.sum(g2, 0))


def on_device(hidden_in, cotangent, prefix, w_qkv, w_out, w_in, w_down, biases, gains):
    rows = w_qkv.shape[0]
    n_t = lax.axis_size("tensor")
    t_me, d_me = lax.axis_index("tensor"), lax.axis_index("dp")
    n_dev = n_t * lax.axis_size("dp")
    s = jnp.stack([jnp.concatenate([w_qkv.reshape(rows, -1), w_out.T], axis=1), w_in, w_down.T])
    vecs = jnp.concatenate([biases, gains], 0)
    width = vecs.shape[1]
    vecs = jnp.pad(vecs, ((0, 4), (0, 128 - width)))
    seqs = lambda a: jnp.transpose(a, (1, 0, 2))
    h, c = seqs(hidden_in), seqs(cotangent)
    my_prefix = lax.dynamic_slice_in_dim(prefix, t_me, 1, 0)
    if lax.axis_size("dp") == 8:
        g, xs, vec, proj, projT, heads, ot, lse = front(prefix, s, h, vecs)
        oo, g1, g1low, doutw, d, v = mid(xs, c, heads, g, vec)
        gs, vs, xx = back(prefix, xs, g1low, g1, g, proj, projT, ot, lse, doutw, d.reshape(2, 2, 2, 4, 2, rows, 768), v)
        qv = vs[16:24, :256].reshape(4, 2, 256)
        vs = jnp.concatenate([qv[:, 0, :192].reshape(1, 768), qv[:, 1, :192].reshape(1, 768), vs[2:16]])
    else:
        ein = functools.partial(jnp.einsum, preferred_element_type=f32)
        g = lax.all_gather(lax.all_gather(s, "dp", axis=1, tiled=True), "tensor", axis=1)
        x = lax.all_to_all(h, "tensor", 0, 0, tiled=True).reshape(1024, 768)
        cot = lax.all_to_all(c, "tensor", 0, 0, tiled=True).reshape(1024, 768)
        b = lax.all_gather(vecs, ("dp", "tensor"), axis=0)
        w1, w2, w3 = [a.reshape(n_t, 768, 768) for a in g]
        vec = b.reshape(n_dev, 16, 128)[:, :12, :width].transpose(1, 0, 2).reshape(12, 768)
        bqkv = jnp.pad(jnp.stack([vec[0].reshape(4, 192), jnp.zeros((4, 192), f32), vec[1].reshape(4, 192)], 1).reshape(4, 1, 576), ((0, 0), (0, 0), (0, 64)))
        proj, projT, heads, ot, lse = attn_fwd(my_prefix, x, w1, bqkv)
        out, g1, g1low, doutw, d2, d3, small = middle(
            x, cot, heads, w1, w2, w3, vec[2], vec[3:7].reshape(4, 768), vec[7], vec[8], vec[9], vec[10], vec[11]
        )
        dgain1, dgain2, dshift1, dshift2, dbo, dbh, dbd = small
        gproj = attn_bwd(my_prefix, g1low, w1, proj, projT, ot, lse)
        gp = gproj[:, :, :576]
        dqkv = ein("pd,tpc->tdc", x, gp).astype(bf16)
        x4 = (g1 + ein("tpc,tdc->pd", gp, w1[:, :, :576])).astype(bf16).reshape(4, 256, 768)
        dbq = jnp.sum(gp[:, :, :192], 1, dtype=f32).reshape(1, 768)
        dbv = jnp.sum(gp[:, :, 384:], 1, dtype=f32).reshape(1, 768)
        d = jnp.stack([jnp.concatenate([dqkv, doutw[:, :, 64:]], 2), d2, d3])
        part = lax.all_to_all(d, "tensor", 1, 1, tiled=True).astype(f32).sum(1)
        part = part.astype(bf16).reshape(3, -1, rows, 768)
        gs = lax.all_to_all(part, "dp", 1, 1, tiled=True).astype(f32).sum(1)
        vs = lax.psum(
            jnp.concatenate([dbq, dbv, dbo[None], dbh, jnp.stack([dbd, dshift1, dshift2, dgain1, dgain2]), jnp.zeros((4, 768), f32)]),
            ("dp", "tensor"),
        )
        oo = lax.all_to_all(out.reshape(4, 256, 768), "tensor", 0, 0, tiled=True)
        xx = lax.all_to_all(x4, "tensor", 0, 0, tiled=True)
    mine = lax.dynamic_slice_in_dim(vs, (d_me * n_t + t_me) * width, width, 1)
    return (
        seqs(oo),
        seqs(xx),
        gs[0, :, :576].reshape(rows, 3, 192),
        gs[0, :, 576:].T,
        gs[1],
        gs[2].T,
        mine[:10],
        mine[10:12],
    )


def solution(mesh):
    placed = (
        P("tensor", "dp", None),
        P("tensor", "dp", None),
        P("dp"),
        P("dp", None, "tensor"),
        P("tensor", "dp"),
        P("dp", "tensor"),
        P("tensor", "dp"),
        P(None, ("dp", "tensor")),
        P(None, ("dp", "tensor")),
    )
    return jax.shard_map(on_device, mesh=mesh, in_specs=placed, out_specs=placed[:2] + placed[3:], check_vma=False)
```

```python
import functools
import math

import jax
import jax.numpy as jnp
from jax import lax
from jax.experimental import pallas as pl
from jax.experimental.pallas import tpu as pltpu
from jax.sharding import PartitionSpec as P

f32=jnp.float32; bf16=jnp.bfloat16
L=1024; QB=256; NK=(512,512,768,1024)
C2=0.125*math.log2(math.e)
NEG=-1e30
def dotf(a,b): return jnp.dot(a,b,preferred_element_type=f32)
def dot_nt(a,b): return lax.dot_general(a,b,(((1,),(1,)),((),())),preferred_element_type=f32)
def masks(mask_ref, prefix):
    k=lax.broadcasted_iota(jnp.int32,(256,256),0); q=lax.broadcasted_iota(jnp.int32,(256,256),1)
    diag=k<=q
    mask_ref[0]=jnp.where(diag|(k<prefix),0.0,NEG)
    mask_ref[1]=jnp.where(k+256<prefix,0.0,NEG)+jnp.zeros((256,256),f32)
    mask_ref[2]=jnp.where(diag|(k+256<prefix),0.0,NEG)
    mask_ref[3]=jnp.where(diag,0.0,NEG)
MASKMAP={0:{0:0,1:1},1:{1:2},2:{2:3},3:{3:3}}
def masked(st,qb,mask_ref):
    parts=[]
    for kb in range(NK[qb]//256):
        p=st[kb*256:(kb+1)*256]
        mi=MASKMAP[qb].get(kb)
        parts.append(p if mi is None else p+mask_ref[mi])
    return jnp.concatenate(parts,0)
def fwd_kernel(prefix_ref,x_ref,w_ref,b_ref,proj_ref,projT_ref,heads_ref,ot_ref,lse_ref,zq_ref,mask_ref):
    masks(mask_ref,prefix_ref[0])
    proj=(dotf(x_ref[...],w_ref[:,:640])+b_ref[...]).astype(bf16)
    proj_ref[...]=proj
    projT_ref[...]=proj.T
    zq_ref[...]=jnp.zeros_like(zq_ref)
    for h in range(3):
        zq_ref[h,64+64*h:128+64*h,:]=projT_ref[64*h:64*h+64,:]
    ot_ref[...]=jnp.zeros_like(ot_ref)
    for h in range(3):
        for qb in range(4):
            nk=NK[qb]; qs=slice(qb*QB,qb*QB+QB)
            st=dotf(proj_ref[:nk,128:384],zq_ref[h,:,qs])
            st=masked(st,qb,mask_ref)
            m=jnp.max(st,axis=0,keepdims=True)
            p=jnp.exp2((st-m)*C2)
            l=jnp.sum(p,axis=0,keepdims=True)
            ot=dotf(projT_ref[384+64*h:448+64*h,:nk],p.astype(bf16))
            ot_ref[64+64*h:128+64*h,qs]=(ot/l).astype(bf16)
            lse_ref[h:h+1,qs]=m*C2+jnp.log2(l)
    heads_ref[...]=ot_ref[...].T
def attn_fwd(prefix,x,w1,bqkv):
    sq=pl.squeezed
    return pl.pallas_call(fwd_kernel,grid_spec=pltpu.PrefetchScalarGridSpec(num_scalar_prefetch=1,grid=(4,),
      in_specs=[pl.BlockSpec((L,768),lambda t,p:(0,0)),pl.BlockSpec((sq,768,768),lambda t,p:(t,0,0)),pl.BlockSpec((sq,1,640),lambda t,p:(t,0,0))],
      out_specs=[pl.BlockSpec((sq,L,640),lambda t,p:(t,0,0)),pl.BlockSpec((sq,640,L),lambda t,p:(t,0,0)),pl.BlockSpec((sq,L,256),lambda t,p:(t,0,0)),pl.BlockSpec((sq,256,L),lambda t,p:(t,0,0)),pl.BlockSpec((sq,8,L),lambda t,p:(t,0,0))],
      scratch_shapes=[pltpu.VMEM((3,256,L),bf16),pltpu.VMEM((4,256,256),f32)]),
      out_shape=[jax.ShapeDtypeStruct((4,L,640),bf16),jax.ShapeDtypeStruct((4,640,L),bf16),jax.ShapeDtypeStruct((4,L,256),bf16),jax.ShapeDtypeStruct((4,256,L),bf16),jax.ShapeDtypeStruct((4,8,L),f32)],
      compiler_params=pltpu.CompilerParams(vmem_limit_bytes=62<<20))(prefix,x,w1,bqkv)
def bwd_kernel(prefix_ref,g_ref,w_ref,proj_ref,projT_ref,ot_ref,lse_ref,gproj_ref,
               zq_ref,zdo_ref,qm_ref,dom_ref,pt_ref,ds_ref,mask_ref,gt_ref,dqt_ref):
    masks(mask_ref,prefix_ref[0])
    gh=dotf(g_ref[...],w_ref[:,512:768]).astype(bf16)
    gt_ref[...]=gh.T
    zq_ref[...]=jnp.zeros_like(zq_ref); zdo_ref[...]=jnp.zeros_like(zdo_ref)
    lane=lax.broadcasted_iota(jnp.int32,(1,256),1)
    for h in range(3):
        zq_ref[h,64+64*h:128+64*h,:]=projT_ref[64*h:64*h+64,:]
        zdo_ref[h,64*h:64*h+64,:]=gt_ref[64+64*h:128+64*h,:]*0.125
        sel=(lane>=64*h)&(lane<64*h+64)
        qm_ref[h]=jnp.where(sel,proj_ref[:,0:256],0)
        sel2=(lane>=64*h+64)&(lane<64*h+128)
        dom_ref[h]=jnp.where(sel2,gh,0)
    for h in range(3):
        d=jnp.sum(gt_ref[64+64*h:128+64*h,:].astype(f32)*ot_ref[64+64*h:128+64*h,:].astype(f32),axis=0,keepdims=True)*0.125
        for qb in range(4):
            nk=NK[qb]; qs=slice(qb*QB,qb*QB+QB)
            st=dotf(proj_ref[:nk,128:384],zq_ref[h,:,qs])
            st=masked(st,qb,mask_ref)
            p=jnp.exp2(st*C2-lse_ref[h:h+1,qs])
            dp=dotf(proj_ref[:nk,384:640],zdo_ref[h,:,qs])
            ds=(p*(dp-d[:,qs])).astype(bf16)
            pt_ref[h,:nk,qs]=p.astype(bf16)
            ds_ref[h,:nk,qs]=ds
            dqt_ref[64*h:64*h+64,qs]=dotf(projT_ref[192+64*h:256+64*h,:nk],ds).astype(bf16)
    gproj_ref[:,0:192]=dqt_ref[...].T
    for (k0,k1,q0) in ((0,512,0),(512,768,512),(768,1024,768)):
        dk=jnp.zeros((k1-k0,256),f32); dv=jnp.zeros((k1-k0,256),f32)
        for h in range(3):
            dk=dk+dotf(ds_ref[h,k0:k1,q0:],qm_ref[h,q0:,:])
            dv=dv+dotf(pt_ref[h,k0:k1,q0:],dom_ref[h,q0:,:])
        gproj_ref[k0:k1,192:384]=dk[:,0:192].astype(bf16)
        gproj_ref[k0:k1,384:576]=dv[:,64:256].astype(bf16)
    gproj_ref[:,576:640]=jnp.zeros((L,64),bf16)
def attn_bwd(prefix,g,w1,proj,projT,ot,lse):
    sq=pl.squeezed
    sp=lambda *s: pl.BlockSpec((sq,)+s,lambda t,p:(t,0,0))
    return pl.pallas_call(functools.partial(bwd_kernel),grid_spec=pltpu.PrefetchScalarGridSpec(num_scalar_prefetch=1,grid=(4,),
      in_specs=[pl.BlockSpec((L,768),lambda t,p:(0,0)),sp(768,768),sp(L,640),sp(640,L),sp(256,L),sp(8,L)],
      out_specs=sp(L,640),
      scratch_shapes=[pltpu.VMEM((3,256,L),bf16),pltpu.VMEM((3,256,L),bf16),pltpu.VMEM((3,L,256),bf16),pltpu.VMEM((3,L,256),bf16),pltpu.VMEM((3,L,L),bf16),pltpu.VMEM((3,L,L),bf16),pltpu.VMEM((4,256,256),f32),pltpu.VMEM((256,L),bf16),pltpu.VMEM((192,L),bf16)]),
      out_shape=jax.ShapeDtypeStruct((4,L,640),bf16),
      compiler_params=pltpu.CompilerParams(vmem_limit_bytes=62<<20))(prefix,g,w1,proj,projT,ot,lse)
MESH=pl.DeviceIdType.MESH
class Place:
    def __init__(self):
        dp=lax.axis_index("dp"); t=lax.axis_index("tensor")
        self.dp,self.t=dp,t
        self.z,self.x,self.y,self.c=dp//2,dp%2,t//2,t%2
    def peer(self,dim,j=1):
        return {'x':lambda:(self.dp^1,self.t),'z':lambda:(self.dp^(2*j),self.t),'y':lambda:(self.dp,self.t^2),'c':lambda:(self.dp,self.t^1)}[dim]()
    def peers_all(self):
        return [self.peer('x'),self.peer('y'),self.peer('c'),self.peer('z',1),self.peer('z',2),self.peer('z',3),(self.dp,self.t^3)]
def barrier(peers):
    b=pltpu.get_barrier_semaphore()
    for p in peers: pl.semaphore_signal(b,inc=1,device_id=p,device_id_type=MESH)
    pl.semaphore_wait(b,len(peers))
class Sems:
    def __init__(self,send,recv): self.s,self.r,self.n=send,recv,0
    def take(self):
        i=self.n; self.n+=1
        return self.s.at[i],self.r.at[i]
def rcopy(src,dst,sems,dev):
    a,b=sems.take()
    return pltpu.make_async_remote_copy(src_ref=src,dst_ref=dst,send_sem=a,recv_sem=b,device_id=dev,device_id_type=MESH)
def local(src,dst,sem):
    k=pltpu.make_async_copy(src,dst,sem); k.start(); return k
def exchange(pc,src,dst,sems):
    out=[]
    for j in (2,3,1):
        p=(pc.dp,pc.t^j)
        k=rcopy(src.at[pc.t^j],dst.at[pc.t],sems,p); k.start(); out.append(k)
    return out
HBM=pl.BlockSpec(memory_space=pltpu.HBM); VM=pl.BlockSpec(memory_space=pltpu.VMEM)
def point(steps, k, h):
    for kk in range(4):
        todo = steps.get((kk, h))
        if todo:
            @pl.when(k == kk)
            def _(todo=todo):
                for step in todo:
                    step()


def add_into(dst, src, n, pick_dst, pick_src):
    def body(j, _):
        a, b = pick_dst(j), pick_src(j)
        dst[a] = (dst[a].astype(f32) + src[b].astype(f32)).astype(bf16)
        return 0
    lax.fori_loop(0, n, body, 0)


class Reduce:
    def __init__(self, pc, kind, d_ref, half, lc, rc, r1, r2, r3, sems, lsem):
        self.pc, self.kind, self.lc, self.rc, self.r1, self.r2, self.r3 = pc, kind, lc, rc, r1, r2, r3
        rows = pl.ds(48 * half, 48)
        self.own = pltpu.make_async_copy(d_ref.at[:, pc.c, :, :, rows], lc, lsem)
        self.q0 = rcopy(d_ref.at[:, 1 - pc.c, :, :, rows], rc, sems, pc.peer("c"))
        if kind == "x":
            self.q1 = rcopy(lc.at[:, :, 1 - pc.x], r1, sems, pc.peer("x"))
            self.q2 = [rcopy(lc.at[:, pc.z ^ j, pc.x], r2.at[j - 1], sems, pc.peer("z", j)) for j in (3, 2, 1)]
            self.q3 = [rcopy(lc.at[1 - pc.y, pc.z, pc.x], r3.at[0], sems, pc.peer("y"))]
        else:
            self.q1 = rcopy(lc.at[1 - pc.y], r1, sems, pc.peer("y"))
            self.q2 = [rcopy(lc.at[pc.y, :, 1 - pc.x], r2, sems, pc.peer("x"))]
            self.q3 = [rcopy(lc.at[pc.y, pc.z ^ j, pc.x], r3.at[j - 1], sems, pc.peer("z", j)) for j in (3, 2, 1)]

    def s0(self):
        self.own.start()
        self.q0.start()

    def s1(self):
        self.own.wait()
        self.q0.wait_recv()
        at = lambda j: (j // 8, (j // 2) % 4, j % 2)
        add_into(self.lc, self.rc, 16, at, at)
        self.q1.start()

    def s2(self):
        self.q1.wait_recv()
        if self.kind == "x":
            add_into(self.lc, self.r1, 8, lambda j: (j // 4, j % 4, self.pc.x), lambda j: (j // 4, j % 4))
        else:
            add_into(self.lc, self.r1, 8, lambda j: (self.pc.y, j // 2, j % 2), lambda j: (j // 2, j % 2))
        for q in self.q2:
            q.start()

    def s3(self):
        pc = self.pc
        for q in self.q2:
            q.wait_recv()
        if self.kind == "x":
            for y in range(2):
                at = (y, pc.z, pc.x)
                total = (self.lc[at].astype(f32) + self.r2[0, y].astype(f32)) + (self.r2[1, y].astype(f32) + self.r2[2, y].astype(f32))
                self.lc[at] = total.astype(bf16)
        else:
            add_into(self.lc, self.r2, 4, lambda j: (pc.y, j, pc.x), lambda j: (j,))
        for q in self.q3:
            q.start()

    def s4(self, out_ref, rows):
        pc = self.pc
        for q in self.q3:
            q.wait_recv()
        total = self.lc[pc.y, pc.z, pc.x].astype(f32) + self.r3[0].astype(f32)
        if self.kind == "y":
            total = total + (self.r3[1].astype(f32) + self.r3[2].astype(f32))
        out_ref[rows] = total

    def end(self):
        for q in [self.q0, self.q1] + self.q2 + self.q3:
            q.wait_send()


N_C = 4 * 6 + 3 + 3 + 8 + 6 + 6


def back_kernel(
    prefix_ref, x_ref, g_ref, gf_ref, w_ref, proj_ref, projT_ref, ot_ref, lse_ref, dout_ref, d_ref, v_ref,
    gs_ref, vs_ref, xo_ref,
    xT, gl, dxa, w_b, proj_b, projT_b, ot_b, lse_b, dout_b,
    zq, zdo, qm, dom, pt, ds, mask_ref, gt, dqt, dkb, dvb, gproj,
    lc, rc, yx1, yx2, yx3, yy1, yy2, yy3, dwb, cr, yr, xr, zr, vb, vr, xst, ss, rs, ls, ins,
):
    pc = Place()
    sems = Sems(ss, rs)
    w1 = w_ref.at[0]
    lane = lax.broadcasted_iota(jnp.int32, (1, 256), 1)

    def loads(k, slot):
        t = pc.t ^ (3 - k)
        pairs = [
            (w1.at[t // 2, t % 2], w_b), (proj_ref.at[t], proj_b), (projT_ref.at[t], projT_b),
            (ot_ref.at[t], ot_b), (lse_ref.at[t], lse_b), (dout_ref.at[t], dout_b),
        ]
        return [pltpu.make_async_copy(a, b.at[slot], ins.at[slot, n]) for n, (a, b) in enumerate(pairs)]

    first = loads(0, 0)
    for q in first:
        q.start()
    l_x = local(x_ref, xst, ls.at[4])
    l_g = local(g_ref, gl, ls.at[5])
    l_f = local(gf_ref, dxa, ls.at[6])
    barrier(pc.peers_all())
    red = []
    for n, (kind, g, i) in enumerate((("y", 1, 0), ("x", 1, 1), ("y", 0, 0), ("x", 0, 1))):
        r1, r2, r3 = [r.at[n // 2] for r in ((yy1, yy2, yy3) if kind == "y" else (yx1, yx2, yx3))]
        red.append(Reduce(pc, kind, d_ref.at[g], i, lc.at[n], rc.at[n], r1, r2, r3, sems, ls.at[n]))
        red[n].s0()
    q_c0 = rcopy(dwb.at[0], cr.at[0], sems, pc.peer("c"))
    q_y = rcopy(dwb.at[1], yr, sems, pc.peer("y"))
    q_c1 = rcopy(dwb.at[2], cr.at[1], sems, pc.peer("c"))
    half = [pl.ds(48 * i, 48) for i in range(2)]
    q_x = [rcopy(dwb.at[3, pc.z ^ j, 1 - pc.x, half[i]], xr.at[i, pc.z ^ j], sems, pc.peer("x")) for i in range(2) for j in (3, 2, 1, 0)]
    q_z = [rcopy(dwb.at[3, pc.z ^ j, pc.x, half[i]], zr.at[i, j - 1], sems, pc.peer("z", j)) for i in range(2) for j in (3, 2, 1)]
    v_q = [rcopy(vb.at[n], vr.at[n], sems, pc.peer(dim)) for n, dim in enumerate("cxy")]
    v_z = [rcopy(vb.at[3], vr.at[2 + j], sems, pc.peer("z", j)) for j in (3, 2, 1)]

    def vstep(n):
        v_q[n].wait_recv()
        vb[n + 1] = vb[n] + vr[n]
        for q in [v_q[n + 1]] if n < 2 else v_z:
            q.start()

    steps = {
        (0, 0): [red[0].s1], (0, 1): [red[1].s1], (0, 2): [red[2].s1], (0, 3): [red[3].s1],
        (1, 1): [red[1].s2], (1, 2): [red[0].s2], (2, 1): [red[3].s2, red[2].s2], (2, 2): [red[1].s3],
        (3, 0): [red[0].s3], (3, 1): [red[3].s3], (3, 2): [red[2].s3],
    }
    masks(mask_ref, prefix_ref[pc.t])
    zq[...] = jnp.zeros_like(zq)
    zdo[...] = jnp.zeros_like(zdo)
    gproj[:, 576:640] = jnp.zeros((L, 64), bf16)
    vb[0] = v_ref[...]
    l_x.wait()
    xT[...] = xst[...].reshape(L, 768).T
    l_g.wait()
    l_f.wait()

    def chip_sum(i, z, x):
        return dwb[3, z, x, half[i]].astype(f32) + (cr[1, z, x, half[i]].astype(f32) + yr[z, x, half[i]].astype(f32))

    def group(k, _):
        slot = k % 2
        for q in loads(k, slot):
            q.wait()

        @pl.when(k < 3)
        def _():
            for q in loads(k + 1, 1 - slot):
                q.start()

        t = pc.t ^ (3 - k)
        w, pj, pjT, o_t, lse = w_b.at[slot], proj_b.at[slot], projT_b.at[slot], ot_b.at[slot], lse_b.at[slot]
        gh = dotf(gl[...], w[...].reshape(768, 768)[:, 512:768]).astype(bf16)
        gt[...] = gh.T
        for h in range(3):
            point(steps, k, h)
            own = slice(64 + 64 * h, 128 + 64 * h)
            zq[h, own, :] = pjT[64 * h : 64 * h + 64, :]
            zdo[h, 64 * h : 64 * h + 64, :] = gt[own, :] * 0.125
            qm[...] = jnp.where((lane >= 64 * h) & (lane < 64 * h + 64), pj[:, 0:256], 0)
            dom[...] = jnp.where((lane >= 64 * h + 64) & (lane < 64 * h + 128), gh, 0)
            d = jnp.sum(gt[own, :].astype(f32) * o_t[own, :].astype(f32), axis=0, keepdims=True) * 0.125
            for qb in range(4):
                nk = NK[qb]
                qs = slice(qb * QB, qb * QB + QB)
                st = masked(dotf(pj[:nk, 128:384], zq[h, :, qs]), qb, mask_ref)
                p = jnp.exp2(st * C2 - lse[h : h + 1, qs])
                dp = dotf(pj[:nk, 384:640], zdo[h, :, qs])
                dsv = (p * (dp - d[:, qs])).astype(bf16)
                pt[:nk, qs] = p.astype(bf16)
                ds[:nk, qs] = dsv
                dqt[64 * h : 64 * h + 64, qs] = dotf(pjT[192 + 64 * h : 256 + 64 * h, :nk], dsv).astype(bf16)
            for k0, k1, q0 in ((0, 512, 0), (512, 768, 512), (768, 1024, 768)):
                dk = dotf(ds[k0:k1, q0:], qm[q0:, :]).astype(bf16)
                dv = dotf(pt[k0:k1, q0:], dom[q0:, :]).astype(bf16)
                dkb[k0:k1] = dk if h == 0 else dkb[k0:k1] + dk
                dvb[k0:k1] = dv if h == 0 else dvb[k0:k1] + dv
        point(steps, k, 3)
        gproj[:, 0:192] = dqt[...].T
        gproj[:, 192:384] = dkb[:, 0:192]
        gproj[:, 384:576] = dvb[:, 64:256]
        vb[0, pl.ds(16 + 2 * t, 1), 0:256] = jnp.sum(gproj[:, 0:256].astype(f32), axis=0, keepdims=True)
        vb[0, pl.ds(17 + 2 * t, 1), 0:256] = jnp.sum(gproj[:, 384:640].astype(f32), axis=0, keepdims=True)

        @pl.when(k == 3)
        def _():
            v_q[0].start()

        dw = dotf(xT[...], gproj[...])
        do = dout_b[slot].astype(f32)
        shape = lambda a: a.astype(bf16).reshape(4, 2, 96, a.shape[1])
        dwb[k, :, :, :, 0:512] = shape(dw[:, 0:512])
        dwb[k, :, :, :, 512:640] = shape(dw[:, 512:640] + do[:, 0:128])
        dwb[k, :, :, :, 640:768] = shape(do[:, 128:256])

        @pl.when(k == 0)
        def _():
            q_c0.start()

        @pl.when(k == 1)
        def _():
            q_c0.wait_recv()
            add_into(dwb.at[1], cr.at[0], 8, lambda j: (j // 2, j % 2), lambda j: (j // 2, j % 2))
            q_y.start()

        @pl.when(k == 2)
        def _():
            q_c1.start()

        @pl.when(k == 3)
        def _():
            vstep(0)
            q_c1.wait_recv()
            q_y.wait_recv()
            for n, q in enumerate(q_x):
                i, z, x = n // 4, pc.z ^ (3 - n % 4), 1 - pc.x
                dwb[3, z, x, half[i]] = chip_sum(i, z, x).astype(bf16)
                q.start()

        dxa[...] += dot_nt(gproj[...], w[...].reshape(768, 768)[:, 0:640])
        return 0

    lax.fori_loop(0, 4, group, 0)
    vstep(1)
    xst[...] = dxa[...].astype(bf16).reshape(4, 256, 768)
    xx = exchange(pc, xst, xo_ref, sems)
    l_o = local(xst.at[pc.t], xo_ref.at[pc.t], ls.at[7])
    vstep(2)

    def arrive(n, j):
        i, z = n // 4, pc.z ^ j
        q_x[n].wait_recv()
        dwb[3, z, pc.x, half[i]] = (chip_sum(i, z, pc.x) + xr[i, z].astype(f32)).astype(bf16)

    for n in range(8):
        j = 3 - n % 4
        arrive(n, j)
        if j:
            q_z[n - n // 4].start()
        if n == 1:
            red[0].s4(gs_ref.at[2], slice(0, 48))
        if n == 3:
            red[2].s4(gs_ref.at[1], slice(0, 48))
    red[1].s4(gs_ref.at[2], slice(48, 96))
    red[3].s4(gs_ref.at[1], slice(48, 96))
    for q in v_z:
        q.wait_recv()
    vs_ref[...] = (vb[3] + vr[3]) + (vr[4] + vr[5])
    for i in range(2):
        for q in q_z[3 * i : 3 * i + 3]:
            q.wait_recv()
        gs_ref[0, 48 * i : 48 * i + 48] = (dwb[3, pc.z, pc.x, half[i]].astype(f32) + zr[i, 0].astype(f32)) + (zr[i, 1].astype(f32) + zr[i, 2].astype(f32))
    l_o.wait()
    for q in xx:
        q.wait()
    for r in red:
        r.end()
    for q in [q_c0, q_y, q_c1] + q_x + q_z + v_q + v_z:
        q.wait_send()


def back(prefix, x, g1low, g1, g, proj, projT, ot, lse, doutw, d, v):
    v_ = pltpu.VMEM
    dma = pltpu.SemaphoreType.DMA
    sd = jax.ShapeDtypeStruct
    return pl.pallas_call(
        back_kernel,
        out_shape=[sd((3, 96, 768), f32), sd((24, 768), f32), sd((4, 256, 768), bf16)],
        in_specs=[pl.BlockSpec(memory_space=pltpu.SMEM)] + [HBM] * 10 + [VM],
        out_specs=[VM, VM, HBM],
        scratch_shapes=[
            v_((768, L), bf16), v_((L, 768), bf16), v_((L, 768), f32),
            v_((2, 4, 2, 96, 768), bf16), v_((2, L, 640), bf16), v_((2, 640, L), bf16), v_((2, 256, L), bf16), v_((2, 8, L), f32), v_((2, 768, 256), bf16),
            v_((3, 256, L), bf16), v_((3, 256, L), bf16), v_((L, 256), bf16), v_((L, 256), bf16), v_((L, L), bf16), v_((L, L), bf16),
            v_((4, 256, 256), f32), v_((256, L), bf16), v_((192, L), bf16), v_((L, 256), bf16), v_((L, 256), bf16), v_((L, 640), bf16),
            v_((4, 2, 4, 2, 48, 768), bf16), v_((4, 2, 4, 2, 48, 768), bf16),
            v_((2, 2, 4, 48, 768), bf16), v_((2, 3, 2, 48, 768), bf16), v_((2, 1, 48, 768), bf16),
            v_((2, 4, 2, 48, 768), bf16), v_((2, 4, 48, 768), bf16), v_((2, 3, 48, 768), bf16),
            v_((4, 4, 2, 96, 768), bf16), v_((2, 4, 2, 96, 768), bf16), v_((4, 2, 96, 768), bf16), v_((2, 4, 48, 768), bf16), v_((2, 3, 48, 768), bf16),
            v_((4, 24, 768), f32), v_((6, 24, 768), f32), v_((4, 256, 768), bf16),
            dma((N_C,)), dma((N_C,)), dma((8,)), dma((2, 6)),
        ],
        compiler_params=pltpu.CompilerParams(collective_id=1, has_side_effects=True, vmem_limit_bytes=67043328),
    )(prefix, x, g1low, g1, g, proj, projT, ot, lse, doutw, d, v)


class Gather:
    def __init__(self, pc, src, dst, rows, order, sems):
        self.pc, self.src, self.dst, self.rows, self.order, self.sems = pc, src, dst, rows, order, sems
        self.full, self.sent, self.core = set(), [], []
        self.plan()

    def at(self, over, full):
        pc = self.pc
        ix = {d: over.get(d, slice(None) if d in full else getattr(pc, d)) for d in "yzx"}
        return self.dst.at[(ix["y"], pc.c, ix["z"], ix["x"]) + ((pl.ds(*self.rows),) if self.rows else ())]

    def plan(self):
        pc = self.pc
        src = self.src.at[pl.ds(*self.rows)] if self.rows else self.src
        mine = self.at({}, set())
        self.core.append(rcopy(src, mine, self.sems, pc.peer("c")))
        self.phases = []
        full = set()
        for d in self.order:
            ks = []
            for j in (1, 2, 3) if d == "z" else (1,):
                here = self.at({}, full)
                ks.append(rcopy(here if full else src, here, self.sems, pc.peer(d, j)))
                there = self.at({d: getattr(pc, d) ^ j}, full)
                self.core.append(rcopy(there, there, self.sems, pc.peer("c")))
            self.phases.append(ks)
            full = full | {d}
        self.first = [1]
        for ks in self.phases:
            self.first.append(self.first[-1] + len(ks))

    def start(self):
        self.core[0].start()
        for k in self.phases[0]:
            k.start()

    def arrive(self, p):
        for n, k in enumerate(self.phases[p]):
            k.wait_recv()
            self.core[self.first[p] + n].start()

    def next(self, p):
        self.arrive(p - 1)
        for k in self.phases[p]:
            k.start()

    def from_core(self, a, b):
        for k in self.core[a:b]:
            k.wait_recv()

    def end(self):
        for k in self.core + sum(self.phases, []):
            k.wait_send()


class Slabs:
    def __init__(self, pc, src, dst, kind, rows, sems):
        src = src.at[rows]
        at = lambda y, z, x: dst.at[y, pc.c, z, x, rows]
        every = slice(None)
        mine, other = pc.y, 1 - pc.y
        self.copy, self.fwd = {}, {}

        def add(name, dim, pairs, got):
            self.copy[name] = [rcopy(a, b, sems, pc.peer(dim, j)) for j, a, b in pairs]
            if got is not None:
                self.fwd[name] = rcopy(got, got, sems, pc.peer("c"))

        slab = at(mine, every, pc.x)
        add("z", "z", [(j, src, at(mine, pc.z, pc.x)) for j in (3, 2, 1)], slab)
        if kind in "AB":
            add("x", "x", [(1, slab, slab)], at(mine, every, 1 - pc.x))
        if kind == "A":
            whole = at(mine, every, every)
            add("y", "y", [(1, whole, whole)], at(other, every, every))
        if kind in "CE":
            add("y", "y", [(1, slab, slab)], at(other, every, pc.x))
        if kind == "E":
            whole = at(every, every, pc.x)
            add("x", "x", [(1, whole, whole)], at(every, every, 1 - pc.x))
        if kind == "B":
            add("y", "y", [(1, src, at(mine, pc.z, pc.x))], None)
            one, slab2 = at(other, pc.z, pc.x), at(other, every, pc.x)
            add("z2", "z", [(j, one, one) for j in (3, 2, 1)], slab2)
            add("x2", "x", [(1, slab2, slab2)], at(other, every, 1 - pc.x))

    def start(self, name):
        for k in self.copy[name]:
            k.start()

    def arrive(self, name):
        for k in self.copy[name]:
            k.wait_recv()
        if name in self.fwd:
            self.fwd[name].start()

    def from_core(self, *names):
        for n in names:
            self.fwd[n].wait_recv()

    def end(self):
        for ks in self.copy.values():
            for k in ks:
                k.wait_send()
        for k in self.fwd.values():
            k.wait_send()


N_A = 3 * 8 + 2 * 13 + 6 + 11 + 3


def front_kernel(
    prefix_ref, s_ref, h_ref, b_ref,
    g_ref, x_ref, vec_ref, proj_ref, projT_ref, heads_ref, ot_ref, lse_ref,
    bv, sv, xv, wv, proj_b, projT_b, heads_b, ot_b, lse_b, zq, mask_ref, ss, rs, ls, os_,
):
    pc = Place()
    sems = Sems(ss, rs)
    own = (pc.y, pc.c, pc.z, pc.x)
    l_s = local(s_ref, sv, ls.at[0])
    l_h = local(h_ref.at[pc.t], xv.at[pc.t], ls.at[1])
    l_b = local(b_ref, bv.at[own], ls.at[9])
    barrier(pc.peers_all())
    bias = Gather(pc, b_ref, bv, None, "zxy", sems)
    w1a, w1b, w2a, w2b, w3a, w3b = every = [
        Slabs(pc, s_ref.at[n // 2], g_ref.at[n // 2], kind, rows, sems)
        for n, (kind, rows) in enumerate(zip("ABABCE", [pl.ds(0, 48), pl.ds(48, 48)] * 3))
    ]
    bias.start()
    w1b.start("y")
    w1a.start("z")
    w1b.start("z")
    hx = exchange(pc, h_ref, xv, sems)
    w2b.start("y")
    l_s.wait()
    l_g = [local(sv.at[g], g_ref.at[g].at[own], ls.at[3 + g]) for g in range(3)]
    masks(mask_ref, prefix_ref[pc.t])
    zq[...] = jnp.zeros_like(zq)
    ot_b[...] = jnp.zeros_like(ot_b)
    for q in l_g:
        q.wait()
    l_b.wait()
    w1b.arrive("y")
    w1b.start("z2")
    bias.next(1)
    w1a.arrive("z")
    w1a.start("x")
    bias.next(2)
    w1b.arrive("z")
    w1b.start("x")
    w1a.arrive("x")
    w1a.start("y")
    w2a.start("z")
    w3b.start("z")
    w1b.arrive("z2")
    w1b.start("x2")
    w1b.arrive("x")
    w2b.start("z")
    bias.arrive(2)
    bias.from_core(0, len(bias.core))
    l_h.wait()
    for q in hx:
        q.wait_recv()
    l_x = local(xv, x_ref, ls.at[7])

    def load(k, slot):
        t = pc.t ^ k
        return pltpu.make_async_copy(g_ref.at[0, t // 2, t % 2], wv.at[slot], ls.at[8])

    def go(g, got, then=None, then_g=None):
        def step():
            g.arrive(got)
            if then:
                (then_g or g).start(then)
        return step

    steps = {
        (0, 0): [go(w2b, "y", "z2"), lambda: w3a.start("z")],
        (0, 2): [go(w2a, "z", "x"), lambda: w1a.from_core("z", "x"), lambda: w1b.from_core("z", "x"), lambda: load(1, 1).start()],
        (0, 3): [go(w1b, "x2")],
        (1, 1): [go(w3b, "z", "y")],
        (1, 2): [go(w2a, "x", "y")],
        (1, 3): [go(w1a, "y"), lambda: load(2, 0).start(), go(w2b, "z", "x")],
        (2, 1): [go(w3b, "y", "x")],
        (2, 2): [lambda: w1a.from_core("y"), lambda: w1b.from_core("z2", "x2"), lambda: load(3, 1).start(), go(w2b, "z2", "x2")],
        (3, 0): [go(w2b, "x"), go(w3a, "z", "y")],
        (3, 2): [go(w2a, "y")],
    }
    load(0, 0).start()

    def outs(k, slot):
        t = pc.t ^ k
        pairs = [(proj_b, proj_ref), (projT_b, projT_ref), (heads_b, heads_ref), (ot_b, ot_ref), (lse_b, lse_ref)]
        return [pltpu.make_async_copy(a.at[slot], b.at[t], os_.at[slot, n]) for n, (a, b) in enumerate(pairs)]

    def group(k, _):
        slot = k % 2
        t = pc.t ^ k
        load(k, slot).wait()

        @pl.when(k >= 2)
        def _():
            for q in outs(k - 2, slot):
                q.wait()

        row = jnp.zeros((8, 256), f32)
        for i in range(8):
            piece = bv[(i // 2) % 2, i % 2, t, i // 4, 0:8, :]
            row = row + pltpu.roll(jnp.concatenate([piece, jnp.zeros((8, 128), f32)], 1), 24 * i, 1)
        brow = jnp.concatenate([row[0:1], jnp.zeros((1, 128), f32), row[1:2]], 1)
        pj, pjT, ot, lse = proj_b.at[slot], projT_b.at[slot], ot_b.at[slot], lse_b.at[slot]
        proj = (dotf(xv[...].reshape(L, 768), wv[slot].reshape(768, 768)[:, :640]) + brow).astype(bf16)
        pj[...] = proj
        pjT[...] = proj.T
        for h in range(3):
            point(steps, k, h)
            zq[h, 64 + 64 * h : 128 + 64 * h, :] = pjT[64 * h : 64 * h + 64, :]
            for qb in range(4):
                nk = NK[qb]
                qs = slice(qb * QB, qb * QB + QB)
                st = masked(dotf(pj[:nk, 128:384], zq[h, :, qs]), qb, mask_ref)
                m = jnp.max(st, axis=0, keepdims=True)
                p = jnp.exp2((st - m) * C2)
                l = jnp.sum(p, axis=0, keepdims=True)
                o = dotf(pjT[384 + 64 * h : 448 + 64 * h, :nk], p.astype(bf16))
                ot[64 + 64 * h : 128 + 64 * h, qs] = (o / l).astype(bf16)
                lse[h : h + 1, qs] = m * C2 + jnp.log2(l)
        point(steps, k, 3)
        heads_b[slot] = ot[...].T
        for q in outs(k, slot):
            q.start()
        return 0

    lax.fori_loop(0, 4, group, 0)
    tiles = [jnp.zeros((16, 128), f32) for _ in range(6)]
    lane = lax.broadcasted_iota(jnp.int32, (1, 128), 1)
    for i in range(32):
        z, x, y, c = i // 8, (i // 4) % 2, (i // 2) % 2, i % 2
        j, r = (24 * i) // 128, (24 * i) % 128
        piece = pltpu.roll(bv[y, c, z, x], r, 1) if r else bv[y, c, z, x]
        tiles[j] = tiles[j] + (jnp.where(lane >= r, piece, 0.0) if r > 104 else piece)
        if r > 104:
            tiles[j + 1] = tiles[j + 1] + jnp.where(lane < r, piece, 0.0)
    for j in range(6):
        vec_ref[:, 128 * j : 128 * j + 128] = tiles[j]
    w3b.arrive("x")
    w2b.arrive("x2")
    w3a.arrive("y")
    w2a.from_core("z", "x", "y")
    w2b.from_core("z", "x", "z2", "x2")
    w3a.from_core("z", "y")
    w3b.from_core("z", "y", "x")
    for q in hx:
        q.wait_send()
    l_x.wait()
    for k in (2, 3):
        for q in outs(k, k % 2):
            q.wait()
    bias.end()
    for g in every:
        g.end()


def front(prefix, s, h, b):
    v_ = pltpu.VMEM
    dma = pltpu.SemaphoreType.DMA
    sd = jax.ShapeDtypeStruct
    return pl.pallas_call(
        front_kernel,
        out_shape=[
            sd((3, 2, 2, 4, 2, 96, 768), bf16), sd((4, 256, 768), bf16), sd((16, 768), f32),
            sd((4, L, 640), bf16), sd((4, 640, L), bf16), sd((4, L, 256), bf16), sd((4, 256, L), bf16), sd((4, 8, L), f32),
        ],
        in_specs=[pl.BlockSpec(memory_space=pltpu.SMEM)] + [HBM] * 2 + [VM],
        out_specs=[HBM] * 2 + [VM] + [HBM] * 5,
        scratch_shapes=[
            v_((2, 2, 4, 2, 16, 128), f32), v_((3, 96, 768), bf16), v_((4, 256, 768), bf16), v_((2, 4, 2, 96, 768), bf16),
            v_((2, L, 640), bf16), v_((2, 640, L), bf16), v_((2, L, 256), bf16), v_((2, 256, L), bf16), v_((2, 8, L), f32),
            v_((3, 256, L), bf16), v_((4, 256, 256), f32),
            dma((N_A,)), dma((N_A,)), dma((10,)), dma((2, 5)),
        ],
        compiler_params=pltpu.CompilerParams(collective_id=0, has_side_effects=True, vmem_limit_bytes=67043328),
    )(prefix, s, h, b)


EPSILON = 1e-12


def gelu_pair(v):
    cdf = 0.5 + 0.5 * lax.erf(v * math.sqrt(0.5))
    pdf = jnp.exp2(v * v * (-0.5 * math.log2(math.e))) * (1.0 / math.sqrt(2.0 * math.pi))
    return v * cdf, cdf + v * pdf


def row_mean(a):
    return jnp.sum(a, axis=-1, keepdims=True) * (1.0 / 768.0)


def mid_kernel(
    x_ref, c_ref, heads_ref, g_ref, vec_ref,
    oo_ref, g1_ref, g1low_ref, dout_ref, d_ref, v_ref,
    xv, cv, hv, wo, w2, w3, xhat, inv, low, act, gd, acc, glow, lowT, gT, stage, dst, ls, ds_, ss, rs,
):
    pc = Place()
    sems = Sems(ss, rs)
    l_x = local(x_ref, xv, ls.at[0])
    l_h = local(heads_ref, hv, ls.at[1])
    l_wo = [local(g_ref.at[0, y, c, :, :, :, pl.ds(512, 256)], wo.at[2 * y + c], ls.at[2 + 2 * y + c]) for y in range(2) for c in range(2)]
    l_w2 = local(g_ref.at[1], w2, ls.at[6])
    ra, rb = pl.ds(0, 48), pl.ds(48, 48)
    parts = lambda r: (r.at[:, :, :, pc.x, ra], r.at[:, :, :, :, rb])
    l_w3 = [local(a, b, ls.at[n]) for n, a, b in zip((7, 9), parts(g_ref.at[2]), parts(w3))]
    l_c = local(c_ref.at[pc.t], cv.at[pc.t], ls.at[8])
    barrier([(pc.dp, pc.t ^ j) for j in (1, 2, 3)] + [pc.peer("x")])
    came = w3.at[:, pc.c, :, 1 - pc.x, ra]
    wx = rcopy(g_ref.at[2, :, pc.c, :, pc.x, ra], w3.at[:, pc.c, :, pc.x, ra], sems, pc.peer("x"))
    wc = rcopy(came, came, sems, pc.peer("c"))
    wx.start()
    cx = exchange(pc, c_ref, cv, sems)
    row = lambda n: vec_ref[n : n + 1, :]
    v_ref[...] = jnp.zeros_like(v_ref)

    def add_row(n, a):
        v_ref[n : n + 1, :] += jnp.sum(a, axis=0, keepdims=True)

    for q in [l_x, l_h] + l_wo:
        q.wait()

    def first(b, _):
        rows = pl.ds(pl.multiple_of(b * 256, 256), 256)
        r = xv[b].astype(f32) + row(2)
        for t in range(4):
            r = r + dot_nt(hv[t, rows, :], wo[t].reshape(768, 256))
        center = r - row_mean(r)
        iv = lax.rsqrt(row_mean(center * center) + EPSILON)
        xh = center * iv
        xhat[rows, :] = xh
        inv[rows, :] = jnp.broadcast_to(iv, (256, 128))
        normed = xh * row(10) + row(8)
        low[rows, :] = normed.astype(bf16)
        acc[rows, :] = normed + row(7)
        return 0

    lax.fori_loop(0, 4, first, 0)
    l_w2.wait()

    def up(n, _):
        t, b = n // 4, n % 4
        rows = pl.ds(pl.multiple_of(b * 256, 256), 256)
        pre = dotf(low[rows, :], w2[t // 2, t % 2].reshape(768, 768)) + vec_ref[pl.ds(3 + t, 1), :]
        a, d = gelu_pair(pre)
        act[t, rows, :] = a.astype(bf16)
        gd[t, rows, :] = d.astype(bf16)

        @pl.when(n == 13)
        def _():
            wx.wait_recv()
            wc.start()

        return 0

    lax.fori_loop(0, 16, up, 0)
    wc.wait_recv()
    for q in l_w3:
        q.wait()

    def branch(b, _):
        rows = pl.ds(pl.multiple_of(b * 256, 256), 256)
        total = acc[rows, :]
        for t in range(4):
            total = total + dot_nt(act[t, rows, :], w3[t // 2, t % 2].reshape(768, 768))
        acc[rows, :] = total
        return 0

    lax.fori_loop(0, 4, branch, 0)
    for q in (wx, wc):
        q.wait_send()
    l_c.wait()
    for q in cx:
        q.wait()

    def second(b, _):
        rows = pl.ds(pl.multiple_of(b * 256, 256), 256)
        r = acc[rows, :]
        center = r - row_mean(r)
        iv = lax.rsqrt(row_mean(center * center) + EPSILON)
        xh = center * iv
        stage[b] = (xh * row(11) + row(9)).astype(bf16)
        ct = cv[b].astype(f32)
        e = ct * row(11)
        g2 = (e - row_mean(e) - xh * row_mean(e * xh)) * iv
        acc[rows, :] = g2
        glow[rows, :] = g2.astype(bf16)
        add_row(11, ct * xh)
        add_row(9, ct)
        add_row(7, g2)
        return 0

    lax.fori_loop(0, 4, second, 0)
    ox = exchange(pc, stage, oo_ref, sems)
    l_o = local(stage.at[pc.t], oo_ref.at[pc.t], ls.at[0])
    gT[...] = glow[...].T
    lowT[...] = low[...].T

    def sends(t):
        return [pltpu.make_async_copy(dst.at[t % 2, n], d_ref.at[n, t], ds_.at[t % 2, n]) for n in range(2)]

    def down(t, _):
        wt2, wt3 = w2.at[t // 2, t % 2], w3.at[t // 2, t % 2]

        @pl.when(t >= 2)
        def _():
            for q in sends(t - 2):
                q.wait()

        dst[t % 2, 1] = dotf(gT[...], act[t]).astype(bf16)
        for b in range(4):
            rows = slice(256 * b, 256 * b + 256)
            ga = dotf(glow[rows, :], wt3[...].reshape(768, 768))
            gp = (ga * gd[t, rows, :].astype(f32)).astype(bf16)
            gd[t, rows, :] = gp
            acc[rows, :] += dot_nt(gp, wt2[...].reshape(768, 768))
            v_ref[pl.ds(3 + t, 1), :] += jnp.sum(gp.astype(f32), axis=0, keepdims=True)
        dst[t % 2, 0] = dotf(lowT[...], gd[t]).astype(bf16)
        for q in sends(t):
            q.start()
        return 0

    lax.fori_loop(0, 4, down, 0)

    def last(b, _):
        rows = pl.ds(pl.multiple_of(b * 256, 256), 256)
        gn, xh = acc[rows, :], xhat[rows, :]
        e = gn * row(10)
        g1 = (e - row_mean(e) - xh * row_mean(e * xh)) * inv[rows, 0:1]
        acc[rows, :] = g1
        glow[rows, :] = g1.astype(bf16)
        add_row(10, gn * xh)
        add_row(8, gn)
        add_row(2, g1)
        return 0

    lax.fori_loop(0, 4, last, 0)
    l_g = [local(acc, g1_ref, ls.at[1]), local(glow, g1low_ref, ls.at[2])]
    gT[...] = glow[...].T
    for q in sends(2) + sends(3):
        q.wait()
    for t in range(4):
        dst[t // 2, t % 2, :, 0:256] = dotf(gT[...], hv[t]).astype(bf16)
    l_d = [local(dst.at[t // 2, t % 2, :, pl.ds(0, 256)], dout_ref.at[t], ls.at[3 + t]) for t in range(4)]
    for q in [l_o] + l_g + l_d + ox:
        q.wait()


def mid(xs, cs, heads, g, vec):
    v_ = pltpu.VMEM
    dma = pltpu.SemaphoreType.DMA
    sd = jax.ShapeDtypeStruct
    wt = v_((2, 2, 4, 2, 96, 768), bf16)
    return pl.pallas_call(
        mid_kernel,
        out_shape=[sd((4, 256, 768), bf16), sd((L, 768), f32), sd((L, 768), bf16), sd((4, 768, 256), bf16), sd((2, 4, 768, 768), bf16), sd((24, 768), f32)],
        in_specs=[HBM] * 4 + [VM],
        out_specs=[HBM] * 5 + [VM],
        scratch_shapes=[
            v_((4, 256, 768), bf16), v_((4, 256, 768), bf16), v_((4, L, 256), bf16), v_((4, 4, 2, 96, 256), bf16), wt, wt,
            v_((L, 768), f32), v_((L, 128), f32), v_((L, 768), bf16), v_((4, L, 768), bf16), v_((4, L, 768), bf16), v_((L, 768), f32),
            v_((L, 768), bf16), v_((768, L), bf16), v_((768, L), bf16), v_((4, 256, 768), bf16), v_((2, 2, 768, 768), bf16),
            dma((10,)), dma((2, 2)), dma((8,)), dma((8,)),
        ],
        compiler_params=pltpu.CompilerParams(collective_id=2, has_side_effects=True, vmem_limit_bytes=67043328),
    )(xs, cs, heads, g, vec)


def norm_stats(r):
    center = r - jnp.mean(r, axis=-1, keepdims=True)
    inv = lax.rsqrt(jnp.mean(center * center, axis=-1, keepdims=True) + EPSILON)
    return center * inv, inv


def norm_back(cot, gain, xhat, inv):
    e = cot * gain
    grad = (e - jnp.mean(e, -1, keepdims=True) - xhat * jnp.mean(e * xhat, -1, keepdims=True)) * inv
    return grad, jnp.sum(cot * xhat, 0), jnp.sum(cot, 0)


def middle(x, cot, heads, w1, w2, w3, bias_o, bias_h, bias_d, shift1, shift2, gain1, gain2):
    ein = functools.partial(jnp.einsum, preferred_element_type=f32)
    hid = x.astype(f32)
    resid1 = hid + ein("tpw,tdw->pd", heads, w1[:, :, 512:]) + bias_o
    xhat1, inv1 = norm_stats(resid1)
    normed = xhat1 * gain1 + shift1
    low = normed.astype(bf16)
    pre = ein("pd,tdf->tpf", low, w2) + bias_h[:, None, :]
    act, gelu_back = jax.vjp(lambda v: jax.nn.gelu(v, approximate=False), pre)
    act = act.astype(bf16)
    resid2 = normed + ein("tpf,tdf->pd", act, w3) + bias_d
    xhat2, inv2 = norm_stats(resid2)
    out = (xhat2 * gain2 + shift2).astype(bf16)
    g2, dgain2, dshift2 = norm_back(cot.astype(f32), gain2, xhat2, inv2)
    g2low = g2.astype(bf16)
    d3 = ein("pd,tpf->tdf", g2low, act).astype(bf16)
    gpre = gelu_back(ein("pd,tdf->tpf", g2low, w3))[0].astype(bf16)
    d2 = ein("pd,tpf->tdf", low, gpre).astype(bf16)
    gn = g2 + ein("tpf,tdf->pd", gpre, w2)
    g1, dgain1, dshift1 = norm_back(gn, gain1, xhat1, inv1)
    g1low = g1.astype(bf16)
    dout = ein("pd,tpw->tdw", g1low, heads).astype(bf16)
    dbh = jnp.sum(gpre, 1, dtype=f32)
    return out, g1, g1low, dout, d2, d3, (dgain1, dgain2, dshift1, dshift2, jnp.sum(g1, 0), dbh, jnp.sum(g2, 0))


def on_device(hidden_in, cotangent, prefix, w_qkv, w_out, w_in, w_down, biases, gains):
    rows = w_qkv.shape[0]
    n_t = lax.axis_size("tensor")
    t_me, d_me = lax.axis_index("tensor"), lax.axis_index("dp")
    n_dev = n_t * lax.axis_size("dp")
    s = jnp.stack([jnp.concatenate([w_qkv.reshape(rows, -1), w_out.T], axis=1), w_in, w_down.T])
    vecs = jnp.concatenate([biases, gains], 0)
    width = vecs.shape[1]
    vecs = jnp.pad(vecs, ((0, 4), (0, 128 - width)))
    seqs = lambda a: jnp.transpose(a, (1, 0, 2))
    h, c = seqs(hidden_in), seqs(cotangent)
    my_prefix = lax.dynamic_slice_in_dim(prefix, t_me, 1, 0)
    if lax.axis_size("dp") == 8:
        g, xs, vec, proj, projT, heads, ot, lse = front(prefix, s, h, vecs)
        oo, g1, g1low, doutw, d, v = mid(xs, c, heads, g, vec)
        gs, vs, xx = back(prefix, xs, g1low, g1, g, proj, projT, ot, lse, doutw, d.reshape(2, 2, 2, 4, 2, rows, 768), v)
        qv = vs[16:24, :256].reshape(4, 2, 256)
        vs = jnp.concatenate([qv[:, 0, :192].reshape(1, 768), qv[:, 1, :192].reshape(1, 768), vs[2:16]])
    else:
        ein = functools.partial(jnp.einsum, preferred_element_type=f32)
        g = lax.all_gather(lax.all_gather(s, "dp", axis=1, tiled=True), "tensor", axis=1)
        x = lax.all_to_all(h, "tensor", 0, 0, tiled=True).reshape(1024, 768)
        cot = lax.all_to_all(c, "tensor", 0, 0, tiled=True).reshape(1024, 768)
        b = lax.all_gather(vecs, ("dp", "tensor"), axis=0)
        w1, w2, w3 = [a.reshape(n_t, 768, 768) for a in g]
        vec = b.reshape(n_dev, 16, 128)[:, :12, :width].transpose(1, 0, 2).reshape(12, 768)
        bqkv = jnp.pad(jnp.stack([vec[0].reshape(4, 192), jnp.zeros((4, 192), f32), vec[1].reshape(4, 192)], 1).reshape(4, 1, 576), ((0, 0), (0, 0), (0, 64)))
        proj, projT, heads, ot, lse = attn_fwd(my_prefix, x, w1, bqkv)
        out, g1, g1low, doutw, d2, d3, small = middle(
            x, cot, heads, w1, w2, w3, vec[2], vec[3:7].reshape(4, 768), vec[7], vec[8], vec[9], vec[10], vec[11]
        )
        dgain1, dgain2, dshift1, dshift2, dbo, dbh, dbd = small
        gproj = attn_bwd(my_prefix, g1low, w1, proj, projT, ot, lse)
        gp = gproj[:, :, :576]
        dqkv = ein("pd,tpc->tdc", x, gp).astype(bf16)
        x4 = (g1 + ein("tpc,tdc->pd", gp, w1[:, :, :576])).astype(bf16).reshape(4, 256, 768)
        dbq = jnp.sum(gp[:, :, :192], 1, dtype=f32).reshape(1, 768)
        dbv = jnp.sum(gp[:, :, 384:], 1, dtype=f32).reshape(1, 768)
        d = jnp.stack([jnp.concatenate([dqkv, doutw[:, :, 64:]], 2), d2, d3])
        part = lax.all_to_all(d, "tensor", 1, 1, tiled=True).astype(f32).sum(1)
        part = part.astype(bf16).reshape(3, -1, rows, 768)
        gs = lax.all_to_all(part, "dp", 1, 1, tiled=True).astype(f32).sum(1)
        vs = lax.psum(
            jnp.concatenate([dbq, dbv, dbo[None], dbh, jnp.stack([dbd, dshift1, dshift2, dgain1, dgain2]), jnp.zeros((4, 768), f32)]),
            ("dp", "tensor"),
        )
        oo = lax.all_to_all(out.reshape(4, 256, 768), "tensor", 0, 0, tiled=True)
        xx = lax.all_to_all(x4, "tensor", 0, 0, tiled=True)
    mine = lax.dynamic_slice_in_dim(vs, (d_me * n_t + t_me) * width, width, 1)
    return (
        seqs(oo),
        seqs(xx),
        gs[0, :, :576].reshape(rows, 3, 192),
        gs[0, :, 576:].T,
        gs[1],
        gs[2].T,
        mine[:10],
        mine[10:12],
    )


def solution(mesh):
    placed = (
        P("tensor", "dp", None),
        P("tensor", "dp", None),
        P("dp"),
        P("dp", None, "tensor"),
        P("tensor", "dp"),
        P("dp", "tensor"),
        P("tensor", "dp"),
        P(None, ("dp", "tensor")),
        P(None, ("dp", "tensor")),
    )
    return jax.shard_map(on_device, mesh=mesh, in_specs=placed, out_specs=placed[:2] + placed[3:], check_vma=False)
```
